32 devices in a mesh: seq: 4 (over y, x), fsdp: 8 (over z, core).
Axes of the slice: x: 2, y: 2, z: 4, core: 2. Of those that a mesh axis runs over, the one named last changes fastest.
Arguments:
- tokens: bfloat16 [8, 1280, 1536], P('fsdp', 'seq'), may hold values from -6 to 6
- conditioning: bfloat16 [8, 2, 130, 1536], P('fsdp'), may hold values from -6 to 6
- lengths: int32 [8, 2], P('fsdp'), may hold values from 1 to 1024, 1280 in all within a row
- grad_output: bfloat16 [8, 1280, 1536], P('fsdp', 'seq'), may hold values from -6 to 6
- norm_first: bfloat16 [1536], P(('seq', 'fsdp')), may hold values from 0.099609375 to 1.8984375
- proj_self: bfloat16 [1536, 4608], P(('seq', 'fsdp')), may hold values from -0.15625 to 0.15625
- out_self: bfloat16 [1536, 1536], P(('seq', 'fsdp')), may hold values from -2.5 to 2.5
- norm_second: bfloat16 [1536], P(('seq', 'fsdp')), may hold values from 0.099609375 to 1.8984375
- proj_query: bfloat16 [1536, 1536], P(('seq', 'fsdp')), may hold values from -0.15625 to 0.15625
- proj_keyval: bfloat16 [1536, 3072], P(('seq', 'fsdp')), may hold values from -0.15625 to 0.15625
- out_cross: bfloat16 [1536, 1536], P(('seq', 'fsdp')), may hold values from -1.25 to 1.25
- norm_third: bfloat16 [1536], P(('seq', 'fsdp')), may hold values from 0.099609375 to 1.8984375
- proj_gateup: bfloat16 [1536, 12288], P(('seq', 'fsdp')), may hold values from -0.15625 to 0.15625
- bias_gateup: bfloat16 [12288], P(('seq', 'fsdp')), may hold values from -3 to 3
- proj_down: bfloat16 [6144, 1536], P(('seq', 'fsdp')), may hold values from -0.078125 to 0.078125
- bias_down: bfloat16 [1536], P(('seq', 'fsdp')), may hold values from -3 to 3
Outputs:
- layer_out: bfloat16 [8, 1280, 1536], P('fsdp', 'seq')
- grad_tokens: float32 [8, 1280, 1536], P('fsdp', 'seq')
- grad_cond: float32 [8, 2, 130, 1536], P('fsdp')
- grad_norm_first: float32 [1536], P(('seq', 'fsdp'))
- grad_proj_self: float32 [1536, 4608], P(('seq', 'fsdp'))
- grad_out_self: float32 [1536, 1536], P(('seq', 'fsdp'))
- grad_norm_second: float32 [1536], P(('seq', 'fsdp'))
- grad_proj_query: float32 [1536, 1536], P(('seq', 'fsdp'))
- grad_proj_keyval: float32 [1536, 3072], P(('seq', 'fsdp'))
- grad_out_cross: float32 [1536, 1536], P(('seq', 'fsdp'))
- grad_norm_third: float32 [1536], P(('seq', 'fsdp'))
- grad_proj_gateup: float32 [1536, 12288], P(('seq', 'fsdp'))
- grad_bias_gateup: float32 [12288], P(('seq', 'fsdp'))
- grad_proj_down: float32 [6144, 1536], P(('seq', 'fsdp'))
- grad_bias_down: float32 [1536], P(('seq', 'fsdp'))
The draws below stay inside these ranges and needn't reach their ends.
Inputs may be any that keep to these rules, and one draw needn't show every extreme that they name: Each row of lengths holds the lengths of the 2 sequences of one group, which sum to 1280; the largest in each row is at most 1024.
All inputs are finite; a program needn't handle non-finite values.
Results may differ from the reference program's by a relative error of at most 0.028.
Values may be sent and summed in bfloat16 or wider, within the bound.
No kernel may reach another device: no remote copies, remote signals or barrier semaphores. Data moves between devices by JAX's collectives and lax.ppermute only.
A program may use at most 576 MiB of HBM per device.

```python
import math
import jax
import jax.numpy as jnp
import numpy as np
from jax import lax

D = 1536
HEADS = 24
HEAD = 64
FF = 6144
COND = 130
SEQS_GRP = 2
GROUP = 1280
LONGEST = 1024
N_FSDP = 8


def levels(key, dims, split, smallest, high):
    factor_of, own = 1.0, jax.random.fold_in(key, 6)
    for axis_at, shards_of in split:
        draws = jnp.exp(jax.random.uniform(jax.random.fold_in(own, axis_at), (shards_of,), jnp.float32, smallest / len(split), high / len(split)))
        factor_of = factor_of * jnp.repeat(draws, dims[axis_at] // shards_of).reshape([-1 if axis == axis_at else 1 for axis in range(len(dims))])
    return factor_of


def length_profile(amount, total, reach, lean):
    portions = [(1 << 20) // math.isqrt(rank ** lean) + 1 for rank in range(2, amount + 1)]
    spare, holding = total - reach - (amount - 1), [1] * (amount - 1)
    while spare > 0:
        candidates = [i for i in range(amount - 1) if holding[i] < reach]
        pool, left = sum([portions[i] for i in candidates]), spare
        for i in candidates:
            addition = min(reach - holding[i], max(1, left * portions[i] // pool), spare)
            holding[i] = holding[i] + addition
            spare = spare - addition
    return np.array([reach] + holding)


def ragged(stream_key, count, total, most, skew):
    if count == 2:
        one = jax.random.randint(stream_key, (), max(1, total - most), min(most, total - 1) + 1)
        return jnp.stack([one, total - one])
    sizes = jnp.asarray(length_profile(count, total, most, skew), jnp.int32)
    couples = (count - 1) // 2
    donor, sink = sizes[1:1 + 2 * couples:2], sizes[2:2 + 2 * couples:2]
    slack = jnp.minimum(donor - 1, most - sink)
    shifted = jax.random.randint(jax.random.fold_in(stream_key, 1), (couples,), 0, 1 << 20) % (slack + 1)
    sizes = sizes.at[1:1 + 2 * couples:2].set(donor - shifted).at[2:2 + 2 * couples:2].set(sink + shifted)
    return sizes[jax.random.permutation(jax.random.fold_in(stream_key, 2), count)]


def bell_draw(stream_key, dims, scale, bound, shards=(), kind=jnp.bfloat16):
    factor_of = levels(stream_key, dims, shards, -0.22, 0.18) if shards else 1.0
    drawn = jax.random.normal(stream_key, dims, jnp.float32) * scale * factor_of
    return jnp.minimum(jnp.maximum(drawn, -bound), bound).astype(kind)


def setup_inputs(seed: int = 0) -> dict:
    key_of = jax.random.split(jax.random.key(seed), 17)
    return {
        "tokens": bell_draw(key_of[0], (N_FSDP, GROUP, D), 1.0, 6.0, ((0, 8), (1, 4))),
        "conditioning": bell_draw(key_of[1], (N_FSDP, SEQS_GRP, COND, D), 1.0, 6.0, ((0, 8),)),
        "lengths": jax.vmap(lambda own: ragged(own, SEQS_GRP, GROUP, LONGEST, 2))(jax.random.split(key_of[2], N_FSDP)).reshape((N_FSDP, SEQS_GRP)).astype(jnp.int32),
        "grad_output": bell_draw(key_of[3], (N_FSDP, GROUP, D), 1.0, 6.0, ((0, 8), (1, 4))),
        "norm_first": jnp.clip(1.0 + 0.18 * jax.random.normal(key_of[4], (D,), jnp.float32), 0.099609375, 1.8984375).astype(jnp.bfloat16),
        "proj_self": bell_draw(key_of[5], (D, 3 * D), D ** -0.5, 0.15625, ((0, 32),)),
        "out_self": bell_draw(key_of[6], (D, D), (max(D // 256, 1)) ** -0.5, 2.5, ((0, 32),)),
        "norm_second": jnp.clip(1.0 + 0.18 * jax.random.normal(key_of[7], (D,), jnp.float32), 0.099609375, 1.8984375).astype(jnp.bfloat16),
        "proj_query": bell_draw(key_of[8], (D, D), D ** -0.5, 0.15625, ((0, 32),)),
        "proj_keyval": bell_draw(key_of[9], (D, 2 * D), D ** -0.5, 0.15625, ((0, 32),)),
        "out_cross": bell_draw(key_of[10], (D, D), (max(D // 64, 1)) ** -0.5, 1.25, ((0, 32),)),
        "norm_third": jnp.clip(1.0 + 0.18 * jax.random.normal(key_of[11], (D,), jnp.float32), 0.099609375, 1.8984375).astype(jnp.bfloat16),
        "proj_gateup": bell_draw(key_of[12], (D, 2 * FF), D ** -0.5, 0.15625, ((0, 32),)),
        "bias_gateup": bell_draw(key_of[13], (2 * FF,), 0.5, 3.0, ((0, 32),)),
        "proj_down": bell_draw(key_of[14], (FF, D), FF ** -0.5, 0.078125, ((0, 32),)),
        "bias_down": bell_draw(key_of[15], (D,), 0.5, 3.0, ((0, 32),)),
    }


highest = lax.Precision.HIGHEST
epsilon = 1e-05
masked_score = -1e+30

@jax.custom_vjp
def low(v):
    return lax.optimization_barrier(v.astype(jnp.bfloat16)).astype(jnp.float32)

@jax.custom_vjp
def low_back(v):
    return v

def low_keep(v):
    return (low(v), None)

def low_pass(kept, grad):
    return (grad,)

def back_keep(v):
    return (v, None)

def back_low(kept, grad):
    return (low(grad),)
low.defvjp(low_keep, low_pass)
low_back.defvjp(back_keep, back_low)

def seq_info(global_rows, group_lengths):
    ends = jnp.cumsum(group_lengths).astype(jnp.int32)
    starts = (ends - group_lengths).astype(jnp.int32)
    ident = lax.optimization_barrier(jnp.sum((global_rows[:, None] >= ends[None, :]).astype(jnp.int32), axis=1))
    onehot = ident[:, None] == jnp.arange(group_lengths.shape[0], dtype=jnp.int32)[None, :]
    begin = lax.optimization_barrier(jnp.sum(jnp.where(onehot, starts[None, :], 0), axis=1)).astype(jnp.int32)
    return (ident, (global_rows - begin).astype(jnp.float32))

def angles(positions):
    half = HEAD // 2
    inverse = jnp.power(10000.0, -jnp.arange(half, dtype=jnp.float32) / half)
    turned = positions[:, None] * inverse[None, :]
    return (jnp.cos(turned), jnp.sin(turned))

def rotate(vector, cosine, sine):
    half = vector.shape[-1] // 2
    first_half = vector[..., :half]
    second_half = vector[..., half:]
    cos_rows = cosine[:, None, :]
    sin_rows = sine[:, None, :]
    return jnp.concatenate([first_half * cos_rows - second_half * sin_rows, second_half * cos_rows + first_half * sin_rows], axis=-1)

def norm_rows(values, gain):
    centre = values - lax.optimization_barrier(jnp.mean(values, axis=-1, keepdims=True))
    spread = lax.optimization_barrier(jnp.mean(centre * centre, axis=-1, keepdims=True))
    return centre * lax.rsqrt(spread + epsilon) * gain

def softmax_masked(scores, allowed):
    scores = jnp.where(allowed, scores, masked_score)
    largest = lax.optimization_barrier(jnp.max(scores, axis=-1, keepdims=True))
    expo = jnp.where(allowed, jnp.exp(scores - largest), 0.0)
    return expo / lax.optimization_barrier(jnp.sum(expo, axis=-1, keepdims=True))

def layer(tokens, cond_rows, weights, row_ids, cosine, sine, key_ids):
    norm_first, proj_self, out_self, norm_second, proj_query, proj_keyval, out_cross, norm_third, proj_gateup, bias_gateup, proj_down, bias_down = weights
    rows = tokens.shape[0]
    normed = low(norm_rows(tokens, norm_first))
    packed = low_back(jnp.dot(normed, proj_self, precision=highest))
    queries = low(rotate(packed[:, :D].reshape(rows, HEADS, HEAD), cosine, sine))
    keys = low(rotate(packed[:, D:2 * D].reshape(rows, HEADS, HEAD), cosine, sine))
    values = low(packed[:, 2 * D:].reshape(rows, HEADS, HEAD))
    block = math.gcd(rows, 512)

    def attend(inputs):
        query_block, block_ids = inputs
        scores = low_back(jnp.einsum('qhd,khd->hqk', query_block, keys, precision=highest) * 0.125)
        allowed = (block_ids[:, None] == row_ids[None, :])[None]
        probs = low(softmax_masked(scores, allowed))
        return jnp.einsum('hqk,khd->qhd', probs, values, precision=highest)
    mixed = lax.map(jax.checkpoint(attend), (queries.reshape(rows // block, block, HEADS, HEAD), row_ids.reshape(rows // block, block)))
    mixed = low(low_back(mixed.reshape(rows, D)))
    first = tokens + low_back(jnp.dot(mixed, out_self, precision=highest))
    normed_two = low(norm_rows(first, norm_second))
    cross_query = low(low_back(jnp.dot(normed_two, proj_query, precision=highest))).reshape(rows, HEADS, HEAD)
    keyval = low(low_back(jnp.dot(cond_rows, proj_keyval, precision=highest)))
    count = keyval.shape[0]
    cross_keys = keyval[:, :D].reshape(count, HEADS, HEAD)
    cross_values = keyval[:, D:].reshape(count, HEADS, HEAD)
    cross_scores = low_back(jnp.einsum('qhd,khd->hqk', cross_query, cross_keys, precision=highest) * 0.125)
    cross_allowed = (row_ids[:, None] == key_ids[None, :])[None]
    cross_probs = low(softmax_masked(cross_scores, cross_allowed))
    cross_mixed = jnp.einsum('hqk,khd->qhd', cross_probs, cross_values, precision=highest)
    cross_mixed = low(low_back(cross_mixed.reshape(rows, D)))
    second = first + low_back(jnp.dot(cross_mixed, out_cross, precision=highest))
    normed_three = low(norm_rows(second, norm_third))
    gateup = low_back(jnp.dot(normed_three, proj_gateup, precision=highest) + bias_gateup)
    gate = gateup[:, :FF]
    upper = gateup[:, FF:]
    active = low(jax.nn.silu(gate) * upper)
    return second + low_back(jnp.dot(active, proj_down, precision=highest) + bias_down)

def reference(tokens, conditioning, lengths, grad_output, norm_first, proj_self, out_self, norm_second, proj_query, proj_keyval, out_cross, norm_third, proj_gateup, bias_gateup, proj_down, bias_down):
    weights = tuple((weight.astype(jnp.float32) for weight in (norm_first, proj_self, out_self, norm_second, proj_query, proj_keyval, out_cross, norm_third, proj_gateup, bias_gateup, proj_down, bias_down)))
    all_rows = jnp.arange(GROUP, dtype=jnp.int32)
    key_ids = (jnp.arange(SEQS_GRP * COND, dtype=jnp.int32) // COND).astype(jnp.int32)

    def per_group(totals, inputs):
        group_tokens, group_cond, group_lengths, group_grad = inputs
        row_ids, positions = seq_info(all_rows, group_lengths)
        cosine, sine = angles(positions)
        cond_rows = group_cond.astype(jnp.float32).reshape(SEQS_GRP * COND, D)

        def forward(tok_rows, cond_part, weight_set):
            return layer(tok_rows, cond_part, weight_set, row_ids, cosine, sine, key_ids)
        result, pullback = jax.vjp(forward, group_tokens.astype(jnp.float32), cond_rows, weights)
        grad_tok, grad_cnd, grad_weights = pullback(group_grad.astype(jnp.float32))
        totals = jax.tree.map(lambda total, term: total + term, totals, grad_weights)
        return (totals, (result.astype(jnp.bfloat16), grad_tok, grad_cnd.reshape(SEQS_GRP, COND, D)))
    start = tuple((jnp.zeros_like(weight) for weight in weights))
    totals, (outputs, grad_toks, grad_conds) = lax.scan(per_group, start, (tokens, conditioning, lengths, grad_output))
    return (outputs, grad_toks, grad_conds, totals[0], totals[1], totals[2], totals[3], totals[4], totals[5], totals[6], totals[7], totals[8], totals[9], totals[10], totals[11])
```

```python
import functools

import jax
import jax.numpy as jnp
from jax import lax
from jax.experimental import pallas as pl
from jax.experimental.pallas import tpu as pltpu
from jax.sharding import PartitionSpec as P

D = 1536
HEADS = 24
HEAD = 64
FF = 6144
COND = 130
SEQS_GRP = 2
LANES = 128

epsilon = 1e-05
masked_score = -1e30
bf16 = jnp.bfloat16
f32 = jnp.float32
ALL = ("seq", "fsdp")


def seq_info(global_rows, group_lengths):
    ends = jnp.cumsum(group_lengths)
    starts = ends - group_lengths
    ident = jnp.sum((global_rows[:, None] >= ends[None, :]).astype(jnp.int32), axis=1)
    onehot = ident[:, None] == jnp.arange(group_lengths.shape[0], dtype=jnp.int32)[None, :]
    begin = jnp.sum(jnp.where(onehot, starts[None, :], 0), axis=1)
    return (ident, (global_rows - begin).astype(f32))


def angle_tables(positions):
    half = HEAD // 2
    inverse = jnp.power(10000.0, -jnp.arange(half, dtype=f32) / half)
    turned = positions[:, None] * inverse[None, :]
    cosine, sine = jnp.cos(turned), jnp.sin(turned)
    reps = LANES // HEAD
    return (
        jnp.concatenate([cosine, cosine] * reps, axis=1),
        jnp.concatenate([-sine, sine] * reps, axis=1),
    )


def norm_rows(values, gain):
    centre = values - jnp.mean(values, axis=-1, keepdims=True)
    spread = jnp.mean(centre * centre, axis=-1, keepdims=True)
    scaled = lax.rsqrt(spread + epsilon)
    normal = centre * scaled
    return (normal, scaled, normal * gain)


def norm_back(grad_rows, normal, scaled, gain):
    weighted = grad_rows * gain
    mean_one = jnp.mean(weighted, axis=-1, keepdims=True)
    mean_two = jnp.mean(weighted * normal, axis=-1, keepdims=True)
    return (scaled * (weighted - mean_one - normal * mean_two), jnp.sum(grad_rows * normal, axis=0))


def dot(left, right):
    return jnp.dot(left, right, preferred_element_type=f32)


def outer_sum(left, right):
    return lax.dot_general(left, right, (((0,), (0,)), ((), ())), preferred_element_type=f32)


def back_prod(left, weight):
    return lax.dot_general(left, weight, (((1,), (1,)), ((), ())), preferred_element_type=f32)


def hop(value, j):
    return lax.ppermute(value, "seq", [(i, i ^ j) for i in range(4)])


def block_ids(n):
    if n == 4:
        return lax.axis_index("seq") ^ jnp.arange(n, dtype=jnp.int32)
    return jnp.arange(n, dtype=jnp.int32)


def gather_rows(value, n):
    if n != 4:
        return lax.all_gather(value, "seq", axis=0, tiled=True)
    half = value.shape[0] // 2
    first, second = hop(value, 1), hop(value, 2)
    third, fourth = hop(second[:half], 1), hop(first[half:], 2)
    return jnp.concatenate([value, first, second, third, fourth], axis=0)


def scatter_rows(blocks, n):
    if n != 4:
        whole = jnp.concatenate([blocks(j) for j in range(n)], axis=0)
        return lax.psum_scatter(whole.astype(bf16), "seq", scatter_dimension=0, tiled=True).astype(f32)
    last = blocks(3).astype(bf16)
    half = last.shape[0] // 2
    to_first, to_second = hop(last[:half], 1), hop(last[half:], 2)
    one, two = blocks(1), blocks(2)
    plain_one, plain_two = hop(one[:half].astype(bf16), 1), hop(two[half:].astype(bf16), 2)
    sum_one = hop((one[half:] + to_second.astype(f32)).astype(bf16), 1)
    sum_two = hop((two[:half] + to_first.astype(f32)).astype(bf16), 2)
    own = blocks(0)
    return own + jnp.concatenate(
        [
            plain_one.astype(f32) + sum_two.astype(f32),
            sum_one.astype(f32) + plain_two.astype(f32),
        ],
        axis=0,
    )


def swap_halves(value):
    lane = lax.broadcasted_iota(jnp.int32, value.shape, 1)
    half = HEAD // 2
    return jnp.where(
        lane % HEAD < half, pltpu.roll(value, LANES - half, 1), pltpu.roll(value, half, 1)
    )


def head_rows(h):
    return slice(h * HEAD, (h + 1) * HEAD)


def lane_mask(value, h):
    lane = lax.broadcasted_iota(jnp.int32, value.shape, 1)
    return jnp.where(lane // HEAD == h, value, jnp.zeros_like(value))


def row_mask(value, h):
    row = lax.broadcasted_iota(jnp.int32, value.shape, 0)
    return jnp.where(row // HEAD == h, value, jnp.zeros_like(value))


def attend_kernel(rope, tile, *refs):
    if rope:
        q_ref, k_ref, v_ref, cos_ref, sin_ref, qid_ref, kid_ref = refs[:7]
        qo_ref, ko_ref, vo_ref, o_ref, lse_ref, qt, vt, ot, kb = refs[7:]
        q, k = q_ref[...], k_ref[...]
        q = (q * cos_ref[...] + swap_halves(q) * sin_ref[...]).astype(bf16)
        k = (k * cos_ref[...] + swap_halves(k) * sin_ref[...]).astype(bf16)
        v = v_ref[...].astype(bf16)
        qo_ref[...] = q
        ko_ref[...] = k
        vo_ref[...] = v
    else:
        q_ref, k_ref, v_ref, qid_ref, kid_ref, o_ref, lse_ref, qt, vt, ot, kb = refs
        q, k, v = q_ref[...], k_ref[...], v_ref[...]
    kb[...] = k
    qt[...] = q.astype(f32).T.astype(bf16)
    vt[...] = v.astype(f32).T.astype(bf16)

    def body(t, carry):
        at = pl.ds(pl.multiple_of(t * tile, tile), tile)
        queries = qt[:, at]
        allowed = kid_ref[...] == qid_ref[:, at]
        for h in range(LANES // HEAD):
            s = dot(kb[...], row_mask(queries, h)) * 0.125
            s = jnp.where(allowed, s, masked_score)
            top = jnp.max(s, axis=0, keepdims=True)
            e = jnp.exp(s - top)
            total = jnp.sum(e, axis=0, keepdims=True)
            p = (e * (1.0 / total)).astype(bf16)
            ot[head_rows(h), at] = dot(vt[head_rows(h), :], p)
            lse_ref[0, h : h + 1, at] = top + jnp.log(total)
        return carry

    lax.fori_loop(0, qt.shape[1] // tile, body, 0)
    o_ref[...] = ot[...].T.astype(bf16)


def attend_back_kernel(rope, tile, *refs):
    if rope:
        q_ref, k_ref, v_ref, do_ref, o_ref, lse_ref, cos_ref, sin_ref, qid_ref, kid_ref = refs[:10]
        dq_ref, dk_ref, dv_ref, qt, dot_t, kt, dqt, dk_acc, dv_acc, delta = refs[10:]
    else:
        q_ref, k_ref, v_ref, do_ref, o_ref, lse_ref, qid_ref, kid_ref = refs[:8]
        dq_ref, dk_ref, dv_ref, qt, dot_t, kt, dqt, dk_acc, dv_acc, delta = refs[8:]
    qt[...] = q_ref[...].astype(f32).T.astype(bf16)
    kt[...] = k_ref[...].astype(f32).T.astype(bf16)
    dof_t = do_ref[...].astype(f32).T
    dot_t[...] = dof_t.astype(bf16)
    product = dof_t * o_ref[...].astype(f32).T
    for h in range(LANES // HEAD):
        delta[h : h + 1, :] = jnp.sum(product[head_rows(h), :], axis=0, keepdims=True)
    dk_acc[...] = jnp.zeros_like(dk_acc)
    dv_acc[...] = jnp.zeros_like(dv_acc)

    def body(t, carry):
        at = pl.ds(pl.multiple_of(t * tile, tile), tile)
        allowed = kid_ref[...] == qid_ref[:, at]
        for h in range(LANES // HEAD):
            s = dot(k_ref[...], row_mask(qt[:, at], h)) * 0.125
            p = jnp.where(allowed, jnp.exp(s - lse_ref[0, h : h + 1, at]), 0.0)
            dp = dot(v_ref[...], row_mask(dot_t[:, at], h))
            dv_acc[...] += dot(p.astype(bf16), lane_mask(do_ref[at, :], h))
            ds = (p * (dp - delta[h : h + 1, at])).astype(bf16)
            dk_acc[...] += dot(ds, lane_mask(q_ref[at, :], h))
            dqt[head_rows(h), at] = dot(kt[head_rows(h), :], ds)
        return carry

    lax.fori_loop(0, qt.shape[1] // tile, body, 0)
    dq = dqt[...].T * 0.125
    dk = dk_acc[...] * 0.125
    if rope:
        dq = dq * cos_ref[...] - swap_halves(dq) * sin_ref[...]
        dk = dk * cos_ref[...] - swap_halves(dk) * sin_ref[...]
    dq_ref[...] = dq.astype(bf16)
    dk_ref[...] = dk.astype(bf16)
    dv_ref[...] = dv_acc[...].astype(bf16)


def query_tile(rows):
    for tile in (256, 128):
        if rows % tile == 0:
            return tile
    return rows


def spec(rows, offset=0):
    return pl.BlockSpec((rows, LANES), lambda i: (0, i + offset))


def whole(shape):
    return pl.BlockSpec(shape, lambda i: (0,) * len(shape), pipeline_mode=pl.Buffered(1))


LIMIT = 56 * 1024 * 1024


def attend(q, k, v, offsets, pairs, qid, kid, tables=None):
    nq, nk = q.shape[0], k.shape[0]
    rope = tables is not None
    tile = query_tile(nq)
    ins = [spec(nq, offsets[0]), spec(nk, offsets[1]), spec(nk, offsets[2])]
    args = [q, k, v]
    outs, shapes = [], []
    if rope:
        ins += [whole((nq, LANES)), whole((nq, LANES))]
        args += list(tables)
        outs += [spec(nq), spec(nk), spec(nk)]
        shapes += [jax.ShapeDtypeStruct((rows, pairs * LANES), bf16) for rows in (nq, nk, nk)]
    ins += [whole((1, nq)), whole((nk, 1))]
    args += [qid[None, :], kid[:, None]]
    outs += [spec(nq), pl.BlockSpec((1, 8, nq), lambda i: (i, 0, 0))]
    shapes += [
        jax.ShapeDtypeStruct((nq, pairs * LANES), bf16),
        jax.ShapeDtypeStruct((pairs, 8, nq), f32),
    ]
    return pl.pallas_call(
        functools.partial(attend_kernel, rope, tile),
        out_shape=shapes,
        grid=(pairs,),
        in_specs=ins,
        out_specs=outs,
        scratch_shapes=[
            pltpu.VMEM((LANES, nq), bf16),
            pltpu.VMEM((LANES, nk), bf16),
            pltpu.VMEM((LANES, nq), f32),
            pltpu.VMEM((nk, LANES), bf16),
        ],
        compiler_params=pltpu.CompilerParams(vmem_limit_bytes=LIMIT),
        cost_estimate=pl.CostEstimate(
            flops=2 * 2 * 2 * pairs * nq * nk * LANES,
            bytes_accessed=pairs * LANES * (nq + nk) * 12,
            transcendentals=2 * pairs * nq * nk,
        ),
        name="attend_self" if rope else "attend_cross",
    )(*args)


def attend_back(q, k, v, offsets, pairs, grad, mixed, lse, qid, kid, tables=None):
    nq, nk = q.shape[0], k.shape[0]
    rope = tables is not None
    tile = query_tile(nq)
    ins = [spec(nq, offsets[0]), spec(nk, offsets[1]), spec(nk, offsets[2]), spec(nq), spec(nq)]
    args = [q, k, v, grad, mixed]
    ins += [pl.BlockSpec((1, 8, nq), lambda i: (i, 0, 0))]
    args += [lse]
    if rope:
        ins += [whole((nq, LANES)), whole((nq, LANES))]
        args += list(tables)
    ins += [whole((1, nq)), whole((nk, 1))]
    args += [qid[None, :], kid[:, None]]
    return pl.pallas_call(
        functools.partial(attend_back_kernel, rope, tile),
        out_shape=[jax.ShapeDtypeStruct((rows, pairs * LANES), bf16) for rows in (nq, nk, nk)],
        grid=(pairs,),
        in_specs=ins,
        out_specs=[spec(nq), spec(nk), spec(nk)],
        scratch_shapes=[
            pltpu.VMEM((LANES, nq), bf16),
            pltpu.VMEM((LANES, nq), bf16),
            pltpu.VMEM((LANES, nk), bf16),
            pltpu.VMEM((LANES, nq), f32),
            pltpu.VMEM((nk, LANES), f32),
            pltpu.VMEM((nk, LANES), f32),
            pltpu.VMEM((8, nq), f32),
        ],
        compiler_params=pltpu.CompilerParams(vmem_limit_bytes=LIMIT),
        cost_estimate=pl.CostEstimate(
            flops=2 * 5 * 2 * pairs * nq * nk * LANES,
            bytes_accessed=pairs * LANES * (nq + nk) * 12,
            transcendentals=2 * pairs * nq * nk,
        ),
        name="back_self" if rope else "back_cross",
    )(*args)


def column_parts(shard, parts, n):
    r, columns = shard.shape
    c = columns // (parts * n)
    return shard.reshape(r, parts, n, c).transpose(2, 0, 1, 3).reshape(n, r, parts * c)


def natural_columns(pieces, parts, n):
    r, columns = pieces.shape[1:]
    c = columns // parts
    return pieces.reshape(n, r, parts, c).transpose(1, 2, 0, 3).reshape(r, parts * n * c)


def to_seq(pieces):
    return lax.all_to_all(pieces, "seq", 0, 0, tiled=True)


def gather_columns(pieces, n, nf):
    r, c = pieces.shape[1:]
    gathered = lax.all_gather(pieces.reshape(n * r, c), "fsdp", axis=0, tiled=True)
    return gathered.reshape(nf, n, r, c).transpose(1, 0, 2, 3).reshape(n * nf * r, c)


def scatter_columns(grad, n, nf):
    rows, c = grad.shape
    r = rows // (n * nf)
    ordered = grad.astype(bf16).reshape(n, nf, r, c).transpose(1, 0, 2, 3).reshape(rows, c)
    return lax.psum_scatter(ordered, "fsdp", scatter_dimension=0, tiled=True).reshape(n, r, c)


def scatter_plain(grad):
    return lax.psum_scatter(grad.astype(bf16), "fsdp", scatter_dimension=0, tiled=True)


def pad_heads(value, parts):
    rows, columns = value.shape
    c = columns // parts
    if c % LANES == 0:
        return value
    padded = -(-c // LANES) * LANES
    return jnp.pad(value.reshape(rows, parts, c), ((0, 0), (0, 0), (0, padded - c))).reshape(
        rows, parts * padded
    )


def shards(
    tokens,
    conditioning,
    lengths,
    grad_output,
    norm_first,
    proj_self,
    out_self,
    norm_second,
    proj_query,
    proj_keyval,
    out_cross,
    norm_third,
    proj_gateup,
    bias_gateup,
    proj_down,
    bias_down,
):
    rows = tokens.shape[1]
    n = lax.axis_size("seq")
    nf = lax.axis_size("fsdp")
    me = lax.axis_index("seq")
    group = rows * n
    wide = D // n
    pairs = -(-wide // LANES)
    hidden = FF // n
    r = norm_first.shape[0]

    small = jnp.concatenate(
        [v.reshape(r, -1) for v in (norm_first, norm_second, norm_third, bias_down, bias_gateup)],
        axis=1,
    )
    small = jnp.pad(small, ((0, 0), (0, LANES - small.shape[1])))
    self_in = jnp.concatenate(
        [column_parts(proj_self, 3, n), jnp.broadcast_to(small[None], (n, r, LANES))], axis=2
    )
    self_pieces = to_seq(self_in)
    rest_in = jnp.concatenate(
        [column_parts(proj_keyval, 2, n), column_parts(proj_query, 1, n), column_parts(proj_gateup, 2, n)],
        axis=2,
    )
    rest_pieces = to_seq(rest_in)
    self_all = gather_columns(self_pieces, n, nf)
    w_self = self_all[:, : 3 * wide]
    vectors = self_all[:, 3 * wide : 3 * wide + 12]
    gain_one, gain_two, gain_three, b_down = (vectors[:, j].astype(f32) for j in range(4))
    b_gateup = vectors[:, 4:12].reshape(2 * FF).astype(f32)
    b_gate = lax.dynamic_slice_in_dim(b_gateup, me * hidden, hidden, 0)
    b_upper = lax.dynamic_slice_in_dim(b_gateup, FF + me * hidden, hidden, 0)
    outs = lax.all_gather(jnp.concatenate([out_self, out_cross], axis=0), "fsdp", axis=0, tiled=True)
    outs = outs.reshape(nf, 2, r, D)
    w_out = outs[:, 0].reshape(nf * r, D)
    w_cross = outs[:, 1].reshape(nf * r, D)
    kvq = gather_columns(rest_pieces[:, :, : 3 * wide], n, nf)
    w_keyval, w_query = kvq[:, : 2 * wide], kvq[:, 2 * wide :]
    w_gateup = gather_columns(rest_pieces[:, :, 3 * wide :], n, nf)
    w_down = lax.all_gather(proj_down, "fsdp", axis=0, tiled=True)

    group_lengths = lengths[0]
    order = block_ids(n)
    all_rows = (order[:, None] * rows + jnp.arange(rows, dtype=jnp.int32)[None, :]).reshape(group)
    ids, positions = seq_info(all_rows, group_lengths)
    tables = angle_tables(positions)
    group_tokens = gather_rows(tokens[0], n)
    group_grad = gather_rows(grad_output[0], n)

    def block(value, j):
        return lax.slice_in_dim(value, j * rows, (j + 1) * rows, axis=0)

    inputs = tokens[0].astype(f32)
    normal_one, scaled_one, _ = norm_rows(inputs, gain_one)
    normed_one = norm_rows(group_tokens.astype(f32), gain_one)[2].astype(bf16)
    packed = pad_heads(dot(normed_one, w_self), 3)
    q, k, v, mixed, lse = attend(packed, packed, packed, (0, pairs, 2 * pairs), pairs, ids, ids, tables)
    mixed_in = mixed[:, :wide]
    first = inputs + scatter_rows(lambda j: dot(block(mixed_in, j), w_out), n)

    normal_two, scaled_two, normed = norm_rows(first, gain_two)
    normed_two = gather_rows(normed.astype(bf16), n)
    cq = pad_heads(dot(normed_two, w_query).astype(bf16), 1)
    cond_rows = conditioning[0].reshape(SEQS_GRP * COND, D)
    count = SEQS_GRP * COND
    count_pad = -(-count // 16) * 16
    keyval = pad_heads(dot(cond_rows, w_keyval).astype(bf16), 2)
    keyval = jnp.pad(keyval, ((0, count_pad - count), (0, 0)))
    index = jnp.arange(count_pad, dtype=jnp.int32)
    cond_ids = jnp.where(index < count, index // COND, -1)
    cmix, clse = attend(cq, keyval, keyval, (0, 0, pairs), pairs, ids, cond_ids)
    cmix_in = cmix[:, :wide]
    second = first + scatter_rows(lambda j: dot(block(cmix_in, j), w_cross), n)

    normal_three, scaled_three, normed = norm_rows(second, gain_three)
    normed_three = gather_rows(normed.astype(bf16), n)
    gate = dot(normed_three, w_gateup[:, :hidden]) + b_gate
    upper = dot(normed_three, w_gateup[:, hidden:]) + b_upper
    sigma = jax.nn.sigmoid(gate)
    silu_gate = gate * sigma
    active = (silu_gate * upper).astype(bf16)
    result = second + scatter_rows(lambda j: dot(block(active, j), w_down), n) + b_down

    grad_rows = grad_output[0].astype(f32)
    grad_b_down = jnp.sum(grad_rows, axis=0)
    grad_active = back_prod(group_grad, w_down)
    grad_gate = grad_active * upper * sigma * (1.0 + gate * (1.0 - sigma))
    grad_upper = grad_active * silu_gate
    grad_gateup = jnp.concatenate([grad_gate, grad_upper], axis=1).astype(bf16)
    grad_w_down = scatter_plain(outer_sum(active, group_grad))
    through = scatter_rows(lambda j: back_prod(block(grad_gateup, j), w_gateup), n)
    grad_w_gateup = scatter_columns(outer_sum(normed_three, grad_gateup), n, nf)
    grad_b_gateup = jnp.sum(grad_gateup.astype(f32), axis=0)
    through, grad_gain_three = norm_back(through, normal_three, scaled_three, gain_three)
    grad_second = grad_rows + through

    group_second = gather_rows(grad_second.astype(bf16), n)
    grad_cmix = pad_heads(back_prod(group_second, w_cross).astype(bf16), 1)
    dcq, dck, dcv = attend_back(
        cq, keyval, keyval, (0, 0, pairs), pairs, grad_cmix, cmix, clse, ids, cond_ids
    )
    dcq, dck, dcv = dcq[:, :wide], dck[:count, :wide], dcv[:count, :wide]
    through = scatter_rows(lambda j: back_prod(block(dcq, j), w_query), n)
    grad_keyval = jnp.concatenate([dck, dcv], axis=1)
    grad_w_cross = scatter_plain(outer_sum(cmix_in, group_second))
    grad_w_kvq = scatter_columns(
        jnp.concatenate([outer_sum(cond_rows, grad_keyval), outer_sum(normed_two, dcq)], axis=1), n, nf
    )
    grad_cond = lax.psum(back_prod(grad_keyval, w_keyval), "seq").reshape(1, SEQS_GRP, COND, D)
    through, grad_gain_two = norm_back(through, normal_two, scaled_two, gain_two)
    grad_first = grad_second + through

    group_first = gather_rows(grad_first.astype(bf16), n)
    grad_mixed = pad_heads(back_prod(group_first, w_out).astype(bf16), 1)
    dq, dk, dv = attend_back(q, k, v, (0, 0, 0), pairs, grad_mixed, mixed, lse, ids, ids, tables)
    grad_packed = jnp.concatenate([dq[:, :wide], dk[:, :wide], dv[:, :wide]], axis=1)
    through = scatter_rows(lambda j: back_prod(block(grad_packed, j), w_self), n)
    grad_w_out = scatter_plain(outer_sum(mixed_in, group_first))
    grad_w_self = scatter_columns(outer_sum(normed_one, grad_packed), n, nf)
    through, grad_gain_one = norm_back(through, normal_one, scaled_one, gain_one)
    grad_inputs = grad_first + through

    rest = to_seq(jnp.concatenate([grad_w_kvq, grad_w_gateup], axis=2))
    own_self = to_seq(grad_w_self)
    place = me * nf + lax.axis_index("fsdp")
    b_whole = jnp.zeros((2, FF), f32)
    b_whole = lax.dynamic_update_slice(b_whole, grad_b_gateup.reshape(2, hidden), (0, me * hidden))
    early = lax.psum(
        jnp.concatenate([grad_gain_two, grad_gain_three, grad_b_down, b_whole.reshape(2 * FF)]), ALL
    )
    late = lax.psum(grad_gain_one, ALL)

    def mine(vector):
        count = vector.shape[0] // (n * nf)
        return lax.dynamic_slice_in_dim(vector, place * count, count, 0)

    return (
        result.astype(bf16)[None],
        grad_inputs[None],
        grad_cond,
        mine(late),
        natural_columns(own_self, 3, n).astype(f32),
        grad_w_out.astype(f32),
        mine(early[:D]),
        natural_columns(rest[:, :, 2 * wide : 3 * wide], 1, n).astype(f32),
        natural_columns(rest[:, :, : 2 * wide], 2, n).astype(f32),
        grad_w_cross.astype(f32),
        mine(early[D : 2 * D]),
        natural_columns(rest[:, :, 3 * wide :], 2, n).astype(f32),
        mine(early[3 * D :]),
        grad_w_down.astype(f32),
        mine(early[2 * D : 3 * D]),
    )


def solution(mesh):
    rows_of = P("fsdp", "seq", None)
    matrix = P(ALL, None)
    vector = P(ALL)
    return jax.shard_map(
        shards,
        mesh=mesh,
        in_specs=(
            rows_of,
            P("fsdp", None, None, None),
            P("fsdp", None),
            rows_of,
            vector,
            matrix,
            matrix,
            vector,
            matrix,
            matrix,
            matrix,
            vector,
            matrix,
            vector,
            matrix,
            vector,
        ),
        out_specs=(
            rows_of,
            rows_of,
            P("fsdp", None, None, None),
            vector,
            matrix,
            matrix,
            vector,
            matrix,
            matrix,
            matrix,
            vector,
            matrix,
            vector,
            matrix,
            vector,
        ),
        check_vma=False,
    )
```

```python
import functools

import jax
import jax.numpy as jnp
from jax import lax
from jax.experimental import pallas as pl
from jax.experimental.pallas import tpu as pltpu
from jax.sharding import PartitionSpec as P

D = 1536
HEADS = 24
HEAD = 64
FF = 6144
COND = 130
SEQS_GRP = 2
LANES = 128

epsilon = 1e-05
masked_score = -1e30
bf16 = jnp.bfloat16
f32 = jnp.float32
ALL = ("seq", "fsdp")


def seq_info(global_rows, group_lengths):
    ends = jnp.cumsum(group_lengths)
    starts = ends - group_lengths
    ident = jnp.sum((global_rows[:, None] >= ends[None, :]).astype(jnp.int32), axis=1)
    onehot = ident[:, None] == jnp.arange(group_lengths.shape[0], dtype=jnp.int32)[None, :]
    begin = jnp.sum(jnp.where(onehot, starts[None, :], 0), axis=1)
    return (ident, (global_rows - begin).astype(f32))


def angle_tables(positions):
    half = HEAD // 2
    inverse = jnp.power(10000.0, -jnp.arange(half, dtype=f32) / half)
    turned = positions[:, None] * inverse[None, :]
    cosine, sine = jnp.cos(turned), jnp.sin(turned)
    reps = LANES // HEAD
    return (
        jnp.concatenate([cosine, cosine] * reps, axis=1),
        jnp.concatenate([-sine, sine] * reps, axis=1),
    )


def norm_rows(values, gain):
    centre = values - jnp.mean(values, axis=-1, keepdims=True)
    spread = jnp.mean(centre * centre, axis=-1, keepdims=True)
    scaled = lax.rsqrt(spread + epsilon)
    normal = centre * scaled
    return (normal, scaled, normal * gain)


def norm_back(grad_rows, normal, scaled, gain):
    weighted = grad_rows * gain
    mean_one = jnp.mean(weighted, axis=-1, keepdims=True)
    mean_two = jnp.mean(weighted * normal, axis=-1, keepdims=True)
    return (scaled * (weighted - mean_one - normal * mean_two), jnp.sum(grad_rows * normal, axis=0))


def dot(left, right):
    return jnp.dot(left, right, preferred_element_type=f32)


def outer_sum(left, right):
    return lax.dot_general(left, right, (((0,), (0,)), ((), ())), preferred_element_type=f32)


def back_prod(left, weight):
    return lax.dot_general(left, weight, (((1,), (1,)), ((), ())), preferred_element_type=f32)


def hop(value, j):
    return lax.ppermute(value, "seq", [(i, i ^ j) for i in range(4)])


def block_ids(n):
    if n == 4:
        return lax.axis_index("seq") ^ jnp.arange(n, dtype=jnp.int32)
    return jnp.arange(n, dtype=jnp.int32)


def gather_rows(value, n):
    if n != 4:
        return lax.all_gather(value, "seq", axis=0, tiled=True)
    half = value.shape[0] // 2
    first, second = hop(value, 1), hop(value, 2)
    third, fourth = hop(second[:half], 1), hop(first[half:], 2)
    return jnp.concatenate([value, first, second, third, fourth], axis=0)


def scatter_rows(blocks, n):
    if n != 4:
        whole = jnp.concatenate([blocks(j) for j in range(n)], axis=0)
        return lax.psum_scatter(whole.astype(bf16), "seq", scatter_dimension=0, tiled=True).astype(f32)
    last = blocks(3).astype(bf16)
    half = last.shape[0] // 2
    to_first, to_second = hop(last[:half], 1), hop(last[half:], 2)
    one, two = blocks(1), blocks(2)
    plain_one, plain_two = hop(one[:half].astype(bf16), 1), hop(two[half:].astype(bf16), 2)
    sum_one = hop((one[half:] + to_second.astype(f32)).astype(bf16), 1)
    sum_two = hop((two[:half] + to_first.astype(f32)).astype(bf16), 2)
    own = blocks(0)
    return own + jnp.concatenate(
        [
            plain_one.astype(f32) + sum_two.astype(f32),
            sum_one.astype(f32) + plain_two.astype(f32),
        ],
        axis=0,
    )


def swap_halves(value):
    lane = lax.broadcasted_iota(jnp.int32, value.shape, 1)
    half = HEAD // 2
    return jnp.where(
        lane % HEAD < half, pltpu.roll(value, LANES - half, 1), pltpu.roll(value, half, 1)
    )


def head_rows(h):
    return slice(h * HEAD, (h + 1) * HEAD)


def lane_mask(value, h):
    lane = lax.broadcasted_iota(jnp.int32, value.shape, 1)
    return jnp.where(lane // HEAD == h, value, jnp.zeros_like(value))


def row_mask(value, h):
    row = lax.broadcasted_iota(jnp.int32, value.shape, 0)
    return jnp.where(row // HEAD == h, value, jnp.zeros_like(value))


def attend_kernel(rope, tile, *refs):
    if rope:
        q_ref, k_ref, v_ref, cos_ref, sin_ref, qid_ref, kid_ref = refs[:7]
        qo_ref, ko_ref, vo_ref, o_ref, lse_ref, qt, vt, ot, kb = refs[7:]
        q, k = q_ref[...], k_ref[...]
        q = (q * cos_ref[...] + swap_halves(q) * sin_ref[...]).astype(bf16)
        k = (k * cos_ref[...] + swap_halves(k) * sin_ref[...]).astype(bf16)
        v = v_ref[...].astype(bf16)
        qo_ref[...] = q
        ko_ref[...] = k
        vo_ref[...] = v
    else:
        q_ref, k_ref, v_ref, qid_ref, kid_ref, o_ref, lse_ref, qt, vt, ot, kb = refs
        q, k, v = q_ref[...], k_ref[...], v_ref[...]
    kb[...] = k
    qt[...] = q.astype(f32).T.astype(bf16)
    vt[...] = v.astype(f32).T.astype(bf16)

    def body(t, carry):
        at = pl.ds(pl.multiple_of(t * tile, tile), tile)
        queries = qt[:, at]
        allowed = kid_ref[...] == qid_ref[:, at]
        for h in range(LANES // HEAD):
            s = dot(kb[...], row_mask(queries, h)) * 0.125
            s = jnp.where(allowed, s, masked_score)
            top = jnp.max(s, axis=0, keepdims=True)
            e = jnp.exp(s - top)
            total = jnp.sum(e, axis=0, keepdims=True)
            p = (e * (1.0 / total)).astype(bf16)
            ot[head_rows(h), at] = dot(vt[head_rows(h), :], p)
            lse_ref[0, h : h + 1, at] = top + jnp.log(total)
        return carry

    lax.fori_loop(0, qt.shape[1] // tile, body, 0)
    o_ref[...] = ot[...].T.astype(bf16)


def attend_back_kernel(rope, tile, *refs):
    if rope:
        q_ref, k_ref, v_ref, do_ref, o_ref, lse_ref, cos_ref, sin_ref, qid_ref, kid_ref = refs[:10]
        dq_ref, dk_ref, dv_ref, qt, dot_t, kt, dqt, dk_acc, dv_acc, delta = refs[10:]
    else:
        q_ref, k_ref, v_ref, do_ref, o_ref, lse_ref, qid_ref, kid_ref = refs[:8]
        dq_ref, dk_ref, dv_ref, qt, dot_t, kt, dqt, dk_acc, dv_acc, delta = refs[8:]
    qt[...] = q_ref[...].astype(f32).T.astype(bf16)
    kt[...] = k_ref[...].astype(f32).T.astype(bf16)
    dof_t = do_ref[...].astype(f32).T
    dot_t[...] = dof_t.astype(bf16)
    product = dof_t * o_ref[...].astype(f32).T
    for h in range(LANES // HEAD):
        delta[h : h + 1, :] = jnp.sum(product[head_rows(h), :], axis=0, keepdims=True)
    dk_acc[...] = jnp.zeros_like(dk_acc)
    dv_acc[...] = jnp.zeros_like(dv_acc)

    def body(t, carry):
        at = pl.ds(pl.multiple_of(t * tile, tile), tile)
        allowed = kid_ref[...] == qid_ref[:, at]
        for h in range(LANES // HEAD):
            s = dot(k_ref[...], row_mask(qt[:, at], h)) * 0.125
            p = jnp.where(allowed, jnp.exp(s - lse_ref[0, h : h + 1, at]), 0.0)
            dp = dot(v_ref[...], row_mask(dot_t[:, at], h))
            dv_acc[...] += dot(p.astype(bf16), lane_mask(do_ref[at, :], h))
            ds = (p * (dp - delta[h : h + 1, at])).astype(bf16)
            dk_acc[...] += dot(ds, lane_mask(q_ref[at, :], h))
            dqt[head_rows(h), at] = dot(kt[head_rows(h), :], ds)
        return carry

    lax.fori_loop(0, qt.shape[1] // tile, body, 0)
    dq = dqt[...].T * 0.125
    dk = dk_acc[...] * 0.125
    if rope:
        dq = dq * cos_ref[...] - swap_halves(dq) * sin_ref[...]
        dk = dk * cos_ref[...] - swap_halves(dk) * sin_ref[...]
    dq_ref[...] = dq.astype(bf16)
    dk_ref[...] = dk.astype(bf16)
    dv_ref[...] = dv_acc[...].astype(bf16)


def query_tile(rows):
    for tile in (256, 128):
        if rows % tile == 0:
            return tile
    return rows


def spec(rows, offset=0):
    return pl.BlockSpec((rows, LANES), lambda i: (0, i + offset))


def whole(shape):
    return pl.BlockSpec(shape, lambda i: (0,) * len(shape), pipeline_mode=pl.Buffered(1))


LIMIT = 56 * 1024 * 1024


def attend(q, k, v, offsets, pairs, qid, kid, tables=None):
    nq, nk = q.shape[0], k.shape[0]
    rope = tables is not None
    tile = query_tile(nq)
    ins = [spec(nq, offsets[0]), spec(nk, offsets[1]), spec(nk, offsets[2])]
    args = [q, k, v]
    outs, shapes = [], []
    if rope:
        ins += [whole((nq, LANES)), whole((nq, LANES))]
        args += list(tables)
        outs += [spec(nq), spec(nk), spec(nk)]
        shapes += [jax.ShapeDtypeStruct((rows, pairs * LANES), bf16) for rows in (nq, nk, nk)]
    ins += [whole((1, nq)), whole((nk, 1))]
    args += [qid[None, :], kid[:, None]]
    outs += [spec(nq), pl.BlockSpec((1, 8, nq), lambda i: (i, 0, 0))]
    shapes += [
        jax.ShapeDtypeStruct((nq, pairs * LANES), bf16),
        jax.ShapeDtypeStruct((pairs, 8, nq), f32),
    ]
    return pl.pallas_call(
        functools.partial(attend_kernel, rope, tile),
        out_shape=shapes,
        grid=(pairs,),
        in_specs=ins,
        out_specs=outs,
        scratch_shapes=[
            pltpu.VMEM((LANES, nq), bf16),
            pltpu.VMEM((LANES, nk), bf16),
            pltpu.VMEM((LANES, nq), f32),
            pltpu.VMEM((nk, LANES), bf16),
        ],
        compiler_params=pltpu.CompilerParams(vmem_limit_bytes=LIMIT),
        cost_estimate=pl.CostEstimate(
            flops=2 * 2 * 2 * pairs * nq * nk * LANES,
            bytes_accessed=pairs * LANES * (nq + nk) * 12,
            transcendentals=2 * pairs * nq * nk,
        ),
        name="attend_self" if rope else "attend_cross",
    )(*args)


def attend_back(q, k, v, offsets, pairs, grad, mixed, lse, qid, kid, tables=None):
    nq, nk = q.shape[0], k.shape[0]
    rope = tables is not None
    tile = query_tile(nq)
    ins = [spec(nq, offsets[0]), spec(nk, offsets[1]), spec(nk, offsets[2]), spec(nq), spec(nq)]
    args = [q, k, v, grad, mixed]
    ins += [pl.BlockSpec((1, 8, nq), lambda i: (i, 0, 0))]
    args += [lse]
    if rope:
        ins += [whole((nq, LANES)), whole((nq, LANES))]
        args += list(tables)
    ins += [whole((1, nq)), whole((nk, 1))]
    args += [qid[None, :], kid[:, None]]
    return pl.pallas_call(
        functools.partial(attend_back_kernel, rope, tile),
        out_shape=[jax.ShapeDtypeStruct((rows, pairs * LANES), bf16) for rows in (nq, nk, nk)],
        grid=(pairs,),
        in_specs=ins,
        out_specs=[spec(nq), spec(nk), spec(nk)],
        scratch_shapes=[
            pltpu.VMEM((LANES, nq), bf16),
            pltpu.VMEM((LANES, nq), bf16),
            pltpu.VMEM((LANES, nk), bf16),
            pltpu.VMEM((LANES, nq), f32),
            pltpu.VMEM((nk, LANES), f32),
            pltpu.VMEM((nk, LANES), f32),
            pltpu.VMEM((8, nq), f32),
        ],
        compiler_params=pltpu.CompilerParams(vmem_limit_bytes=LIMIT),
        cost_estimate=pl.CostEstimate(
            flops=2 * 5 * 2 * pairs * nq * nk * LANES,
            bytes_accessed=pairs * LANES * (nq + nk) * 12,
            transcendentals=2 * pairs * nq * nk,
        ),
        name="back_self" if rope else "back_cross",
    )(*args)


def column_parts(shard, parts, n):
    r, columns = shard.shape
    c = columns // (parts * n)
    return shard.reshape(r, parts, n, c).transpose(2, 0, 1, 3).reshape(n, r, parts * c)


def natural_columns(pieces, parts, n):
    r, columns = pieces.shape[1:]
    c = columns // parts
    return pieces.reshape(n, r, parts, c).transpose(1, 2, 0, 3).reshape(r, parts * n * c)


def to_seq(pieces):
    return lax.all_to_all(pieces, "seq", 0, 0, tiled=True)


def gather_columns(pieces, n, nf):
    r, c = pieces.shape[1:]
    gathered = lax.all_gather(pieces.reshape(n * r, c), "fsdp", axis=0, tiled=True)
    return gathered.reshape(nf, n, r, c).transpose(1, 0, 2, 3).reshape(n * nf * r, c)


def columns_by_owner(grad, n, nf):
    rows, c = grad.shape
    r = rows // (n * nf)
    return grad.astype(bf16).reshape(n, nf, r, c).transpose(1, 0, 2, 3).reshape(rows, c)


def rows_by_owner(grad, n, nf):
    rows, columns = grad.shape
    r = rows // nf
    return grad.reshape(nf, r, n, columns // n).transpose(0, 2, 1, 3).reshape(nf * n * r, columns // n)


def share(rows_of_fsdp, n):
    rows, c = rows_of_fsdp.shape
    return to_seq(rows_of_fsdp.reshape(n, rows // n, c))


def rows_to_pieces(shard, n):
    r, columns = shard.shape
    return shard.reshape(r, n, columns // n).transpose(1, 0, 2).reshape(n * r, columns // n)


def after(value, *others):
    return lax.optimization_barrier((value,) + others)[0]


def sum_over_seq(value, n):
    if n != 4:
        return lax.psum(value, "seq")
    half = value.shape[1] // 2

    def step(part, j):
        low = part.astype(bf16)
        return low.astype(f32) + hop(low, j).astype(f32)

    return jnp.concatenate(
        [step(step(value[:, :half], 1), 2), step(step(value[:, half:], 2), 1)], axis=1
    )


def pad_heads(value, parts):
    rows, columns = value.shape
    c = columns // parts
    if c % LANES == 0:
        return value
    padded = -(-c // LANES) * LANES
    return jnp.pad(value.reshape(rows, parts, c), ((0, 0), (0, 0), (0, padded - c))).reshape(
        rows, parts * padded
    )


def shards(
    tokens,
    conditioning,
    lengths,
    grad_output,
    norm_first,
    proj_self,
    out_self,
    norm_second,
    proj_query,
    proj_keyval,
    out_cross,
    norm_third,
    proj_gateup,
    bias_gateup,
    proj_down,
    bias_down,
):
    rows = tokens.shape[1]
    n = lax.axis_size("seq")
    nf = lax.axis_size("fsdp")
    me = lax.axis_index("seq")
    group = rows * n
    wide = D // n
    pairs = -(-wide // LANES)
    hidden = FF // n
    r = norm_first.shape[0]

    small = jnp.concatenate(
        [v.reshape(r, -1) for v in (norm_first, norm_second, norm_third, bias_down, bias_gateup)],
        axis=1,
    )
    small = jnp.pad(small, ((0, 0), (0, LANES - small.shape[1])))
    self_in = jnp.concatenate(
        [column_parts(proj_self, 3, n), jnp.broadcast_to(small[None], (n, r, LANES))], axis=2
    )
    self_pieces = to_seq(self_in)
    mid_pieces = to_seq(
        after(
            jnp.concatenate([column_parts(proj_keyval, 2, n), column_parts(proj_query, 1, n)], axis=2),
            self_pieces,
        )
    )
    group_tokens = gather_rows(after(tokens[0], self_pieces), n)
    gateup_pieces = to_seq(after(column_parts(proj_gateup, 2, n), mid_pieces))

    self_all = gather_columns(self_pieces, n, nf)
    w_self = self_all[:, : 3 * wide]
    vectors = self_all[:, 3 * wide : 3 * wide + 12]
    gain_one, gain_two, gain_three, b_down = (vectors[:, j].astype(f32) for j in range(4))
    b_gateup = vectors[:, 4:12].reshape(2 * FF).astype(f32)
    b_gate = lax.dynamic_slice_in_dim(b_gateup, me * hidden, hidden, 0)
    b_upper = lax.dynamic_slice_in_dim(b_gateup, FF + me * hidden, hidden, 0)
    mid = jnp.concatenate(
        [
            mid_pieces.reshape(n * r, 3 * wide),
            rows_to_pieces(out_self, n),
            rows_to_pieces(out_cross, n),
        ],
        axis=1,
    )
    mid = lax.all_gather(mid, "fsdp", axis=0, tiled=True).reshape(nf, n, r, 5 * wide)
    kvq = mid[..., : 3 * wide].transpose(1, 0, 2, 3).reshape(D, 3 * wide)
    w_keyval, w_query = kvq[:, : 2 * wide], kvq[:, 2 * wide :]
    w_out = mid[..., 3 * wide : 4 * wide].transpose(0, 2, 1, 3).reshape(nf * r, D)
    w_cross = mid[..., 4 * wide :].transpose(0, 2, 1, 3).reshape(nf * r, D)
    w_gateup = gather_columns(gateup_pieces, n, nf)
    w_down = lax.all_gather(after(proj_down, gateup_pieces), "fsdp", axis=0, tiled=True)

    group_lengths = lengths[0]
    order = block_ids(n)
    all_rows = (order[:, None] * rows + jnp.arange(rows, dtype=jnp.int32)[None, :]).reshape(group)
    ids, positions = seq_info(all_rows, group_lengths)
    tables = angle_tables(positions)

    def block(value, j):
        return lax.slice_in_dim(value, j * rows, (j + 1) * rows, axis=0)

    inputs = tokens[0].astype(f32)
    normal_one, scaled_one, _ = norm_rows(inputs, gain_one)
    normed_one = norm_rows(group_tokens.astype(f32), gain_one)[2].astype(bf16)
    packed = pad_heads(dot(normed_one, w_self), 3)
    group_grad = gather_rows(after(grad_output[0], packed), n)
    q, k, v, mixed, lse = attend(packed, packed, packed, (0, pairs, 2 * pairs), pairs, ids, ids, tables)
    mixed_in = mixed[:, :wide]
    first = inputs + scatter_rows(lambda j: dot(block(mixed_in, j), w_out), n)

    normal_two, scaled_two, normed = norm_rows(first, gain_two)
    normed_two = gather_rows(normed.astype(bf16), n)
    cq = pad_heads(dot(normed_two, w_query).astype(bf16), 1)
    cond_rows = conditioning[0].reshape(SEQS_GRP * COND, D)
    count = SEQS_GRP * COND
    count_pad = -(-count // 16) * 16
    keyval = pad_heads(dot(cond_rows, w_keyval).astype(bf16), 2)
    keyval = jnp.pad(keyval, ((0, count_pad - count), (0, 0)))
    index = jnp.arange(count_pad, dtype=jnp.int32)
    cond_ids = jnp.where(index < count, index // COND, -1)
    cmix, clse = attend(cq, keyval, keyval, (0, 0, pairs), pairs, ids, cond_ids)
    cmix_in = cmix[:, :wide]
    second = first + scatter_rows(lambda j: dot(block(cmix_in, j), w_cross), n)

    normal_three, scaled_three, normed = norm_rows(second, gain_three)
    normed_three = gather_rows(normed.astype(bf16), n)
    gate = dot(normed_three, w_gateup[:, :hidden]) + b_gate
    upper = dot(normed_three, w_gateup[:, hidden:]) + b_upper
    sigma = jax.nn.sigmoid(gate)
    silu_gate = gate * sigma
    active = (silu_gate * upper).astype(bf16)
    result = second + scatter_rows(lambda j: dot(block(active, j), w_down), n) + b_down

    grad_rows = grad_output[0].astype(f32)
    grad_b_down = jnp.sum(grad_rows, axis=0)
    grad_w_down = outer_sum(active, group_grad).astype(bf16)
    grad_active = back_prod(group_grad, w_down)
    grad_gate = grad_active * upper * sigma * (1.0 + gate * (1.0 - sigma))
    grad_upper = grad_active * silu_gate
    grad_gateup = jnp.concatenate([grad_gate, grad_upper], axis=1).astype(bf16)
    own_down = lax.psum_scatter(grad_w_down, "fsdp", scatter_dimension=0, tiled=True)
    grad_gateup, result = lax.optimization_barrier((grad_gateup, result))
    through = scatter_rows(lambda j: back_prod(block(grad_gateup, j), w_gateup), n)
    grad_w_gateup = columns_by_owner(outer_sum(normed_three, grad_gateup), n, nf)
    through, grad_w_gateup = lax.optimization_barrier((through, grad_w_gateup))
    own_gateup = lax.psum_scatter(after(grad_w_gateup, own_down), "fsdp", scatter_dimension=0, tiled=True)
    grad_b_gateup = jnp.sum(grad_gateup.astype(f32), axis=0)
    through, grad_gain_three = norm_back(through, normal_three, scaled_three, gain_three)
    grad_second = grad_rows + through

    group_second = gather_rows(grad_second.astype(bf16), n)
    grad_cmix = pad_heads(back_prod(group_second, w_cross).astype(bf16), 1)
    dcq, dck, dcv = attend_back(
        cq, keyval, keyval, (0, 0, pairs), pairs, grad_cmix, cmix, clse, ids, cond_ids
    )
    dcq, dck, dcv = dcq[:, :wide], dck[:count, :wide], dcv[:count, :wide]
    through = scatter_rows(lambda j: back_prod(block(dcq, j), w_query), n)
    grad_keyval = jnp.concatenate([dck, dcv], axis=1)
    grad_w_cross = outer_sum(cmix_in, group_second).astype(bf16)
    b_whole = lax.dynamic_update_slice(
        jnp.zeros((2, FF), f32), grad_b_gateup.reshape(2, hidden), (0, me * hidden)
    )
    vectors = jnp.concatenate(
        [v.reshape(n, nf, r, -1) for v in (grad_gain_three, grad_b_down, b_whole)], axis=3
    )
    vectors = vectors.astype(bf16).transpose(1, 0, 2, 3).reshape(nf * n * r, -1)
    vectors = jnp.pad(vectors, ((0, 0), (0, LANES - vectors.shape[1])))
    grad_w_mid = jnp.concatenate(
        [
            columns_by_owner(outer_sum(cond_rows, grad_keyval), n, nf),
            columns_by_owner(outer_sum(normed_two, dcq), n, nf),
            vectors,
            rows_by_owner(grad_w_cross, n, nf),
        ],
        axis=1,
    )
    through, grad_w_mid = lax.optimization_barrier((through, grad_w_mid))
    own_mid = lax.psum_scatter(after(grad_w_mid, own_gateup), "fsdp", scatter_dimension=0, tiled=True)
    through, grad_gain_two = norm_back(through, normal_two, scaled_two, gain_two)
    grad_first = grad_second + through

    group_first = gather_rows(grad_first.astype(bf16), n)
    own_gateup = share(after(own_gateup, group_first), n)
    grad_mixed = pad_heads(back_prod(group_first, w_out).astype(bf16), 1)
    grad_w_out = outer_sum(mixed_in, group_first).astype(bf16)
    dq, dk, dv = attend_back(q, k, v, (0, 0, 0), pairs, grad_mixed, mixed, lse, ids, ids, tables)
    own_gateup = after(own_gateup, dq)
    grad_packed = jnp.concatenate([dq[:, :wide], dk[:, :wide], dv[:, :wide]], axis=1)
    w_grad = outer_sum(normed_one, grad_packed)
    gain_part = (jnp.sum(w_grad * w_self.astype(f32), axis=1) / gain_one).reshape(n, nf, r, 1)
    gain_part = jnp.concatenate([gain_part, grad_gain_two.reshape(n, nf, r, 1)], axis=3)
    gain_part = gain_part.astype(bf16).transpose(1, 0, 2, 3).reshape(nf * n * r, 2)
    grad_w_self = jnp.concatenate(
        [
            columns_by_owner(w_grad, n, nf),
            jnp.pad(gain_part, ((0, 0), (0, LANES - 2))),
            rows_by_owner(grad_w_out, n, nf),
        ],
        axis=1,
    )
    grad_packed, grad_w_self, own_gateup = lax.optimization_barrier((grad_packed, grad_w_self, own_gateup))
    own_self = lax.psum_scatter(after(grad_w_self, own_mid), "fsdp", scatter_dimension=0, tiled=True)
    through = scatter_rows(lambda j: back_prod(block(grad_packed, j), w_self), n)
    grad_cond = sum_over_seq(after(back_prod(grad_keyval, w_keyval), through), n)
    grad_cond = grad_cond.reshape(1, SEQS_GRP, COND, D)
    grad_inputs = grad_first + norm_back(through, normal_one, scaled_one, gain_one)[0]

    def joined(pieces):
        return pieces.reshape(n, r, wide).transpose(1, 0, 2).reshape(r, D)

    split = 3 * wide + LANES
    mid_part = share(own_mid[:, :split], n)
    vectors = jnp.sum(mid_part[:, :, 3 * wide :].astype(f32), axis=0)
    own_cross = joined(own_mid[:, split:])
    own_out = joined(own_self[:, split:])
    self_part = share(own_self[:, :split], n)
    gains = jnp.sum(self_part[:, :, 3 * wide :].astype(f32), axis=0)

    return (
        result.astype(bf16)[None],
        grad_inputs[None],
        grad_cond,
        gains[:, 0],
        natural_columns(self_part[:, :, : 3 * wide], 3, n).astype(f32),
        own_out.astype(f32),
        gains[:, 1],
        natural_columns(mid_part[:, :, 2 * wide : 3 * wide], 1, n).astype(f32),
        natural_columns(mid_part[:, :, : 2 * wide], 2, n).astype(f32),
        own_cross.astype(f32),
        vectors[:, 0],
        natural_columns(own_gateup, 2, n).astype(f32),
        vectors[:, 2:10].reshape(8 * r),
        own_down.astype(f32),
        vectors[:, 1],
    )


def solution(mesh):
    rows_of = P("fsdp", "seq", None)
    matrix = P(ALL, None)
    vector = P(ALL)
    return jax.shard_map(
        shards,
        mesh=mesh,
        in_specs=(
            rows_of,
            P("fsdp", None, None, None),
            P("fsdp", None),
            rows_of,
            vector,
            matrix,
            matrix,
            vector,
            matrix,
            matrix,
            matrix,
            vector,
            matrix,
            vector,
            matrix,
            vector,
        ),
        out_specs=(
            rows_of,
            rows_of,
            P("fsdp", None, None, None),
            vector,
            matrix,
            matrix,
            vector,
            matrix,
            matrix,
            matrix,
            vector,
            matrix,
            vector,
            matrix,
            vector,
        ),
        check_vma=False,
    )
```

```python
import functools

import jax
import jax.numpy as jnp
from jax import lax
from jax.experimental import pallas as pl
from jax.experimental.pallas import tpu as pltpu
from jax.sharding import PartitionSpec as P

D = 1536
HEADS = 24
HEAD = 64
FF = 6144
COND = 130
SEQS_GRP = 2
LANES = 128

epsilon = 1e-05
masked_score = -1e30
bf16 = jnp.bfloat16
f32 = jnp.float32
ALL = ("seq", "fsdp")


def seq_info(global_rows, group_lengths):
    ends = jnp.cumsum(group_lengths)
    starts = ends - group_lengths
    ident = jnp.sum((global_rows[:, None] >= ends[None, :]).astype(jnp.int32), axis=1)
    onehot = ident[:, None] == jnp.arange(group_lengths.shape[0], dtype=jnp.int32)[None, :]
    begin = jnp.sum(jnp.where(onehot, starts[None, :], 0), axis=1)
    return (ident, (global_rows - begin).astype(f32))


def angle_tables(positions):
    half = HEAD // 2
    inverse = jnp.power(10000.0, -jnp.arange(half, dtype=f32) / half)
    turned = positions[:, None] * inverse[None, :]
    cosine, sine = jnp.cos(turned), jnp.sin(turned)
    reps = LANES // HEAD
    return (
        jnp.concatenate([cosine, cosine] * reps, axis=1),
        jnp.concatenate([-sine, sine] * reps, axis=1),
    )


def norm_rows(values, gain):
    centre = values - jnp.mean(values, axis=-1, keepdims=True)
    spread = jnp.mean(centre * centre, axis=-1, keepdims=True)
    scaled = lax.rsqrt(spread + epsilon)
    normal = centre * scaled
    return (normal, scaled, normal * gain)


def norm_back(grad_rows, normal, scaled, gain):
    weighted = grad_rows * gain
    mean_one = jnp.mean(weighted, axis=-1, keepdims=True)
    mean_two = jnp.mean(weighted * normal, axis=-1, keepdims=True)
    return (scaled * (weighted - mean_one - normal * mean_two), jnp.sum(grad_rows * normal, axis=0))


def dot(left, right):
    return jnp.dot(left, right, preferred_element_type=f32)


def outer_sum(left, right):
    return lax.dot_general(left, right, (((0,), (0,)), ((), ())), preferred_element_type=f32)


def back_prod(left, weight):
    return lax.dot_general(left, weight, (((1,), (1,)), ((), ())), preferred_element_type=f32)


def hop(value, j):
    return lax.ppermute(value, "seq", [(i, i ^ j) for i in range(4)])


def block_ids(n):
    if n == 4:
        return lax.axis_index("seq") ^ jnp.arange(n, dtype=jnp.int32)
    return jnp.arange(n, dtype=jnp.int32)


def gather_rows(value, n):
    if n != 4:
        return lax.all_gather(value, "seq", axis=0, tiled=True)
    half = value.shape[0] // 2
    first, second = hop(value, 1), hop(value, 2)
    third, fourth = hop(second[:half], 1), hop(first[half:], 2)
    return jnp.concatenate([value, first, second, third, fourth], axis=0)


def scatter_rows(blocks, n):
    if n != 4:
        whole = jnp.concatenate([blocks(j) for j in range(n)], axis=0)
        return lax.psum_scatter(whole.astype(bf16), "seq", scatter_dimension=0, tiled=True).astype(f32)
    last = blocks(3).astype(bf16)
    half = last.shape[0] // 2
    to_first, to_second = hop(last[:half], 1), hop(last[half:], 2)
    one, two = blocks(1), blocks(2)
    plain_one, plain_two = hop(one[:half].astype(bf16), 1), hop(two[half:].astype(bf16), 2)
    sum_one = hop((one[half:] + to_second.astype(f32)).astype(bf16), 1)
    sum_two = hop((two[:half] + to_first.astype(f32)).astype(bf16), 2)
    own = blocks(0)
    return own + jnp.concatenate(
        [
            plain_one.astype(f32) + sum_two.astype(f32),
            sum_one.astype(f32) + plain_two.astype(f32),
        ],
        axis=0,
    )


def swap_halves(value):
    lane = lax.broadcasted_iota(jnp.int32, value.shape, 1)
    half = HEAD // 2
    return jnp.where(
        lane % HEAD < half, pltpu.roll(value, LANES - half, 1), pltpu.roll(value, half, 1)
    )


def head_rows(h):
    return slice(h * HEAD, (h + 1) * HEAD)


def lane_mask(value, h):
    lane = lax.broadcasted_iota(jnp.int32, value.shape, 1)
    return jnp.where(lane // HEAD == h, value, jnp.zeros_like(value))


FAR = 1e30


def pieces_of(value):
    high = value.astype(bf16).astype(f32)
    rest = value - high
    middle = rest.astype(bf16).astype(f32)
    return high, middle, rest - middle


def key_lanes(keys, kid, h):
    lane = lax.broadcasted_iota(jnp.int32, keys.shape, 1)
    spare = lane % HEAD
    ones = jnp.where(spare <= SEQS_GRP + 3, 1.0, 0.0)
    padding = jnp.where(spare == SEQS_GRP, jnp.where(kid < 0, 1.0, 0.0), ones)
    extra = jnp.where(spare < SEQS_GRP, jnp.where(kid == spare, 1.0, 0.0), padding)
    return jnp.where(lane // HEAD == h, keys.astype(f32), extra).astype(bf16)


def query_rows(turned, qid, h, offsets=()):
    row = lax.broadcasted_iota(jnp.int32, turned.shape, 0)
    spare = row % HEAD
    extra = jnp.where(spare <= SEQS_GRP, jnp.where(qid == spare, 0.0, -FAR), 0.0)
    for j, offset in enumerate(offsets):
        extra = jnp.where(spare == SEQS_GRP + 1 + j, offset, extra)
    return jnp.where(row // HEAD == h, turned, extra).astype(bf16)


def value_lanes(values, h):
    lane = lax.broadcasted_iota(jnp.int32, values.shape, 1)
    ones = jnp.where(lane % HEAD < 3, 1.0, 0.0)
    return jnp.where(lane // HEAD == h, values.astype(f32), ones).astype(bf16)


def grad_rows_of(turned, h, offsets):
    row = lax.broadcasted_iota(jnp.int32, turned.shape, 0)
    extra = jnp.zeros_like(turned)
    for j, offset in enumerate(offsets):
        extra = jnp.where(row % HEAD == j, offset, extra)
    return jnp.where(row // HEAD == h, turned, extra).astype(bf16)


PAIR = LANES // HEAD


def attend_kernel(rope, tile, *refs):
    if rope:
        q_ref, k_ref, v_ref, cos_ref, sin_ref, qid_ref, kid_ref = refs[:7]
        qo_ref, ko_ref, vo_ref, o_ref, lse_ref, qt, kb, vt, ot = refs[7:]
        q, k = q_ref[...], k_ref[...]
        q = (q * cos_ref[...] + swap_halves(q) * sin_ref[...]).astype(bf16)
        k = (k * cos_ref[...] + swap_halves(k) * sin_ref[...]).astype(bf16)
        v = v_ref[...].astype(bf16)
        qo_ref[...] = q
        ko_ref[...] = k
        vo_ref[...] = v
    else:
        q_ref, k_ref, v_ref, qid_ref, kid_ref, o_ref, lse_ref, qt, kb, vt, ot = refs
        q, k, v = q_ref[...], k_ref[...], v_ref[...]
    turned = q.astype(f32).T * 0.125
    for h in range(PAIR):
        qt[h] = query_rows(turned, qid_ref[...], h)
        kb[h] = key_lanes(k, kid_ref[...], h)
    vt[...] = v.astype(f32).T.astype(bf16)
    units = [(t * tile, h) for t in range(ot.shape[1] // tile) for h in range(PAIR)]

    def scores(unit):
        start, h = unit
        return dot(kb[h], qt[h, :, start : start + tile])

    later = scores(units[0])
    for i, (start, h) in enumerate(units):
        s = later
        if i + 1 < len(units):
            later = scores(units[i + 1])
        at = slice(start, start + tile)
        top = jnp.max(s, axis=0, keepdims=True)
        e = jnp.exp(s - top)
        total = jnp.sum(e, axis=0, keepdims=True)
        ot[head_rows(h), at] = dot(vt[head_rows(h), :], e.astype(bf16)) * (1.0 / total)
        lse_ref[0, h : h + 1, at] = top + jnp.log(total)
    o_ref[...] = ot[...].T.astype(bf16)


def attend_back_kernel(rope, tile, *refs):
    if rope:
        q_ref, k_ref, v_ref, do_ref, o_ref, lse_ref, cos_ref, sin_ref, qid_ref, kid_ref = refs[:10]
        dq_ref, dk_ref, dv_ref, qt, gt, kb, vb, kt, dqt, dk_acc, dv_acc = refs[10:]
    else:
        q_ref, k_ref, v_ref, do_ref, o_ref, lse_ref, qid_ref, kid_ref = refs[:8]
        dq_ref, dk_ref, dv_ref, qt, gt, kb, vb, kt, dqt, dk_acc, dv_acc = refs[8:]
    turned = q_ref[...].astype(f32).T * 0.125
    grads = do_ref[...].astype(f32).T
    product = grads * o_ref[...].astype(f32).T
    kt[...] = k_ref[...].astype(f32).T.astype(bf16)
    for h in range(PAIR):
        delta = jnp.sum(product[head_rows(h), :], axis=0, keepdims=True)
        qt[h] = query_rows(turned, qid_ref[...], h, pieces_of(-lse_ref[0, h : h + 1, :]))
        gt[h] = grad_rows_of(grads, h, pieces_of(-delta))
        kb[h] = key_lanes(k_ref[...], kid_ref[...], h)
        vb[h] = value_lanes(v_ref[...], h)
    tiles = dqt.shape[1] // tile
    units = [(t * tile, h) for t in range(tiles) for h in range(PAIR)]

    def products(unit):
        start, h = unit
        at = slice(start, start + tile)
        return dot(kb[h], qt[h, :, at]), dot(vb[h], gt[h, :, at])

    later = products(units[0])
    low_p, low_ds = [], []
    for i, (start, h) in enumerate(units):
        s, dp = later
        if i + 1 < len(units):
            later = products(units[i + 1])
        at = slice(start, start + tile)
        p = jnp.exp(s)
        ds = (p * dp).astype(bf16)
        dqt[head_rows(h), at] = dot(kt[head_rows(h), :], ds)
        low_p.append(p.astype(bf16))
        low_ds.append(ds)
        if h == PAIR - 1:
            rows_do = jnp.concatenate([lane_mask(do_ref[at, :], j) for j in range(PAIR)], axis=0)
            rows_q = jnp.concatenate([lane_mask(q_ref[at, :], j) for j in range(PAIR)], axis=0)
            dv = dot(jnp.concatenate(low_p, axis=1), rows_do)
            dk = dot(jnp.concatenate(low_ds, axis=1), rows_q)
            dv_acc[...] = dv if start == 0 else dv_acc[...] + dv
            dk_acc[...] = dk if start == 0 else dk_acc[...] + dk
            low_p, low_ds = [], []
    dq = dqt[...].T * 0.125
    dk = dk_acc[...] * 0.125
    if rope:
        dq = dq * cos_ref[...] - swap_halves(dq) * sin_ref[...]
        dk = dk * cos_ref[...] - swap_halves(dk) * sin_ref[...]
    dq_ref[...] = dq.astype(bf16)
    dk_ref[...] = dk.astype(bf16)
    dv_ref[...] = dv_acc[...].astype(bf16)


def query_tile(rows):
    for tile in (256, 128):
        if rows % tile == 0:
            return tile
    return rows


def spec(rows, offset=0):
    return pl.BlockSpec((rows, LANES), lambda i: (0, i + offset))


def whole(shape):
    return pl.BlockSpec(shape, lambda i: (0,) * len(shape), pipeline_mode=pl.Buffered(1))


LIMIT = 56 * 1024 * 1024
TILE, CHUNK, GTILE = 256, 320, 512


def attend(q, k, v, offsets, pairs, qid, kid, tables=None):
    nq, nk = q.shape[0], k.shape[0]
    rope = tables is not None
    tile = query_tile(nq)
    ins = [spec(nq, offsets[0]), spec(nk, offsets[1]), spec(nk, offsets[2])]
    args = [q, k, v]
    outs, shapes = [], []
    if rope:
        ins += [whole((nq, LANES)), whole((nq, LANES))]
        args += list(tables)
        outs += [spec(nq), spec(nk), spec(nk)]
        shapes += [jax.ShapeDtypeStruct((rows, pairs * LANES), bf16) for rows in (nq, nk, nk)]
    ins += [whole((1, nq)), whole((nk, 1))]
    args += [qid[None, :], kid[:, None]]
    outs += [spec(nq), pl.BlockSpec((1, 8, nq), lambda i: (i, 0, 0))]
    shapes += [
        jax.ShapeDtypeStruct((nq, pairs * LANES), bf16),
        jax.ShapeDtypeStruct((pairs, 8, nq), f32),
    ]
    return pl.pallas_call(
        functools.partial(attend_kernel, rope, tile),
        out_shape=shapes,
        grid=(pairs,),
        in_specs=ins,
        out_specs=outs,
        scratch_shapes=[
            pltpu.VMEM((PAIR, LANES, nq), bf16),
            pltpu.VMEM((PAIR, nk, LANES), bf16),
            pltpu.VMEM((LANES, nk), bf16),
            pltpu.VMEM((LANES, nq), f32),
        ],
        compiler_params=pltpu.CompilerParams(vmem_limit_bytes=LIMIT),
        cost_estimate=pl.CostEstimate(
            flops=2 * 2 * 2 * pairs * nq * nk * LANES,
            bytes_accessed=pairs * LANES * (nq + nk) * 12,
            transcendentals=2 * pairs * nq * nk,
        ),
        name="attend_self" if rope else "attend_cross",
    )(*args)


def attend_back(q, k, v, offsets, pairs, grad, mixed, lse, qid, kid, tables=None):
    nq, nk = q.shape[0], k.shape[0]
    rope = tables is not None
    tile = query_tile(nq)
    ins = [spec(nq, offsets[0]), spec(nk, offsets[1]), spec(nk, offsets[2]), spec(nq), spec(nq)]
    args = [q, k, v, grad, mixed]
    ins += [pl.BlockSpec((1, 8, nq), lambda i: (i, 0, 0))]
    args += [lse]
    if rope:
        ins += [whole((nq, LANES)), whole((nq, LANES))]
        args += list(tables)
    ins += [whole((1, nq)), whole((nk, 1))]
    args += [qid[None, :], kid[:, None]]
    return pl.pallas_call(
        functools.partial(attend_back_kernel, rope, tile),
        out_shape=[jax.ShapeDtypeStruct((rows, pairs * LANES), bf16) for rows in (nq, nk, nk)],
        grid=(pairs,),
        in_specs=ins,
        out_specs=[spec(nq), spec(nk), spec(nk)],
        scratch_shapes=[
            pltpu.VMEM((PAIR, LANES, nq), bf16),
            pltpu.VMEM((PAIR, LANES, nq), bf16),
            pltpu.VMEM((PAIR, nk, LANES), bf16),
            pltpu.VMEM((PAIR, nk, LANES), bf16),
            pltpu.VMEM((LANES, nk), bf16),
            pltpu.VMEM((LANES, nq), f32),
            pltpu.VMEM((nk, LANES), f32),
            pltpu.VMEM((nk, LANES), f32),
        ],
        compiler_params=pltpu.CompilerParams(vmem_limit_bytes=LIMIT),
        cost_estimate=pl.CostEstimate(
            flops=2 * 5 * 2 * pairs * nq * nk * LANES,
            bytes_accessed=pairs * LANES * (nq + nk) * 12,
            transcendentals=2 * pairs * nq * nk,
        ),
        name="back_self" if rope else "back_cross",
    )(*args)


def contract(left, right, dims):
    return lax.dot_general(left, right, (dims, ((), ())), preferred_element_type=f32)


def feed_kernel(chunk, *refs):
    h_ref, gy_ref, wg_ref, wu_ref, wd_ref, bg_ref, bu_ref = refs[:7]
    act_ref, dg_ref, du_ref, sg_ref, su_ref, dh_ref, both, total = refs[7:]
    step = pl.program_id(0)
    span = wg_ref.shape[0] * wg_ref.shape[2]
    tile = wg_ref.shape[3]
    for j in range(wg_ref.shape[1]):
        at = slice(j * span, (j + 1) * span)
        both[at, :tile] = wg_ref[:, j].reshape(span, tile)
        both[at, tile:] = wu_ref[:, j].reshape(span, tile)
    sg_ref[...] = jnp.zeros_like(sg_ref)
    su_ref[...] = jnp.zeros_like(su_ref)

    @pl.when(step == 0)
    def _():
        total[...] = jnp.zeros_like(total)

    def rows_at(i):
        return slice(i * chunk, (i + 1) * chunk)

    def products(i):
        at = rows_at(i)
        return dot(h_ref[at, :], both[...]), contract(gy_ref[at, :], wd_ref[...], ((1,), (1,)))

    def finish(i, pair, grad):
        at = rows_at(i)
        gate = pair[:, :tile] + bg_ref[...]
        upper = pair[:, tile:] + bu_ref[...]
        sigma = jax.nn.sigmoid(gate)
        silu = gate * sigma
        act_ref[at, :] = (silu * upper).astype(bf16)
        dg = (grad * upper * sigma * (1.0 + gate * (1.0 - sigma))).astype(bf16)
        du = (grad * silu).astype(bf16)
        dg_ref[at, :] = dg
        du_ref[at, :] = du
        sg_ref[...] += jnp.sum(dg.astype(f32), axis=0, keepdims=True)
        su_ref[...] += jnp.sum(du.astype(f32), axis=0, keepdims=True)
        return jnp.concatenate([dg, du], axis=1)

    chunks = h_ref.shape[0] // chunk
    now = products(0)
    for i in range(chunks):
        later = products(i + 1) if i + 1 < chunks else None
        grads = finish(i, *now)
        total[rows_at(i), :] += contract(grads, both[...], ((1,), (1,)))
        now = later

    @pl.when(step == pl.num_programs(0) - 1)
    def _():
        dh_ref[...] = total[...].astype(bf16)


def feed(h, gy, w_gateup, w_down, b_gate, b_upper):
    rows = h.shape[0]
    hidden = w_down.shape[0]
    tile = TILE if rows <= 1280 else 128
    steps = hidden // tile
    lead = w_gateup.shape[:3]
    chunk = CHUNK if rows % CHUNK == 0 else rows
    one = pl.Buffered(1)
    rows_all = pl.BlockSpec((rows, D), lambda t: (0, 0), pipeline_mode=one)
    columns = pl.BlockSpec((rows, tile), lambda t: (0, t))
    vector = pl.BlockSpec((1, tile), lambda t: (0, t))
    return pl.pallas_call(
        functools.partial(feed_kernel, chunk),
        out_shape=[jax.ShapeDtypeStruct((rows, hidden), bf16)] * 3
        + [jax.ShapeDtypeStruct((1, hidden), f32)] * 2
        + [jax.ShapeDtypeStruct((rows, D), bf16)],
        grid=(steps,),
        in_specs=[
            rows_all,
            rows_all,
            pl.BlockSpec(lead + (tile,), lambda t: (0, 0, 0, t)),
            pl.BlockSpec(lead + (tile,), lambda t: (0, 0, 0, t + steps)),
            pl.BlockSpec((tile, D), lambda t: (t, 0)),
            vector,
            vector,
        ],
        out_specs=[columns, columns, columns, vector, vector, rows_all],
        scratch_shapes=[
            pltpu.VMEM((D, 2 * tile), bf16),
            pltpu.VMEM((rows, D), f32),
        ],
        compiler_params=pltpu.CompilerParams(vmem_limit_bytes=LIMIT),
        cost_estimate=pl.CostEstimate(
            flops=2 * 5 * rows * D * hidden,
            bytes_accessed=2 * (3 * rows * D + 3 * rows * hidden + 3 * D * hidden),
            transcendentals=rows * hidden,
        ),
        name="feed",
    )(h, gy, w_gateup, w_gateup, w_down, b_gate[None], b_upper[None])


def place_rows(out_ref, start, value):
    nf, _, r, _ = out_ref.shape
    width = value.shape[1]
    out_ref[:, 0, :, start : start + width] = value.astype(bf16).reshape(nf, r, width)


def gateup_kernel(h_ref, dg_ref, du_ref, out_ref, turned):
    step = pl.program_id(0)
    half = pl.num_programs(0) // 2
    nf, n, r, tile = out_ref.shape
    wide = nf * r

    @pl.when(step == 0)
    def _():
        for s in range(n):
            at = slice(s * wide, (s + 1) * wide)
            turned[at, :] = h_ref[:, at].T

    def fill(grad):
        for s in range(n):
            value = dot(turned[s * wide : (s + 1) * wide, :], grad)
            out_ref[:, s] = value.astype(bf16).reshape(nf, r, tile)

    @pl.when(step < half)
    def _():
        fill(dg_ref[...])

    @pl.when(step >= half)
    def _():
        fill(du_ref[...])


def gateup_grads(h, dg, du, n, nf):
    rows, hidden = dg.shape
    r, wide = D // (n * nf), D // n
    if r % 16 or wide % LANES:
        joined = jnp.concatenate([dg, du], axis=1)
        return columns_by_owner(outer_sum(h, joined), n, nf)
    tile = GTILE
    half = hidden // tile
    out = pl.pallas_call(
        gateup_kernel,
        out_shape=jax.ShapeDtypeStruct((nf, n, r, 2 * hidden), bf16),
        grid=(2 * half,),
        in_specs=[
            pl.BlockSpec((rows, D), lambda t: (0, 0), pipeline_mode=pl.Buffered(1)),
            pl.BlockSpec((rows, tile), lambda t: (0, jnp.minimum(t, half - 1))),
            pl.BlockSpec((rows, tile), lambda t: (0, jnp.maximum(t - half, 0))),
        ],
        out_specs=pl.BlockSpec((nf, n, r, tile), lambda t: (0, 0, 0, t)),
        scratch_shapes=[pltpu.VMEM((D, rows), bf16)],
        compiler_params=pltpu.CompilerParams(vmem_limit_bytes=LIMIT),
        cost_estimate=pl.CostEstimate(
            flops=4 * rows * D * hidden, bytes_accessed=4 * D * hidden + 6 * rows * hidden, transcendentals=0
        ),
        name="gateup_grads",
    )(h, dg, du)
    return out.reshape(D, 2 * hidden)


def mid_kernel(cond_ref, dk_ref, dv_ref, h_ref, dq_ref, mix_ref, gy_ref, vec_ref, out_ref):
    wide = dq_ref.shape[1]
    outer = ((0,), (0,))
    place_rows(out_ref, 0, contract(cond_ref[...], dk_ref[...], outer))
    place_rows(out_ref, wide, contract(cond_ref[...], dv_ref[...], outer))
    place_rows(out_ref, 2 * wide, contract(h_ref[...], dq_ref[...], outer))
    out_ref[:, 0, :, 3 * wide : 3 * wide + LANES] = vec_ref[:, 0]
    place_rows(out_ref, 3 * wide + LANES, contract(mix_ref[...], gy_ref[...], outer))


def mid_grads(cond, dk, dv, h, dq, mix, gy, vectors, n, nf):
    rows, wide = dq.shape
    r = D // (n * nf)
    if r % 16 or wide % LANES:
        return jnp.concatenate(
            [
                columns_by_owner(outer_sum(cond, jnp.concatenate([dk, dv], axis=1)), n, nf),
                columns_by_owner(outer_sum(h, dq), n, nf),
                vectors,
                rows_by_owner(outer_sum(mix, gy).astype(bf16), n, nf),
            ],
            axis=1,
        )
    count = cond.shape[0]
    columns = 4 * wide + LANES

    def full(value):
        return pl.BlockSpec(value.shape, lambda s: (0, 0), pipeline_mode=pl.Buffered(1))

    out = pl.pallas_call(
        mid_kernel,
        out_shape=jax.ShapeDtypeStruct((nf, n, r, columns), bf16),
        grid=(n,),
        in_specs=[
            pl.BlockSpec((count, wide), lambda s: (0, s)),
            full(dk),
            full(dv),
            pl.BlockSpec((rows, wide), lambda s: (0, s)),
            full(dq),
            full(mix),
            pl.BlockSpec((rows, wide), lambda s: (0, s)),
            pl.BlockSpec((nf, 1, r, LANES), lambda s: (0, s, 0, 0)),
        ],
        out_specs=pl.BlockSpec((nf, 1, r, columns), lambda s: (0, s, 0, 0)),
        compiler_params=pltpu.CompilerParams(vmem_limit_bytes=LIMIT),
        cost_estimate=pl.CostEstimate(
            flops=2 * D * wide * (2 * count + 2 * rows),
            bytes_accessed=2 * D * (columns + 2 * rows + count),
            transcendentals=0,
        ),
        name="mid_grads",
    )(cond, dk, dv, h, dq, mix, gy, vectors.reshape(nf, n, r, LANES))
    return out.reshape(D, columns)


def self_kernel(h_ref, dq_ref, dk_ref, dv_ref, w_ref, gain_ref, mix_ref, gy_ref, vec_ref, out_ref):
    wide = dq_ref.shape[1]
    nf, _, r, _ = out_ref.shape
    outer = ((0,), (0,))
    along = jnp.zeros((wide, 1), f32)
    for j, ref in enumerate((dq_ref, dk_ref, dv_ref)):
        grad = contract(h_ref[...], ref[...], outer)
        place_rows(out_ref, j * wide, grad)
        weight = w_ref[:, j * wide : (j + 1) * wide].astype(f32)
        along = along + jnp.sum(grad * weight, axis=1, keepdims=True)
    along = jnp.broadcast_to(along / gain_ref[...], (wide, LANES)).reshape(nf, r, LANES)
    lane = lax.broadcasted_iota(jnp.int32, along.shape, 2)
    vec = jnp.where(lane == 0, along, vec_ref[:, 0].astype(f32))
    out_ref[:, 0, :, 3 * wide : 3 * wide + LANES] = vec.astype(bf16)
    place_rows(out_ref, 3 * wide + LANES, contract(mix_ref[...], gy_ref[...], outer))


def self_grads(h, dq, dk, dv, w_self, gain, mix, gy, vectors, n, nf):
    rows, wide = dq.shape
    r = D // (n * nf)
    if r % 16 or wide % LANES:
        grad = outer_sum(h, jnp.concatenate([dq, dk, dv], axis=1))
        along = (jnp.sum(grad * w_self.astype(f32), axis=1) / gain).astype(bf16)
        along = along.reshape(n, nf, r, 1).transpose(1, 0, 2, 3).reshape(D, 1)
        return jnp.concatenate(
            [
                columns_by_owner(grad, n, nf),
                jnp.concatenate([along, vectors[:, 1:]], axis=1),
                rows_by_owner(outer_sum(mix, gy).astype(bf16), n, nf),
            ],
            axis=1,
        )
    columns = 4 * wide + LANES

    def full(value):
        return pl.BlockSpec(value.shape, lambda s: (0, 0), pipeline_mode=pl.Buffered(1))

    out = pl.pallas_call(
        self_kernel,
        out_shape=jax.ShapeDtypeStruct((nf, n, r, columns), bf16),
        grid=(n,),
        in_specs=[
            pl.BlockSpec((rows, wide), lambda s: (0, s)),
            full(dq),
            full(dk),
            full(dv),
            pl.BlockSpec((wide, 3 * wide), lambda s: (s, 0)),
            pl.BlockSpec((wide, 1), lambda s: (s, 0)),
            full(mix),
            pl.BlockSpec((rows, wide), lambda s: (0, s)),
            pl.BlockSpec((nf, 1, r, LANES), lambda s: (0, s, 0, 0)),
        ],
        out_specs=pl.BlockSpec((nf, 1, r, columns), lambda s: (0, s, 0, 0)),
        compiler_params=pltpu.CompilerParams(vmem_limit_bytes=LIMIT),
        cost_estimate=pl.CostEstimate(
            flops=8 * D * wide * rows, bytes_accessed=2 * D * (columns + 2 * rows + 3 * wide), transcendentals=0
        ),
        name="self_grads",
    )(h, dq, dk, dv, w_self, gain[:, None], mix, gy, vectors.reshape(nf, n, r, LANES))
    return out.reshape(D, columns)


def column_parts(shard, parts, n):
    r, columns = shard.shape
    c = columns // (parts * n)
    return shard.reshape(r, parts, n, c).transpose(2, 0, 1, 3).reshape(n, r, parts * c)


def natural_columns(pieces, parts, n):
    r, columns = pieces.shape[1:]
    c = columns // parts
    return pieces.reshape(n, r, parts, c).transpose(1, 2, 0, 3).reshape(r, parts * n * c)


def to_seq(pieces):
    return lax.all_to_all(pieces, "seq", 0, 0, tiled=True)


def gather_columns(pieces, n, nf):
    r, c = pieces.shape[1:]
    gathered = lax.all_gather(pieces.reshape(n * r, c), "fsdp", axis=0, tiled=True)
    return gathered.reshape(nf, n, r, c).transpose(1, 0, 2, 3).reshape(n * nf * r, c)


def columns_by_owner(grad, n, nf):
    rows, c = grad.shape
    r = rows // (n * nf)
    return grad.astype(bf16).reshape(n, nf, r, c).transpose(1, 0, 2, 3).reshape(rows, c)


def rows_by_owner(grad, n, nf):
    rows, columns = grad.shape
    r = rows // nf
    return grad.reshape(nf, r, n, columns // n).transpose(0, 2, 1, 3).reshape(nf * n * r, columns // n)


def share(rows_of_fsdp, n):
    rows, c = rows_of_fsdp.shape
    return to_seq(rows_of_fsdp.reshape(n, rows // n, c))


def rows_to_pieces(shard, n):
    r, columns = shard.shape
    return shard.reshape(r, n, columns // n).transpose(1, 0, 2).reshape(n * r, columns // n)


def after(value, *others):
    return lax.optimization_barrier((value,) + others)[0]


def sum_over_seq(value, n):
    if n != 4:
        return lax.psum(value, "seq")
    half = value.shape[1] // 2

    def step(part, j):
        low = part.astype(bf16)
        return low.astype(f32) + hop(low, j).astype(f32)

    return jnp.concatenate(
        [step(step(value[:, :half], 1), 2), step(step(value[:, half:], 2), 1)], axis=1
    )


def pad_heads(value, parts):
    rows, columns = value.shape
    c = columns // parts
    if c % LANES == 0:
        return value
    padded = -(-c // LANES) * LANES
    return jnp.pad(value.reshape(rows, parts, c), ((0, 0), (0, 0), (0, padded - c))).reshape(
        rows, parts * padded
    )


def shards(
    tokens,
    conditioning,
    lengths,
    grad_output,
    norm_first,
    proj_self,
    out_self,
    norm_second,
    proj_query,
    proj_keyval,
    out_cross,
    norm_third,
    proj_gateup,
    bias_gateup,
    proj_down,
    bias_down,
):
    rows = tokens.shape[1]
    n = lax.axis_size("seq")
    nf = lax.axis_size("fsdp")
    me = lax.axis_index("seq")
    group = rows * n
    wide = D // n
    pairs = -(-wide // LANES)
    hidden = FF // n
    r = norm_first.shape[0]

    small = jnp.concatenate(
        [v.reshape(r, -1) for v in (norm_first, norm_second, norm_third, bias_down, bias_gateup)],
        axis=1,
    )
    small = jnp.pad(small, ((0, 0), (0, LANES - small.shape[1])))
    self_in = jnp.concatenate(
        [column_parts(proj_self, 3, n), jnp.broadcast_to(small[None], (n, r, LANES))], axis=2
    )
    self_pieces = to_seq(self_in)
    mid_pieces = to_seq(
        after(
            jnp.concatenate([column_parts(proj_keyval, 2, n), column_parts(proj_query, 1, n)], axis=2),
            self_pieces,
        )
    )
    group_tokens = gather_rows(after(tokens[0], self_pieces), n)
    gateup_pieces = to_seq(after(column_parts(proj_gateup, 2, n), mid_pieces))

    self_all = gather_columns(self_pieces, n, nf)
    w_self = self_all[:, : 3 * wide]
    vectors = self_all[:, 3 * wide : 3 * wide + 12]
    gain_one, gain_two, gain_three, b_down = (vectors[:, j].astype(f32) for j in range(4))
    b_gateup = vectors[:, 4:12].reshape(2 * FF).astype(f32)
    b_gate = lax.dynamic_slice_in_dim(b_gateup, me * hidden, hidden, 0)
    b_upper = lax.dynamic_slice_in_dim(b_gateup, FF + me * hidden, hidden, 0)
    mid = jnp.concatenate(
        [
            mid_pieces.reshape(n * r, 3 * wide),
            rows_to_pieces(out_self, n),
            rows_to_pieces(out_cross, n),
        ],
        axis=1,
    )
    mid = lax.all_gather(mid, "fsdp", axis=0, tiled=True).reshape(nf, n, r, 5 * wide)
    kvq = mid[..., : 3 * wide].transpose(1, 0, 2, 3).reshape(D, 3 * wide)
    w_keyval, w_query = kvq[:, : 2 * wide], kvq[:, 2 * wide :]
    w_out = mid[..., 3 * wide : 4 * wide].transpose(0, 2, 1, 3).reshape(nf * r, D)
    w_cross = mid[..., 4 * wide :].transpose(0, 2, 1, 3).reshape(nf * r, D)
    w_gateup = lax.all_gather(gateup_pieces.reshape(n * r, 2 * hidden), "fsdp", axis=0, tiled=True)
    w_gateup = w_gateup.reshape(nf, n, r, 2 * hidden)
    if r % 16:
        w_gateup = w_gateup.transpose(1, 0, 2, 3).reshape(1, 1, D, 2 * hidden)
    w_down = lax.all_gather(after(proj_down, gateup_pieces), "fsdp", axis=0, tiled=True)

    group_lengths = lengths[0]
    order = block_ids(n)
    all_rows = (order[:, None] * rows + jnp.arange(rows, dtype=jnp.int32)[None, :]).reshape(group)
    ids, positions = seq_info(all_rows, group_lengths)
    tables = angle_tables(positions)

    def block(value, j):
        return lax.slice_in_dim(value, j * rows, (j + 1) * rows, axis=0)

    inputs = tokens[0].astype(f32)
    normal_one, scaled_one, _ = norm_rows(inputs, gain_one)
    normed_one = norm_rows(group_tokens.astype(f32), gain_one)[2].astype(bf16)
    packed = pad_heads(dot(normed_one, w_self), 3)
    group_grad = gather_rows(after(grad_output[0], packed), n)
    q, k, v, mixed, lse = attend(packed, packed, packed, (0, pairs, 2 * pairs), pairs, ids, ids, tables)
    mixed_in = mixed[:, :wide]
    first = inputs + scatter_rows(lambda j: dot(block(mixed_in, j), w_out), n)

    normal_two, scaled_two, normed = norm_rows(first, gain_two)
    normed_two = gather_rows(normed.astype(bf16), n)
    cq = pad_heads(dot(normed_two, w_query).astype(bf16), 1)
    cond_rows = conditioning[0].reshape(SEQS_GRP * COND, D)
    count = SEQS_GRP * COND
    count_pad = -(-count // 16) * 16
    keyval = pad_heads(dot(cond_rows, w_keyval).astype(bf16), 2)
    keyval = jnp.pad(keyval, ((0, count_pad - count), (0, 0)))
    index = jnp.arange(count_pad, dtype=jnp.int32)
    cond_ids = jnp.where(index < count, index // COND, -1)
    cmix, clse = attend(cq, keyval, keyval, (0, 0, pairs), pairs, ids, cond_ids)
    cmix_in = cmix[:, :wide]
    second = first + scatter_rows(lambda j: dot(block(cmix_in, j), w_cross), n)

    normal_three, scaled_three, normed = norm_rows(second, gain_three)
    normed_three = gather_rows(normed.astype(bf16), n)
    active, grad_gate, grad_upper, sum_gate, sum_upper, back_three = feed(
        normed_three, group_grad, w_gateup, w_down, b_gate, b_upper
    )
    grad_rows = grad_output[0].astype(f32)
    grad_b_down = jnp.sum(grad_rows, axis=0)
    through = scatter_rows(lambda j: block(back_three, j).astype(f32), n)
    grad_w_down = outer_sum(active, group_grad).astype(bf16)
    own_down = lax.psum_scatter(grad_w_down, "fsdp", scatter_dimension=0, tiled=True)
    grad_w_gateup = gateup_grads(normed_three, grad_gate, grad_upper, n, nf)
    through, grad_w_gateup = lax.optimization_barrier((through, grad_w_gateup))
    own_gateup = lax.psum_scatter(after(grad_w_gateup, own_down), "fsdp", scatter_dimension=0, tiled=True)
    through, grad_gain_three = norm_back(through, normal_three, scaled_three, gain_three)
    grad_second = grad_rows + through

    group_second = gather_rows(grad_second.astype(bf16), n)
    grad_cmix = pad_heads(back_prod(group_second, w_cross).astype(bf16), 1)
    dcq, dck, dcv = attend_back(
        cq, keyval, keyval, (0, 0, pairs), pairs, grad_cmix, cmix, clse, ids, cond_ids
    )
    dcq, dck, dcv = dcq[:, :wide], dck[:, :wide], dcv[:, :wide]
    cond_full = jnp.pad(cond_rows, ((0, count_pad - count), (0, 0)))
    through = scatter_rows(lambda j: back_prod(block(dcq, j), w_query), n)
    b_whole = lax.dynamic_update_slice(
        jnp.zeros((2, FF), f32), jnp.concatenate([sum_gate, sum_upper], axis=0), (0, me * hidden)
    )
    vectors = jnp.concatenate(
        [v.reshape(n, nf, r, -1) for v in (grad_gain_three, grad_b_down, b_whole)], axis=3
    )
    vectors = vectors.astype(bf16).transpose(1, 0, 2, 3).reshape(nf * n * r, -1)
    vectors = jnp.pad(vectors, ((0, 0), (0, LANES - vectors.shape[1])))
    grad_w_mid = mid_grads(cond_full, dck, dcv, normed_two, dcq, cmix_in, group_second, vectors, n, nf)
    through, grad_w_mid = lax.optimization_barrier((through, grad_w_mid))
    own_mid = lax.psum_scatter(after(grad_w_mid, own_gateup), "fsdp", scatter_dimension=0, tiled=True)
    through, grad_gain_two = norm_back(through, normal_two, scaled_two, gain_two)
    grad_first = grad_second + through

    group_first = gather_rows(grad_first.astype(bf16), n)
    own_gateup = share(after(own_gateup, group_first), n)
    late_active = after(active, group_first)
    result = second + scatter_rows(lambda j: dot(block(late_active, j), w_down), n) + b_down
    grad_mixed = pad_heads(back_prod(group_first, w_out).astype(bf16), 1)
    dq, dk, dv = attend_back(q, k, v, (0, 0, 0), pairs, grad_mixed, mixed, lse, ids, ids, tables)
    own_gateup = after(own_gateup, dq)
    dq, dk, dv = dq[:, :wide], dk[:, :wide], dv[:, :wide]
    grad_packed = jnp.concatenate([dq, dk, dv], axis=1)
    gains = grad_gain_two.astype(bf16).reshape(n, nf, r, 1).transpose(1, 0, 2, 3).reshape(D, 1)
    gains = jnp.pad(gains, ((0, 0), (1, LANES - 2)))
    grad_w_self = self_grads(
        normed_one, dq, dk, dv, w_self, gain_one, mixed_in, group_first, gains, n, nf
    )
    grad_packed, grad_w_self, own_gateup, result = lax.optimization_barrier(
        (grad_packed, grad_w_self, own_gateup, result)
    )
    own_self = lax.psum_scatter(after(grad_w_self, own_mid), "fsdp", scatter_dimension=0, tiled=True)
    through = scatter_rows(lambda j: back_prod(block(grad_packed, j), w_self), n)
    grad_keyval = jnp.concatenate([dck, dcv], axis=1)[:count]
    grad_cond = sum_over_seq(after(back_prod(grad_keyval, w_keyval), through), n)
    grad_cond = grad_cond.reshape(1, SEQS_GRP, COND, D)
    grad_inputs = grad_first + norm_back(through, normal_one, scaled_one, gain_one)[0]

    def joined(pieces):
        return pieces.reshape(n, r, wide).transpose(1, 0, 2).reshape(r, D)

    split = 3 * wide + LANES
    mid_part = share(own_mid[:, :split], n)
    vectors = jnp.sum(mid_part[:, :, 3 * wide :].astype(f32), axis=0)
    own_cross = joined(own_mid[:, split:])
    own_out = joined(own_self[:, split:])
    self_part = share(own_self[:, :split], n)
    gains = jnp.sum(self_part[:, :, 3 * wide :].astype(f32), axis=0)

    return (
        result.astype(bf16)[None],
        grad_inputs[None],
        grad_cond,
        gains[:, 0],
        natural_columns(self_part[:, :, : 3 * wide], 3, n).astype(f32),
        own_out.astype(f32),
        gains[:, 1],
        natural_columns(mid_part[:, :, 2 * wide : 3 * wide], 1, n).astype(f32),
        natural_columns(mid_part[:, :, : 2 * wide], 2, n).astype(f32),
        own_cross.astype(f32),
        vectors[:, 0],
        natural_columns(own_gateup, 2, n).astype(f32),
        vectors[:, 2:10].reshape(8 * r),
        own_down.astype(f32),
        vectors[:, 1],
    )


def solution(mesh):
    rows_of = P("fsdp", "seq", None)
    matrix = P(ALL, None)
    vector = P(ALL)
    return jax.shard_map(
        shards,
        mesh=mesh,
        in_specs=(
            rows_of,
            P("fsdp", None, None, None),
            P("fsdp", None),
            rows_of,
            vector,
            matrix,
            matrix,
            vector,
            matrix,
            matrix,
            matrix,
            vector,
            matrix,
            vector,
            matrix,
            vector,
        ),
        out_specs=(
            rows_of,
            rows_of,
            P("fsdp", None, None, None),
            vector,
            matrix,
            matrix,
            vector,
            matrix,
            matrix,
            matrix,
            vector,
            matrix,
            vector,
            matrix,
            vector,
        ),
        check_vma=False,
    )
```

```python
import functools

import jax
import jax.numpy as jnp
from jax import lax
from jax.experimental import pallas as pl
from jax.experimental.pallas import tpu as pltpu
from jax.sharding import PartitionSpec as P

D = 1536
HEADS = 24
HEAD = 64
FF = 6144
COND = 130
SEQS_GRP = 2
LANES = 128

epsilon = 1e-05
masked_score = -1e30
bf16 = jnp.bfloat16
f32 = jnp.float32
ALL = ("seq", "fsdp")


def seq_info(global_rows, group_lengths):
    ends = jnp.cumsum(group_lengths)
    starts = ends - group_lengths
    ident = jnp.sum((global_rows[:, None] >= ends[None, :]).astype(jnp.int32), axis=1)
    onehot = ident[:, None] == jnp.arange(group_lengths.shape[0], dtype=jnp.int32)[None, :]
    begin = jnp.sum(jnp.where(onehot, starts[None, :], 0), axis=1)
    return (ident, (global_rows - begin).astype(f32))


def angle_tables(positions):
    half = HEAD // 2
    inverse = jnp.power(10000.0, -jnp.arange(half, dtype=f32) / half)
    turned = positions[:, None] * inverse[None, :]
    cosine, sine = jnp.cos(turned), jnp.sin(turned)
    reps = LANES // HEAD
    return (
        jnp.concatenate([cosine, cosine] * reps, axis=1),
        jnp.concatenate([-sine, sine] * reps, axis=1),
    )


def norm_rows(values, gain):
    centre = values - jnp.mean(values, axis=-1, keepdims=True)
    spread = jnp.mean(centre * centre, axis=-1, keepdims=True)
    scaled = lax.rsqrt(spread + epsilon)
    normal = centre * scaled
    return (normal, scaled, normal * gain)


def norm_back(grad_rows, normal, scaled, gain):
    weighted = grad_rows * gain
    mean_one = jnp.mean(weighted, axis=-1, keepdims=True)
    mean_two = jnp.mean(weighted * normal, axis=-1, keepdims=True)
    return (scaled * (weighted - mean_one - normal * mean_two), jnp.sum(grad_rows * normal, axis=0))


def dot(left, right):
    return jnp.dot(left, right, preferred_element_type=f32)


def outer_sum(left, right):
    return lax.dot_general(left, right, (((0,), (0,)), ((), ())), preferred_element_type=f32)


def back_prod(left, weight):
    return lax.dot_general(left, weight, (((1,), (1,)), ((), ())), preferred_element_type=f32)


def after(value, *others):
    if not others:
        return value
    return lax.optimization_barrier((value,) + others)[0]


def hop(value, j):
    return lax.ppermute(value, "seq", [(i, i ^ j) for i in range(4)])


def block_ids(n):
    if n == 4:
        return lax.axis_index("seq") ^ jnp.arange(n, dtype=jnp.int32)
    return jnp.arange(n, dtype=jnp.int32)


def gather_rows(value, n):
    if n != 4:
        whole = lax.all_gather(value, "seq", axis=0, tiled=True)
        return whole, (whole,), (whole,)
    half = value.shape[0] // 2
    first, second = hop(value, 1), hop(value, 2)
    third, fourth = hop(second[:half], 1), hop(first[half:], 2)
    whole = jnp.concatenate([value, first, second, third, fourth], axis=0)
    return whole, (first, second), (third, fourth)


def scatter_rows(blocks, rows, n):
    if n != 4:
        whole = jnp.concatenate([blocks(j, 0, rows) for j in range(n)], axis=0).astype(bf16)
        out = lax.psum_scatter(whole, "seq", scatter_dimension=0, tiled=True).astype(f32)
        return out, (out,)
    half = rows // 2
    to_first = hop(blocks(3, 0, half).astype(bf16), 1)
    to_second = hop(blocks(3, half, rows).astype(bf16), 2)
    one, two = blocks(1, 0, rows).astype(f32), blocks(2, 0, rows).astype(f32)
    one = jnp.concatenate([one[:half], one[half:] + to_second.astype(f32)], axis=0)
    two = jnp.concatenate([two[:half] + to_first.astype(f32), two[half:]], axis=0)
    one, two = hop(one.astype(bf16), 1), hop(two.astype(bf16), 2)
    own = blocks(0, 0, rows).astype(f32)
    return own + one.astype(f32) + two.astype(f32), (to_first, to_second)


def scatter_start(partial, n):
    if n != 4:
        return (lax.psum_scatter(partial, "seq", scatter_dimension=0, tiled=True),)
    half = partial.shape[0] // 8
    return (
        hop(partial[6 * half : 7 * half], 1),
        hop(partial[7 * half :], 2),
        hop(partial[2 * half : 3 * half], 1),
        hop(partial[5 * half : 6 * half], 2),
    )


def scatter_end(partial, pieces, n):
    if n != 4:
        return pieces[0].astype(f32)
    half = partial.shape[0] // 8
    to_first, to_second, one, two = (piece.astype(f32) for piece in pieces)
    sum_one = hop((partial[3 * half : 4 * half].astype(f32) + to_second).astype(bf16), 1)
    sum_two = hop((partial[4 * half : 5 * half].astype(f32) + to_first).astype(bf16), 2)
    others = jnp.concatenate([one + sum_two.astype(f32), sum_one.astype(f32) + two], axis=0)
    return partial[: 2 * half].astype(f32) + others


def swap_halves(value):
    lane = lax.broadcasted_iota(jnp.int32, value.shape, 1)
    half = HEAD // 2
    return jnp.where(
        lane % HEAD < half, pltpu.roll(value, LANES - half, 1), pltpu.roll(value, half, 1)
    )


def head_rows(h):
    return slice(h * HEAD, (h + 1) * HEAD)


def lane_mask(value, h):
    lane = lax.broadcasted_iota(jnp.int32, value.shape, 1)
    return jnp.where(lane // HEAD == h, value, jnp.zeros_like(value))


FAR = 1e30


def pieces_of(value):
    high = value.astype(bf16).astype(f32)
    rest = value - high
    middle = rest.astype(bf16).astype(f32)
    return high, middle, rest - middle


def key_lanes(keys, kid, h):
    lane = lax.broadcasted_iota(jnp.int32, keys.shape, 1)
    spare = lane % HEAD
    ones = jnp.where(spare <= SEQS_GRP + 3, 1.0, 0.0)
    padding = jnp.where(spare == SEQS_GRP, jnp.where(kid < 0, 1.0, 0.0), ones)
    extra = jnp.where(spare < SEQS_GRP, jnp.where(kid == spare, 1.0, 0.0), padding)
    return jnp.where(lane // HEAD == h, keys.astype(f32), extra).astype(bf16)


def query_rows(turned, qid, h, offsets=()):
    row = lax.broadcasted_iota(jnp.int32, turned.shape, 0)
    spare = row % HEAD
    extra = jnp.where(spare <= SEQS_GRP, jnp.where(qid == spare, 0.0, -FAR), 0.0)
    for j, offset in enumerate(offsets):
        extra = jnp.where(spare == SEQS_GRP + 1 + j, offset, extra)
    return jnp.where(row // HEAD == h, turned, extra).astype(bf16)


def value_lanes(values, h):
    lane = lax.broadcasted_iota(jnp.int32, values.shape, 1)
    ones = jnp.where(lane % HEAD < 3, 1.0, 0.0)
    return jnp.where(lane // HEAD == h, values.astype(f32), ones).astype(bf16)


def grad_rows_of(turned, h, offsets):
    row = lax.broadcasted_iota(jnp.int32, turned.shape, 0)
    extra = jnp.zeros_like(turned)
    for j, offset in enumerate(offsets):
        extra = jnp.where(row % HEAD == j, offset, extra)
    return jnp.where(row // HEAD == h, turned, extra).astype(bf16)


PAIR = LANES // HEAD


def attend_kernel(rope, tile, *refs):
    if rope:
        q_ref, k_ref, v_ref, cos_ref, sin_ref, qid_ref, kid_ref = refs[:7]
        qo_ref, ko_ref, vo_ref, o_ref, lse_ref, qt, kb, vt, ot = refs[7:]
        q, k = q_ref[...], k_ref[...]
        q = (q * cos_ref[...] + swap_halves(q) * sin_ref[...]).astype(bf16)
        k = (k * cos_ref[...] + swap_halves(k) * sin_ref[...]).astype(bf16)
        v = v_ref[...].astype(bf16)
        qo_ref[...] = q
        ko_ref[...] = k
        vo_ref[...] = v
    else:
        q_ref, k_ref, v_ref, qid_ref, kid_ref, o_ref, lse_ref, qt, kb, vt, ot = refs
        q, k, v = q_ref[...], k_ref[...], v_ref[...]
    turned = q.astype(f32).T * 0.125
    for h in range(PAIR):
        qt[h] = query_rows(turned, qid_ref[...], h)
        kb[h] = key_lanes(k, kid_ref[...], h)
    vt[...] = v.astype(f32).T.astype(bf16)
    units = [(t * tile, h) for t in range(ot.shape[1] // tile) for h in range(PAIR)]

    def scores(unit):
        start, h = unit
        return dot(kb[h], qt[h, :, start : start + tile])

    later = scores(units[0])
    for i, (start, h) in enumerate(units):
        s = later
        if i + 1 < len(units):
            later = scores(units[i + 1])
        at = slice(start, start + tile)
        top = jnp.max(s, axis=0, keepdims=True)
        e = jnp.exp(s - top)
        total = jnp.sum(e, axis=0, keepdims=True)
        ot[head_rows(h), at] = dot(vt[head_rows(h), :], e.astype(bf16)) * (1.0 / total)
        lse_ref[0, h : h + 1, at] = top + jnp.log(total)
    o_ref[...] = ot[...].T.astype(bf16)


def attend_back_kernel(rope, tile, *refs):
    if rope:
        q_ref, k_ref, v_ref, do_ref, o_ref, lse_ref, cos_ref, sin_ref, qid_ref, kid_ref = refs[:10]
        dq_ref, dk_ref, dv_ref, qt, gt, kb, vb, kt, dqt, dk_acc, dv_acc = refs[10:]
    else:
        q_ref, k_ref, v_ref, do_ref, o_ref, lse_ref, qid_ref, kid_ref = refs[:8]
        dq_ref, dk_ref, dv_ref, qt, gt, kb, vb, kt, dqt, dk_acc, dv_acc = refs[8:]
    turned = q_ref[...].astype(f32).T * 0.125
    grads = do_ref[...].astype(f32).T
    product = grads * o_ref[...].astype(f32).T
    kt[...] = k_ref[...].astype(f32).T.astype(bf16)
    for h in range(PAIR):
        delta = jnp.sum(product[head_rows(h), :], axis=0, keepdims=True)
        qt[h] = query_rows(turned, qid_ref[...], h, pieces_of(-lse_ref[0, h : h + 1, :]))
        gt[h] = grad_rows_of(grads, h, pieces_of(-delta))
        kb[h] = key_lanes(k_ref[...], kid_ref[...], h)
        vb[h] = value_lanes(v_ref[...], h)
    tiles = dqt.shape[1] // tile
    units = [(t * tile, h) for t in range(tiles) for h in range(PAIR)]

    def products(unit):
        start, h = unit
        at = slice(start, start + tile)
        return dot(kb[h], qt[h, :, at]), dot(vb[h], gt[h, :, at])

    later = products(units[0])
    low_p, low_ds = [], []
    for i, (start, h) in enumerate(units):
        s, dp = later
        if i + 1 < len(units):
            later = products(units[i + 1])
        at = slice(start, start + tile)
        p = jnp.exp(s)
        ds = (p * dp).astype(bf16)
        dqt[head_rows(h), at] = dot(kt[head_rows(h), :], ds)
        low_p.append(p.astype(bf16))
        low_ds.append(ds)
        if h == PAIR - 1:
            rows_do = jnp.concatenate([lane_mask(do_ref[at, :], j) for j in range(PAIR)], axis=0)
            rows_q = jnp.concatenate([lane_mask(q_ref[at, :], j) for j in range(PAIR)], axis=0)
            dv = dot(jnp.concatenate(low_p, axis=1), rows_do)
            dk = dot(jnp.concatenate(low_ds, axis=1), rows_q)
            dv_acc[...] = dv if start == 0 else dv_acc[...] + dv
            dk_acc[...] = dk if start == 0 else dk_acc[...] + dk
            low_p, low_ds = [], []
    dq = dqt[...].T * 0.125
    dk = dk_acc[...] * 0.125
    if rope:
        dq = dq * cos_ref[...] - swap_halves(dq) * sin_ref[...]
        dk = dk * cos_ref[...] - swap_halves(dk) * sin_ref[...]
    dq_ref[...] = dq.astype(bf16)
    dk_ref[...] = dk.astype(bf16)
    dv_ref[...] = dv_acc[...].astype(bf16)


def query_tile(rows):
    for tile in (256, 128):
        if rows % tile == 0:
            return tile
    return rows


def spec(rows, offset=0):
    return pl.BlockSpec((rows, LANES), lambda i: (0, i + offset))


def whole(shape):
    return pl.BlockSpec(shape, lambda i: (0,) * len(shape), pipeline_mode=pl.Buffered(1))


LIMIT = 56 * 1024 * 1024
TILE, CHUNK, GTILE = 256, 320, 512


def attend(q, k, v, offsets, pairs, qid, kid, tables=None):
    nq, nk = q.shape[0], k.shape[0]
    rope = tables is not None
    tile = query_tile(nq)
    ins = [spec(nq, offsets[0]), spec(nk, offsets[1]), spec(nk, offsets[2])]
    args = [q, k, v]
    outs, shapes = [], []
    if rope:
        ins += [whole((nq, LANES)), whole((nq, LANES))]
        args += list(tables)
        outs += [spec(nq), spec(nk), spec(nk)]
        shapes += [jax.ShapeDtypeStruct((rows, pairs * LANES), bf16) for rows in (nq, nk, nk)]
    ins += [whole((1, nq)), whole((nk, 1))]
    args += [qid[None, :], kid[:, None]]
    outs += [spec(nq), pl.BlockSpec((1, 8, nq), lambda i: (i, 0, 0))]
    shapes += [
        jax.ShapeDtypeStruct((nq, pairs * LANES), bf16),
        jax.ShapeDtypeStruct((pairs, 8, nq), f32),
    ]
    return pl.pallas_call(
        functools.partial(attend_kernel, rope, tile),
        out_shape=shapes,
        grid=(pairs,),
        in_specs=ins,
        out_specs=outs,
        scratch_shapes=[
            pltpu.VMEM((PAIR, LANES, nq), bf16),
            pltpu.VMEM((PAIR, nk, LANES), bf16),
            pltpu.VMEM((LANES, nk), bf16),
            pltpu.VMEM((LANES, nq), f32),
        ],
        compiler_params=pltpu.CompilerParams(vmem_limit_bytes=LIMIT),
        cost_estimate=pl.CostEstimate(
            flops=2 * 2 * 2 * pairs * nq * nk * LANES,
            bytes_accessed=pairs * LANES * (nq + nk) * 12,
            transcendentals=2 * pairs * nq * nk,
        ),
        name="attend_self" if rope else "attend_cross",
    )(*args)


def attend_back(q, k, v, offsets, pairs, grad, mixed, lse, qid, kid, tables=None):
    nq, nk = q.shape[0], k.shape[0]
    rope = tables is not None
    tile = query_tile(nq)
    ins = [spec(nq, offsets[0]), spec(nk, offsets[1]), spec(nk, offsets[2]), spec(nq), spec(nq)]
    args = [q, k, v, grad, mixed]
    ins += [pl.BlockSpec((1, 8, nq), lambda i: (i, 0, 0))]
    args += [lse]
    if rope:
        ins += [whole((nq, LANES)), whole((nq, LANES))]
        args += list(tables)
    ins += [whole((1, nq)), whole((nk, 1))]
    args += [qid[None, :], kid[:, None]]
    return pl.pallas_call(
        functools.partial(attend_back_kernel, rope, tile),
        out_shape=[jax.ShapeDtypeStruct((rows, pairs * LANES), bf16) for rows in (nq, nk, nk)],
        grid=(pairs,),
        in_specs=ins,
        out_specs=[spec(nq), spec(nk), spec(nk)],
        scratch_shapes=[
            pltpu.VMEM((PAIR, LANES, nq), bf16),
            pltpu.VMEM((PAIR, LANES, nq), bf16),
            pltpu.VMEM((PAIR, nk, LANES), bf16),
            pltpu.VMEM((PAIR, nk, LANES), bf16),
            pltpu.VMEM((LANES, nk), bf16),
            pltpu.VMEM((LANES, nq), f32),
            pltpu.VMEM((nk, LANES), f32),
            pltpu.VMEM((nk, LANES), f32),
        ],
        compiler_params=pltpu.CompilerParams(vmem_limit_bytes=LIMIT),
        cost_estimate=pl.CostEstimate(
            flops=2 * 5 * 2 * pairs * nq * nk * LANES,
            bytes_accessed=pairs * LANES * (nq + nk) * 12,
            transcendentals=2 * pairs * nq * nk,
        ),
        name="back_self" if rope else "back_cross",
    )(*args)


def contract(left, right, dims):
    return lax.dot_general(left, right, (dims, ((), ())), preferred_element_type=f32)


def feed_kernel(chunk, *refs):
    h_ref, gy_ref, wg_ref, wu_ref, wd_ref, bg_ref, bu_ref = refs[:7]
    act_ref, dg_ref, du_ref, sg_ref, su_ref, dh_ref, dw_ref, both, total = refs[7:]
    step = pl.program_id(0)
    span = wg_ref.shape[0] * wg_ref.shape[2]
    tile = wg_ref.shape[3]
    for j in range(wg_ref.shape[1]):
        at = slice(j * span, (j + 1) * span)
        both[at, :tile] = wg_ref[:, j].reshape(span, tile)
        both[at, tile:] = wu_ref[:, j].reshape(span, tile)
    sg_ref[...] = jnp.zeros_like(sg_ref)
    su_ref[...] = jnp.zeros_like(su_ref)

    @pl.when(step == 0)
    def _():
        total[...] = jnp.zeros_like(total)

    def rows_at(i):
        return slice(i * chunk, (i + 1) * chunk)

    def products(i):
        at = rows_at(i)
        return dot(h_ref[at, :], both[...]), contract(gy_ref[at, :], wd_ref[...], ((1,), (1,)))

    def finish(i, pair, grad):
        at = rows_at(i)
        gate = pair[:, :tile] + bg_ref[...]
        upper = pair[:, tile:] + bu_ref[...]
        sigma = jax.nn.sigmoid(gate)
        silu = gate * sigma
        act_ref[at, :] = (silu * upper).astype(bf16)
        dg = (grad * upper * sigma * (1.0 + gate * (1.0 - sigma))).astype(bf16)
        du = (grad * silu).astype(bf16)
        dg_ref[at, :] = dg
        du_ref[at, :] = du
        sg_ref[...] += jnp.sum(dg.astype(f32), axis=0, keepdims=True)
        su_ref[...] += jnp.sum(du.astype(f32), axis=0, keepdims=True)
        return jnp.concatenate([dg, du], axis=1)

    chunks = h_ref.shape[0] // chunk
    now = products(0)
    for i in range(chunks):
        later = products(i + 1) if i + 1 < chunks else None
        grads = finish(i, *now)
        total[rows_at(i), :] += contract(grads, both[...], ((1,), (1,)))
        now = later
    dw_ref[...] = dot(act_ref[...].T, gy_ref[...]).astype(bf16)

    @pl.when(step == pl.num_programs(0) - 1)
    def _():
        dh_ref[...] = total[...].astype(bf16)


def feed(h, gy, w_gateup, w_down, b_gate, b_upper):
    rows = h.shape[0]
    hidden = w_down.shape[0]
    tile = TILE if rows <= 1280 else 128
    steps = hidden // tile
    lead = w_gateup.shape[:3]
    chunk = CHUNK if rows % CHUNK == 0 else rows
    one = pl.Buffered(1)
    rows_all = pl.BlockSpec((rows, D), lambda t: (0, 0), pipeline_mode=one)
    columns = pl.BlockSpec((rows, tile), lambda t: (0, t))
    vector = pl.BlockSpec((1, tile), lambda t: (0, t))
    return pl.pallas_call(
        functools.partial(feed_kernel, chunk),
        out_shape=[jax.ShapeDtypeStruct((rows, hidden), bf16)] * 3
        + [jax.ShapeDtypeStruct((1, hidden), f32)] * 2
        + [jax.ShapeDtypeStruct((rows, D), bf16), jax.ShapeDtypeStruct((hidden, D), bf16)],
        grid=(steps,),
        in_specs=[
            rows_all,
            rows_all,
            pl.BlockSpec(lead + (tile,), lambda t: (0, 0, 0, t)),
            pl.BlockSpec(lead + (tile,), lambda t: (0, 0, 0, t + steps)),
            pl.BlockSpec((tile, D), lambda t: (t, 0)),
            vector,
            vector,
        ],
        out_specs=[columns, columns, columns, vector, vector, rows_all, pl.BlockSpec((tile, D), lambda t: (t, 0))],
        scratch_shapes=[
            pltpu.VMEM((D, 2 * tile), bf16),
            pltpu.VMEM((rows, D), f32),
        ],
        compiler_params=pltpu.CompilerParams(vmem_limit_bytes=LIMIT),
        cost_estimate=pl.CostEstimate(
            flops=2 * 6 * rows * D * hidden,
            bytes_accessed=2 * (3 * rows * D + 3 * rows * hidden + 4 * D * hidden),
            transcendentals=rows * hidden,
        ),
        name="feed",
    )(h, gy, w_gateup, w_gateup, w_down, b_gate[None], b_upper[None])


def place_rows(out_ref, start, value):
    nf, _, r, _ = out_ref.shape
    width = value.shape[1]
    out_ref[:, 0, :, start : start + width] = value.astype(bf16).reshape(nf, r, width)


def gateup_kernel(h_ref, dg_ref, du_ref, out_ref, turned):
    step = pl.program_id(0)
    half = pl.num_programs(0) // 2
    nf, n, r, tile = out_ref.shape
    wide = nf * r

    @pl.when(step == 0)
    def _():
        for s in range(n):
            at = slice(s * wide, (s + 1) * wide)
            turned[at, :] = h_ref[:, at].T

    def fill(grad):
        for s in range(n):
            value = dot(turned[s * wide : (s + 1) * wide, :], grad)
            out_ref[:, s] = value.astype(bf16).reshape(nf, r, tile)

    @pl.when(step < half)
    def _():
        fill(dg_ref[...])

    @pl.when(step >= half)
    def _():
        fill(du_ref[...])


def gateup_grads(h, dg, du, n, nf):
    rows, hidden = dg.shape
    r, wide = D // (n * nf), D // n
    if r % 16 or wide % LANES:
        joined = jnp.concatenate([dg, du], axis=1)
        return columns_by_owner(outer_sum(h, joined), n, nf)
    tile = GTILE
    half = hidden // tile
    out = pl.pallas_call(
        gateup_kernel,
        out_shape=jax.ShapeDtypeStruct((nf, n, r, 2 * hidden), bf16),
        grid=(2 * half,),
        in_specs=[
            pl.BlockSpec((rows, D), lambda t: (0, 0), pipeline_mode=pl.Buffered(1)),
            pl.BlockSpec((rows, tile), lambda t: (0, jnp.minimum(t, half - 1))),
            pl.BlockSpec((rows, tile), lambda t: (0, jnp.maximum(t - half, 0))),
        ],
        out_specs=pl.BlockSpec((nf, n, r, tile), lambda t: (0, 0, 0, t)),
        scratch_shapes=[pltpu.VMEM((D, rows), bf16)],
        compiler_params=pltpu.CompilerParams(vmem_limit_bytes=LIMIT),
        cost_estimate=pl.CostEstimate(
            flops=4 * rows * D * hidden, bytes_accessed=4 * D * hidden + 6 * rows * hidden, transcendentals=0
        ),
        name="gateup_grads",
    )(h, dg, du)
    return out.reshape(D, 2 * hidden)


def mid_kernel(cond_ref, dk_ref, dv_ref, h_ref, dq_ref, mix_ref, gy_ref, vec_ref, out_ref):
    wide = dq_ref.shape[1]
    outer = ((0,), (0,))
    turned = cond_ref[...].T
    place_rows(out_ref, 0, dot(turned, dk_ref[...]))
    place_rows(out_ref, wide, dot(turned, dv_ref[...]))
    place_rows(out_ref, 2 * wide, contract(h_ref[...], dq_ref[...], outer))
    out_ref[:, 0, :, 3 * wide : 3 * wide + LANES] = vec_ref[:, 0]
    place_rows(out_ref, 3 * wide + LANES, contract(mix_ref[...], gy_ref[...], outer))


def mid_grads(cond, dk, dv, h, dq, mix, gy, vectors, n, nf):
    rows, wide = dq.shape
    r = D // (n * nf)
    if r % 16 or wide % LANES:
        return jnp.concatenate(
            [
                columns_by_owner(outer_sum(cond, jnp.concatenate([dk, dv], axis=1)), n, nf),
                columns_by_owner(outer_sum(h, dq), n, nf),
                vectors,
                rows_by_owner(outer_sum(mix, gy).astype(bf16), n, nf),
            ],
            axis=1,
        )
    count = cond.shape[0]
    columns = 4 * wide + LANES

    def full(value):
        return pl.BlockSpec(value.shape, lambda s: (0, 0), pipeline_mode=pl.Buffered(1))

    out = pl.pallas_call(
        mid_kernel,
        out_shape=jax.ShapeDtypeStruct((nf, n, r, columns), bf16),
        grid=(n,),
        in_specs=[
            pl.BlockSpec((count, wide), lambda s: (0, s)),
            full(dk),
            full(dv),
            pl.BlockSpec((rows, wide), lambda s: (0, s)),
            full(dq),
            full(mix),
            pl.BlockSpec((rows, wide), lambda s: (0, s)),
            pl.BlockSpec((nf, 1, r, LANES), lambda s: (0, s, 0, 0)),
        ],
        out_specs=pl.BlockSpec((nf, 1, r, columns), lambda s: (0, s, 0, 0)),
        compiler_params=pltpu.CompilerParams(vmem_limit_bytes=LIMIT),
        cost_estimate=pl.CostEstimate(
            flops=2 * D * wide * (2 * count + 2 * rows),
            bytes_accessed=2 * D * (columns + 2 * rows + count),
            transcendentals=0,
        ),
        name="mid_grads",
    )(cond, dk, dv, h, dq, mix, gy, vectors.reshape(nf, n, r, LANES))
    return out.reshape(D, columns)


def self_kernel(h_ref, dq_ref, dk_ref, dv_ref, w_ref, gain_ref, vec_ref, mix_ref, gy_ref, out_ref):
    wide = dq_ref.shape[1]
    nf, _, r, _ = out_ref.shape
    turned = h_ref[...].T
    along = jnp.zeros((wide, 1), f32)
    for j, ref in enumerate((dq_ref, dk_ref, dv_ref)):
        grad = dot(turned, ref[...])
        place_rows(out_ref, j * wide, grad)
        weight = w_ref[:, j * wide : (j + 1) * wide].astype(f32)
        along = along + jnp.sum(grad * weight, axis=1, keepdims=True)
    along = jnp.broadcast_to(along / gain_ref[:, 0:1].astype(f32), (wide, LANES)).reshape(nf, r, LANES)
    lane = lax.broadcasted_iota(jnp.int32, along.shape, 2)
    vec = jnp.where(lane == 0, along, vec_ref[:, 0].astype(f32))
    out_ref[:, 0, :, 3 * wide : 3 * wide + LANES] = vec.astype(bf16)
    place_rows(out_ref, 3 * wide + LANES, contract(mix_ref[...], gy_ref[...], ((0,), (0,))))


def self_grads(h, dq, dk, dv, w_all, vectors, mix, gy, n, nf):
    rows, wide = dq.shape
    r = D // (n * nf)
    if r % 16 or wide % LANES:
        grad = outer_sum(h, jnp.concatenate([dq, dk, dv], axis=1))
        along = jnp.sum(grad * w_all[:, : 3 * wide].astype(f32), axis=1)
        along = (along / w_all[:, 3 * wide].astype(f32)).astype(bf16)
        along = along.reshape(n, nf, r, 1).transpose(1, 0, 2, 3).reshape(D, 1)
        grad_out = rows_by_owner(outer_sum(mix, gy).astype(bf16), n, nf)
        return jnp.concatenate([columns_by_owner(grad, n, nf), along, vectors[:, 1:], grad_out], axis=1)
    columns = 4 * wide + LANES

    def full(value):
        return pl.BlockSpec(value.shape, lambda s: (0, 0), pipeline_mode=pl.Buffered(1))

    out = pl.pallas_call(
        self_kernel,
        out_shape=jax.ShapeDtypeStruct((nf, n, r, columns), bf16),
        grid=(n,),
        in_specs=[
            pl.BlockSpec((rows, wide), lambda s: (0, s)),
            full(dq),
            full(dk),
            full(dv),
            pl.BlockSpec((wide, 3 * wide), lambda s: (s, 0)),
            pl.BlockSpec((wide, LANES), lambda s: (s, 3 * wide // LANES)),
            pl.BlockSpec((nf, 1, r, LANES), lambda s: (0, s, 0, 0)),
            full(mix),
            pl.BlockSpec((rows, wide), lambda s: (0, s)),
        ],
        out_specs=pl.BlockSpec((nf, 1, r, columns), lambda s: (0, s, 0, 0)),
        compiler_params=pltpu.CompilerParams(vmem_limit_bytes=LIMIT),
        cost_estimate=pl.CostEstimate(
            flops=8 * D * wide * rows, bytes_accessed=2 * D * (columns + rows + 3 * wide), transcendentals=0
        ),
        name="self_grads",
    )(h, dq, dk, dv, w_all, w_all, vectors.reshape(nf, n, r, LANES), mix, gy)
    return out.reshape(D, columns)


def column_parts(shard, parts, n):
    r, columns = shard.shape
    c = columns // (parts * n)
    return shard.reshape(r, parts, n, c).transpose(2, 0, 1, 3).reshape(n, r, parts * c)


def natural_columns(pieces, parts, n):
    r, columns = pieces.shape[1:]
    c = columns // parts
    return pieces.reshape(n, r, parts, c).transpose(1, 2, 0, 3).reshape(r, parts * n * c)


def spread_kernel(in_ref, out_ref):
    c = in_ref.shape[2]
    for s in range(in_ref.shape[0]):
        out_ref[:, s * c : (s + 1) * c] = in_ref[s].astype(f32)


def spread(pieces, width, parts, n, first=0):
    r = pieces.shape[1]
    c = width // n
    if r % 16 or c % LANES:
        return natural_columns(pieces[:, :, first * c : (first + parts) * c], parts, n).astype(f32)
    return pl.pallas_call(
        spread_kernel,
        out_shape=jax.ShapeDtypeStruct((r, parts * n * c), f32),
        grid=(parts,),
        in_specs=[pl.BlockSpec((n, r, c), lambda p: (0, 0, first + p))],
        out_specs=pl.BlockSpec((r, n * c), lambda p: (0, p)),
        name="spread",
    )(pieces)


def to_seq(pieces):
    return lax.all_to_all(pieces, "seq", 0, 0, tiled=True)


def gather_columns(pieces, n, nf):
    r, c = pieces.shape[1:]
    gathered = lax.all_gather(pieces.reshape(n * r, c), "fsdp", axis=0, tiled=True)
    return gathered.reshape(nf, n, r, c).transpose(1, 0, 2, 3).reshape(n * nf * r, c)


def columns_by_owner(grad, n, nf):
    rows, c = grad.shape
    r = rows // (n * nf)
    return grad.astype(bf16).reshape(n, nf, r, c).transpose(1, 0, 2, 3).reshape(rows, c)


def rows_by_owner(grad, n, nf):
    rows, columns = grad.shape
    r = rows // nf
    return grad.reshape(nf, r, n, columns // n).transpose(0, 2, 1, 3).reshape(nf * n * r, columns // n)


def share(rows_of_fsdp, n):
    rows, c = rows_of_fsdp.shape
    return to_seq(rows_of_fsdp.reshape(n, rows // n, c))


def rows_to_pieces(shard, n):
    r, columns = shard.shape
    return shard.reshape(r, n, columns // n).transpose(1, 0, 2).reshape(n * r, columns // n)


def pair_sum(part, j):
    low = part.astype(bf16)
    return low.astype(f32) + hop(low, j).astype(f32)


def sum_start(value, n):
    if n != 4:
        return (lax.psum(value, "seq"),)
    half = value.shape[1] // 2
    return pair_sum(value[:, :half], 1), pair_sum(value[:, half:], 2)


def sum_end(parts, n):
    if n != 4:
        return parts[0]
    return jnp.concatenate([pair_sum(parts[0], 2), pair_sum(parts[1], 1)], axis=1)


def pad_heads(value, parts):
    rows, columns = value.shape
    c = columns // parts
    if c % LANES == 0:
        return value
    padded = -(-c // LANES) * LANES
    return jnp.pad(value.reshape(rows, parts, c), ((0, 0), (0, 0), (0, padded - c))).reshape(
        rows, parts * padded
    )


def shards(
    tokens,
    conditioning,
    lengths,
    grad_output,
    norm_first,
    proj_self,
    out_self,
    norm_second,
    proj_query,
    proj_keyval,
    out_cross,
    norm_third,
    proj_gateup,
    bias_gateup,
    proj_down,
    bias_down,
):
    rows = tokens.shape[1]
    n = lax.axis_size("seq")
    nf = lax.axis_size("fsdp")
    me = lax.axis_index("seq")
    group = rows * n
    wide = D // n
    pairs = -(-wide // LANES)
    hidden = FF // n
    r = norm_first.shape[0]

    small = jnp.concatenate(
        [v.reshape(r, -1) for v in (norm_first, norm_second, norm_third, bias_down, bias_gateup)],
        axis=1,
    )
    small = jnp.pad(small, ((0, 0), (0, LANES - small.shape[1])))
    self_in = jnp.concatenate(
        [column_parts(proj_self, 3, n), jnp.broadcast_to(small[None], (n, r, LANES))], axis=2
    )
    self_pieces = to_seq(self_in)
    mid_pieces = to_seq(
        after(
            jnp.concatenate([column_parts(proj_keyval, 2, n), column_parts(proj_query, 1, n)], axis=2),
            self_pieces,
        )
    )
    group_tokens, _, ends = gather_rows(after(tokens[0], self_pieces), n)
    group_grad, grad_early, grad_ends = gather_rows(after(grad_output[0], *ends), n)

    self_all = gather_columns(self_pieces, n, nf)
    w_self = self_all[:, : 3 * wide]
    vectors = self_all[:, 3 * wide : 3 * wide + 12]
    gain_one, gain_two, gain_three, b_down = (vectors[:, j].astype(f32) for j in range(4))
    b_gateup = vectors[:, 4:12].reshape(2 * FF).astype(f32)
    b_gate = lax.dynamic_slice_in_dim(b_gateup, me * hidden, hidden, 0)
    b_upper = lax.dynamic_slice_in_dim(b_gateup, FF + me * hidden, hidden, 0)
    mid = jnp.concatenate(
        [
            mid_pieces.reshape(n * r, 3 * wide),
            rows_to_pieces(out_self, n),
            rows_to_pieces(out_cross, n),
        ],
        axis=1,
    )
    mid = lax.all_gather(mid, "fsdp", axis=0, tiled=True).reshape(nf, n, r, 5 * wide)
    kvq = mid[..., : 3 * wide].transpose(1, 0, 2, 3).reshape(D, 3 * wide)
    w_keyval, w_query = kvq[:, : 2 * wide], kvq[:, 2 * wide :]
    w_out = mid[..., 3 * wide : 4 * wide].transpose(0, 2, 1, 3).reshape(nf * r, D)
    w_cross = mid[..., 4 * wide :].transpose(0, 2, 1, 3).reshape(nf * r, D)
    group_lengths = lengths[0]
    order = block_ids(n)
    all_rows = (order[:, None] * rows + jnp.arange(rows, dtype=jnp.int32)[None, :]).reshape(group)
    ids, positions = seq_info(all_rows, group_lengths)
    tables = angle_tables(positions)

    def block(value, j, low, high):
        return lax.slice_in_dim(value, j * rows + low, j * rows + high, axis=0)

    def scattered(rows_of):
        return scatter_rows(rows_of, rows, n)

    inputs = tokens[0].astype(f32)
    normal_one, scaled_one, _ = norm_rows(inputs, gain_one)
    group_tokens, *tables = lax.optimization_barrier((group_tokens, *tables))
    normed_one = norm_rows(group_tokens.astype(f32), gain_one)[2].astype(bf16)
    packed = after(pad_heads(dot(normed_one, w_self), 3), *grad_early)
    gateup_pieces = to_seq(after(column_parts(proj_gateup, 2, n), packed))
    w_down = lax.all_gather(after(proj_down, mid_pieces), "fsdp", axis=0, tiled=True)
    q, k, v, mixed, lse = attend(packed, packed, packed, (0, pairs, 2 * pairs), pairs, ids, ids, tables)
    gateup_pieces = after(gateup_pieces.reshape(n * r, 2 * hidden), mixed)
    w_gateup = lax.all_gather(gateup_pieces, "fsdp", axis=0, tiled=True)
    w_gateup = w_gateup.reshape(nf, n, r, 2 * hidden)
    if r % 16:
        w_gateup = w_gateup.transpose(1, 0, 2, 3).reshape(1, 1, D, 2 * hidden)
    mixed_in = after(mixed[:, :wide], *grad_ends)
    first = inputs + scattered(lambda *at: dot(block(mixed_in, *at), w_out))[0]

    normal_two, scaled_two, normed = norm_rows(first, gain_two)
    normed_two, _, _ = gather_rows(normed.astype(bf16), n)
    cq = pad_heads(dot(normed_two, w_query).astype(bf16), 1)
    cond_rows = conditioning[0].reshape(SEQS_GRP * COND, D)
    count = SEQS_GRP * COND
    count_pad = -(-count // 16) * 16
    keyval = pad_heads(dot(cond_rows, w_keyval).astype(bf16), 2)
    keyval = jnp.pad(keyval, ((0, count_pad - count), (0, 0)))
    index = jnp.arange(count_pad, dtype=jnp.int32)
    cond_ids = jnp.where(index < count, index // COND, -1)
    cmix, clse = attend(cq, keyval, keyval, (0, 0, pairs), pairs, ids, cond_ids)
    cmix_in = cmix[:, :wide]
    second = first + scattered(lambda *at: dot(block(cmix_in, *at), w_cross))[0]

    normal_three, scaled_three, normed = norm_rows(second, gain_three)
    normed_three, _, _ = gather_rows(normed.astype(bf16), n)
    active, grad_gate, grad_upper, sum_gate, sum_upper, back_three, grad_w_down = feed(
        normed_three, group_grad, w_gateup, w_down, b_gate, b_upper
    )
    grad_rows = grad_output[0].astype(f32)
    grad_b_down = jnp.sum(grad_rows, axis=0)
    through, early = scattered(lambda *at: block(back_three, *at))
    own_down = lax.psum_scatter(grad_w_down, "fsdp", scatter_dimension=0, tiled=True)
    grad_w_gateup = gateup_grads(after(normed_three, *early), grad_gate, grad_upper, n, nf)
    through, grad_w_gateup = lax.optimization_barrier((through, grad_w_gateup))
    through, grad_gain_three = norm_back(through, normal_three, scaled_three, gain_three)
    grad_second = grad_rows + through

    group_second, early, _ = gather_rows(grad_second.astype(bf16), n)
    grad_w_gateup = after(grad_w_gateup, own_down, *early)
    own_gateup = lax.psum_scatter(grad_w_gateup, "fsdp", scatter_dimension=0, tiled=True)
    grad_cmix = pad_heads(back_prod(group_second, w_cross).astype(bf16), 1)
    dcq, dck, dcv = attend_back(
        cq, keyval, keyval, (0, 0, pairs), pairs, grad_cmix, cmix, clse, ids, cond_ids
    )
    dcq, dck, dcv = dcq[:, :wide], dck[:, :wide], dcv[:, :wide]
    cond_full = jnp.pad(cond_rows, ((0, count_pad - count), (0, 0)))
    through, _ = scattered(lambda *at: back_prod(block(dcq, *at), w_query))
    b_whole = lax.dynamic_update_slice(
        jnp.zeros((2, FF), f32), jnp.concatenate([sum_gate, sum_upper], axis=0), (0, me * hidden)
    )
    vectors = jnp.concatenate(
        [v.reshape(n, nf, r, -1) for v in (grad_gain_three, grad_b_down, b_whole)], axis=3
    )
    vectors = vectors.astype(bf16).transpose(1, 0, 2, 3).reshape(nf * n * r, -1)
    vectors = jnp.pad(vectors, ((0, 0), (0, LANES - vectors.shape[1])))
    grad_w_mid = mid_grads(cond_full, dck, dcv, normed_two, dcq, cmix_in, group_second, vectors, n, nf)
    through, grad_w_mid = lax.optimization_barrier((through, grad_w_mid))
    through, grad_gain_two = norm_back(through, normal_two, scaled_two, gain_two)
    grad_first = grad_second + through

    gains = grad_gain_two.astype(bf16).reshape(n, nf, r, 1).transpose(1, 0, 2, 3).reshape(D, 1)
    gains = jnp.pad(gains, ((0, 0), (1, LANES - 2)))
    group_first, _, _ = gather_rows(grad_first.astype(bf16), n)
    group_first, gains = lax.optimization_barrier((group_first, gains))
    grad_w_mid = after(grad_w_mid, own_gateup, group_first)
    own_mid = lax.psum_scatter(grad_w_mid, "fsdp", scatter_dimension=0, tiled=True)
    own_gateup = share(after(own_gateup, group_first), n)
    grad_keyval = jnp.concatenate([dck, dcv], axis=1)[:count]
    cond_part = after(back_prod(grad_keyval, w_keyval), group_first)
    late_active = after(active, group_first)
    down = dot(late_active, w_down).astype(bf16)
    down_pieces = scatter_start(down, n)
    grad_mixed = pad_heads(back_prod(group_first, w_out).astype(bf16), 1)
    grad_mixed = after(grad_mixed, down)
    dq, dk, dv = attend_back(q, k, v, (0, 0, 0), pairs, grad_mixed, mixed, lse, ids, ids, tables)
    dq, dk, dv = dq[:, :wide], dk[:, :wide], dv[:, :wide]
    dq, own_gateup = lax.optimization_barrier((after(dq, *down_pieces), own_gateup))
    grad_w_self = self_grads(normed_one, dq, dk, dv, self_all, gains, mixed_in, group_first, n, nf)
    dq, dk, dv, grad_w_self = lax.optimization_barrier((dq, dk, dv, grad_w_self))
    own_self = lax.psum_scatter(after(grad_w_self, own_mid), "fsdp", scatter_dimension=0, tiled=True)
    grad_packed = jnp.concatenate([dq, dk, dv], axis=1)
    through, early = scattered(lambda *at: back_prod(block(grad_packed, *at), w_self))
    mid_part = share(after(own_mid[:, : 3 * wide + LANES], *early), n)
    through, mid_part = lax.optimization_barrier((through, mid_part))
    down_pieces = [after(piece, *early) for piece in down_pieces]
    result = second + scatter_end(down, down_pieces, n) + b_down
    cond_parts = sum_start(after(cond_part, *early), n)
    grad_cond = sum_end(cond_parts, n).reshape(1, SEQS_GRP, COND, D)
    grad_inputs = grad_first + norm_back(through, normal_one, scaled_one, gain_one)[0]

    def joined(pieces):
        return pieces.reshape(n, r, wide).transpose(1, 0, 2).reshape(r, D)

    split = 3 * wide + LANES
    vectors = jnp.sum(mid_part[:, :, 3 * wide :].astype(f32), axis=0)
    own_cross = joined(own_mid[:, split:])
    own_out = joined(own_self[:, split:])
    self_part = share(own_self[:, :split], n)
    gains = jnp.sum(self_part[:, :, 3 * wide :].astype(f32), axis=0)

    return (
        result.astype(bf16)[None],
        grad_inputs[None],
        grad_cond,
        gains[:, 0],
        spread(self_part, D, 3, n),
        own_out.astype(f32),
        gains[:, 1],
        spread(mid_part, D, 1, n, 2),
        spread(mid_part, D, 2, n),
        own_cross.astype(f32),
        vectors[:, 0],
        spread(own_gateup, FF, 2, n),
        vectors[:, 2:10].reshape(8 * r),
        own_down.astype(f32),
        vectors[:, 1],
    )


def solution(mesh):
    rows_of = P("fsdp", "seq", None)
    matrix = P(ALL, None)
    vector = P(ALL)
    return jax.shard_map(
        shards,
        mesh=mesh,
        in_specs=(
            rows_of,
            P("fsdp", None, None, None),
            P("fsdp", None),
            rows_of,
            vector,
            matrix,
            matrix,
            vector,
            matrix,
            matrix,
            matrix,
            vector,
            matrix,
            vector,
            matrix,
            vector,
        ),
        out_specs=(
            rows_of,
            rows_of,
            P("fsdp", None, None, None),
            vector,
            matrix,
            matrix,
            vector,
            matrix,
            matrix,
            matrix,
            vector,
            matrix,
            vector,
            matrix,
            vector,
        ),
        check_vma=False,
    )
```

```python
import functools
import math

import jax
import jax.numpy as jnp
from jax import lax
from jax.experimental import pallas as pl
from jax.experimental.pallas import tpu as pltpu
from jax.sharding import PartitionSpec as P

D = 1536
HEADS = 24
HEAD = 64
FF = 6144
COND = 130
SEQS_GRP = 2
LANES = 128

epsilon = 1e-05
masked_score = -1e30
bf16 = jnp.bfloat16
f32 = jnp.float32
ALL = ("seq", "fsdp")


def seq_info(global_rows, group_lengths):
    ends = jnp.cumsum(group_lengths)
    starts = ends - group_lengths
    ident = jnp.sum((global_rows[:, None] >= ends[None, :]).astype(jnp.int32), axis=1)
    onehot = ident[:, None] == jnp.arange(group_lengths.shape[0], dtype=jnp.int32)[None, :]
    begin = jnp.sum(jnp.where(onehot, starts[None, :], 0), axis=1)
    return (ident, (global_rows - begin).astype(f32))


def angle_tables(positions):
    half = HEAD // 2
    inverse = jnp.power(10000.0, -jnp.arange(half, dtype=f32) / half)
    turned = positions[:, None] * inverse[None, :]
    cosine, sine = jnp.cos(turned), jnp.sin(turned)
    reps = LANES // HEAD
    return (
        jnp.concatenate([cosine, cosine] * reps, axis=1),
        jnp.concatenate([-sine, sine] * reps, axis=1),
    )


def norm_rows(values, gain):
    centre = values - jnp.mean(values, axis=-1, keepdims=True)
    spread = jnp.mean(centre * centre, axis=-1, keepdims=True)
    scaled = lax.rsqrt(spread + epsilon)
    normal = centre * scaled
    return (normal, scaled, normal * gain)


def norm_back(grad_rows, normal, scaled, gain):
    weighted = grad_rows * gain
    mean_one = jnp.mean(weighted, axis=-1, keepdims=True)
    mean_two = jnp.mean(weighted * normal, axis=-1, keepdims=True)
    return (scaled * (weighted - mean_one - normal * mean_two), jnp.sum(grad_rows * normal, axis=0))


def dot(left, right):
    return jnp.dot(left, right, preferred_element_type=f32)


def outer_sum(left, right):
    return lax.dot_general(left, right, (((0,), (0,)), ((), ())), preferred_element_type=f32)


def back_prod(left, weight):
    return lax.dot_general(left, weight, (((1,), (1,)), ((), ())), preferred_element_type=f32)


def after(value, *others):
    if not others:
        return value
    return lax.optimization_barrier((value,) + others)[0]


def hop(value, j):
    return lax.ppermute(value, "seq", [(i, i ^ j) for i in range(4)])


def block_ids(n):
    if n == 4:
        return lax.axis_index("seq") ^ jnp.arange(n, dtype=jnp.int32)
    return jnp.arange(n, dtype=jnp.int32)


def gather_rows(value, n, gates=()):
    if n != 4:
        whole = lax.all_gather(value, "seq", axis=0, tiled=True)
        return whole, (whole,), (whole,)
    half = value.shape[0] // 2
    first, second = hop(value, 1), hop(value, 2)
    first, second = after(first, *gates), after(second, *gates)
    third, fourth = hop(second[:half], 1), hop(first[half:], 2)
    whole = jnp.concatenate([value, first, second, third, fourth], axis=0)
    return whole, (first, second), (third, fourth)


def scatter_rows(blocks, rows, n, gates=()):
    if n != 4:
        whole = jnp.concatenate([blocks(j, 0, rows) for j in range(n)], axis=0).astype(bf16)
        out = lax.psum_scatter(whole, "seq", scatter_dimension=0, tiled=True).astype(f32)
        return out, (out,)
    half = rows // 2
    to_first = hop(blocks(3, 0, half).astype(bf16), 1)
    to_second = hop(blocks(3, half, rows).astype(bf16), 2)
    to_first, to_second = after(to_first, *gates), after(to_second, *gates)
    one, two = blocks(1, 0, rows).astype(f32), blocks(2, 0, rows).astype(f32)
    one = jnp.concatenate([one[:half], one[half:] + to_second.astype(f32)], axis=0)
    two = jnp.concatenate([two[:half] + to_first.astype(f32), two[half:]], axis=0)
    one, two = hop(one.astype(bf16), 1), hop(two.astype(bf16), 2)
    own = blocks(0, 0, rows).astype(f32)
    return own + one.astype(f32) + two.astype(f32), (to_first, to_second)


def scatter_start(partial, n):
    if n != 4:
        return (lax.psum_scatter(partial, "seq", scatter_dimension=0, tiled=True),)
    half = partial.shape[0] // 8
    return (
        hop(partial[6 * half : 7 * half], 1),
        hop(partial[7 * half :], 2),
        hop(partial[2 * half : 3 * half], 1),
        hop(partial[5 * half : 6 * half], 2),
    )


def scatter_end(partial, pieces, n):
    if n != 4:
        return pieces[0].astype(f32)
    half = partial.shape[0] // 8
    to_first, to_second, one, two = (piece.astype(f32) for piece in pieces)
    sum_one = hop((partial[3 * half : 4 * half].astype(f32) + to_second).astype(bf16), 1)
    sum_two = hop((partial[4 * half : 5 * half].astype(f32) + to_first).astype(bf16), 2)
    others = jnp.concatenate([one + sum_two.astype(f32), sum_one.astype(f32) + two], axis=0)
    return partial[: 2 * half].astype(f32) + others


def swap_halves(value):
    lane = lax.broadcasted_iota(jnp.int32, value.shape, 1)
    half = HEAD // 2
    return jnp.where(
        lane % HEAD < half, pltpu.roll(value, LANES - half, 1), pltpu.roll(value, half, 1)
    )


def head_rows(h):
    return slice(h * HEAD, (h + 1) * HEAD)


def lane_mask(value, h):
    lane = lax.broadcasted_iota(jnp.int32, value.shape, 1)
    return jnp.where(lane // HEAD == h, value, jnp.zeros_like(value))


FAR = 1e30


def pieces_of(value):
    high = value.astype(bf16).astype(f32)
    rest = value - high
    middle = rest.astype(bf16).astype(f32)
    return high, middle, rest - middle


def key_lanes(keys, kid, h):
    lane = lax.broadcasted_iota(jnp.int32, keys.shape, 1)
    spare = lane % HEAD
    ones = jnp.where(spare <= SEQS_GRP + 3, 1.0, 0.0)
    padding = jnp.where(spare == SEQS_GRP, jnp.where(kid < 0, 1.0, 0.0), ones)
    extra = jnp.where(spare < SEQS_GRP, jnp.where(kid == spare, 1.0, 0.0), padding)
    return jnp.where(lane // HEAD == h, keys.astype(f32), extra).astype(bf16)


def query_rows(turned, qid, h, offsets=()):
    row = lax.broadcasted_iota(jnp.int32, turned.shape, 0)
    spare = row % HEAD
    extra = jnp.where(spare <= SEQS_GRP, jnp.where(qid == spare, 0.0, -FAR), 0.0)
    for j, offset in enumerate(offsets):
        extra = jnp.where(spare == SEQS_GRP + 1 + j, offset, extra)
    return jnp.where(row // HEAD == h, turned, extra).astype(bf16)


def value_lanes(values, h):
    lane = lax.broadcasted_iota(jnp.int32, values.shape, 1)
    ones = jnp.where(lane % HEAD < 3, 1.0, 0.0)
    return jnp.where(lane // HEAD == h, values.astype(f32), ones).astype(bf16)


def grad_rows_of(turned, h, offsets):
    row = lax.broadcasted_iota(jnp.int32, turned.shape, 0)
    extra = jnp.zeros_like(turned)
    for j, offset in enumerate(offsets):
        extra = jnp.where(row % HEAD == j, offset, extra)
    return jnp.where(row // HEAD == h, turned, extra).astype(bf16)


PAIR = LANES // HEAD


def attend_kernel(rope, tile, *refs):
    if rope:
        q_ref, k_ref, v_ref, cos_ref, sin_ref, qid_ref, kid_ref = refs[:7]
        qo_ref, ko_ref, vo_ref, o_ref, lse_ref, qt, kb, vt, ot = refs[7:]
        q, k = q_ref[...], k_ref[...]
        q = (q * cos_ref[...] + swap_halves(q) * sin_ref[...]).astype(bf16)
        k = (k * cos_ref[...] + swap_halves(k) * sin_ref[...]).astype(bf16)
        v = v_ref[...].astype(bf16)
        qo_ref[...] = q
        ko_ref[...] = k
        vo_ref[...] = v
    else:
        q_ref, k_ref, v_ref, qid_ref, kid_ref, o_ref, lse_ref, qt, kb, vt, ot = refs
        q, k, v = q_ref[...], k_ref[...], v_ref[...]
    turned = q.astype(f32).T * 0.125
    for h in range(PAIR):
        qt[h] = query_rows(turned, qid_ref[...], h)
        kb[h] = key_lanes(k, kid_ref[...], h)
    vt[...] = v.astype(f32).T.astype(bf16)
    units = [(t * tile, h) for t in range(ot.shape[1] // tile) for h in range(PAIR)]

    def scores(unit):
        start, h = unit
        return dot(kb[h], qt[h, :, start : start + tile])

    later = scores(units[0])
    for i, (start, h) in enumerate(units):
        s = later
        if i + 1 < len(units):
            later = scores(units[i + 1])
        at = slice(start, start + tile)
        top = jnp.max(s, axis=0, keepdims=True)
        e = jnp.exp(s - top)
        total = jnp.sum(e, axis=0, keepdims=True)
        ot[head_rows(h), at] = dot(vt[head_rows(h), :], e.astype(bf16)) * (1.0 / total)
        lse_ref[0, h : h + 1, at] = top + jnp.log(total)
    o_ref[...] = ot[...].T.astype(bf16)


def attend_back_kernel(rope, tile, *refs):
    if rope:
        q_ref, k_ref, v_ref, do_ref, o_ref, lse_ref, cos_ref, sin_ref, qid_ref, kid_ref = refs[:10]
        dq_ref, dk_ref, dv_ref, qt, gt, kb, vb, kt, dqt, dk_acc, dv_acc = refs[10:]
    else:
        q_ref, k_ref, v_ref, do_ref, o_ref, lse_ref, qid_ref, kid_ref = refs[:8]
        dq_ref, dk_ref, dv_ref, qt, gt, kb, vb, kt, dqt, dk_acc, dv_acc = refs[8:]
    turned = q_ref[...].astype(f32).T * 0.125
    grads = do_ref[...].astype(f32).T
    product = grads * o_ref[...].astype(f32).T
    kt[...] = k_ref[...].astype(f32).T.astype(bf16)
    for h in range(PAIR):
        delta = jnp.sum(product[head_rows(h), :], axis=0, keepdims=True)
        qt[h] = query_rows(turned, qid_ref[...], h, pieces_of(-lse_ref[0, h : h + 1, :]))
        gt[h] = grad_rows_of(grads, h, pieces_of(-delta))
        kb[h] = key_lanes(k_ref[...], kid_ref[...], h)
        vb[h] = value_lanes(v_ref[...], h)
    tiles = dqt.shape[1] // tile
    units = [(t * tile, h) for t in range(tiles) for h in range(PAIR)]

    def products(unit):
        start, h = unit
        at = slice(start, start + tile)
        return dot(kb[h], qt[h, :, at]), dot(vb[h], gt[h, :, at])

    later = products(units[0])
    low_p, low_ds = [], []
    for i, (start, h) in enumerate(units):
        s, dp = later
        if i + 1 < len(units):
            later = products(units[i + 1])
        at = slice(start, start + tile)
        p = jnp.exp(s)
        ds = (p * dp).astype(bf16)
        dqt[head_rows(h), at] = dot(kt[head_rows(h), :], ds)
        low_p.append(p.astype(bf16))
        low_ds.append(ds)
        if h == PAIR - 1:
            rows_do = jnp.concatenate([lane_mask(do_ref[at, :], j) for j in range(PAIR)], axis=0)
            rows_q = jnp.concatenate([lane_mask(q_ref[at, :], j) for j in range(PAIR)], axis=0)
            dv = dot(jnp.concatenate(low_p, axis=1), rows_do)
            dk = dot(jnp.concatenate(low_ds, axis=1), rows_q)
            dv_acc[...] = dv if start == 0 else dv_acc[...] + dv
            dk_acc[...] = dk if start == 0 else dk_acc[...] + dk
            low_p, low_ds = [], []
    dq = dqt[...].T * 0.125
    dk = dk_acc[...] * 0.125
    if rope:
        dq = dq * cos_ref[...] - swap_halves(dq) * sin_ref[...]
        dk = dk * cos_ref[...] - swap_halves(dk) * sin_ref[...]
    dq_ref[...] = dq.astype(bf16)
    dk_ref[...] = dk.astype(bf16)
    dv_ref[...] = dv_acc[...].astype(bf16)


def query_tile(rows):
    for tile in (256, 128):
        if rows % tile == 0:
            return tile
    return rows


def spec(rows, offset=0):
    return pl.BlockSpec((rows, LANES), lambda i: (0, i + offset))


def whole(shape):
    return pl.BlockSpec(shape, lambda i: (0,) * len(shape), pipeline_mode=pl.Buffered(1))


LIMIT = 56 * 1024 * 1024
TILE, CHUNK, GTILE = 256, 320, 512


def attend(q, k, v, offsets, pairs, qid, kid, tables=None):
    nq, nk = q.shape[0], k.shape[0]
    rope = tables is not None
    tile = query_tile(nq)
    ins = [spec(nq, offsets[0]), spec(nk, offsets[1]), spec(nk, offsets[2])]
    args = [q, k, v]
    outs, shapes = [], []
    if rope:
        ins += [whole((nq, LANES)), whole((nq, LANES))]
        args += list(tables)
        outs += [spec(nq), spec(nk), spec(nk)]
        shapes += [jax.ShapeDtypeStruct((rows, pairs * LANES), bf16) for rows in (nq, nk, nk)]
    ins += [whole((1, nq)), whole((nk, 1))]
    args += [qid[None, :], kid[:, None]]
    outs += [spec(nq), pl.BlockSpec((1, 8, nq), lambda i: (i, 0, 0))]
    shapes += [
        jax.ShapeDtypeStruct((nq, pairs * LANES), bf16),
        jax.ShapeDtypeStruct((pairs, 8, nq), f32),
    ]
    return pl.pallas_call(
        functools.partial(attend_kernel, rope, tile),
        out_shape=shapes,
        grid=(pairs,),
        in_specs=ins,
        out_specs=outs,
        scratch_shapes=[
            pltpu.VMEM((PAIR, LANES, nq), bf16),
            pltpu.VMEM((PAIR, nk, LANES), bf16),
            pltpu.VMEM((LANES, nk), bf16),
            pltpu.VMEM((LANES, nq), f32),
        ],
        compiler_params=pltpu.CompilerParams(vmem_limit_bytes=LIMIT),
        cost_estimate=pl.CostEstimate(
            flops=2 * 2 * 2 * pairs * nq * nk * LANES,
            bytes_accessed=pairs * LANES * (nq + nk) * 12,
            transcendentals=2 * pairs * nq * nk,
        ),
        name="attend_self" if rope else "attend_cross",
    )(*args)


def attend_back(q, k, v, offsets, pairs, grad, mixed, lse, qid, kid, tables=None):
    nq, nk = q.shape[0], k.shape[0]
    rope = tables is not None
    tile = query_tile(nq)
    ins = [spec(nq, offsets[0]), spec(nk, offsets[1]), spec(nk, offsets[2]), spec(nq), spec(nq)]
    args = [q, k, v, grad, mixed]
    ins += [pl.BlockSpec((1, 8, nq), lambda i: (i, 0, 0))]
    args += [lse]
    if rope:
        ins += [whole((nq, LANES)), whole((nq, LANES))]
        args += list(tables)
    ins += [whole((1, nq)), whole((nk, 1))]
    args += [qid[None, :], kid[:, None]]
    return pl.pallas_call(
        functools.partial(attend_back_kernel, rope, tile),
        out_shape=[jax.ShapeDtypeStruct((rows, pairs * LANES), bf16) for rows in (nq, nk, nk)],
        grid=(pairs,),
        in_specs=ins,
        out_specs=[spec(nq), spec(nk), spec(nk)],
        scratch_shapes=[
            pltpu.VMEM((PAIR, LANES, nq), bf16),
            pltpu.VMEM((PAIR, LANES, nq), bf16),
            pltpu.VMEM((PAIR, nk, LANES), bf16),
            pltpu.VMEM((PAIR, nk, LANES), bf16),
            pltpu.VMEM((LANES, nk), bf16),
            pltpu.VMEM((LANES, nq), f32),
            pltpu.VMEM((nk, LANES), f32),
            pltpu.VMEM((nk, LANES), f32),
        ],
        compiler_params=pltpu.CompilerParams(vmem_limit_bytes=LIMIT),
        cost_estimate=pl.CostEstimate(
            flops=2 * 5 * 2 * pairs * nq * nk * LANES,
            bytes_accessed=pairs * LANES * (nq + nk) * 12,
            transcendentals=2 * pairs * nq * nk,
        ),
        name="back_self" if rope else "back_cross",
    )(*args)


def contract(left, right, dims):
    return lax.dot_general(left, right, (dims, ((), ())), preferred_element_type=f32)


def feed_kernel(chunk, *refs):
    h_ref, gy_ref, wg_ref, wu_ref, wd_ref, bg_ref, bu_ref = refs[:7]
    act_ref, dg_ref, du_ref, sg_ref, su_ref, dh_ref, dw_ref, both, total = refs[7:]
    step = pl.program_id(0)
    span = wg_ref.shape[0] * wg_ref.shape[2]
    tile = wg_ref.shape[3]
    for j in range(wg_ref.shape[1]):
        at = slice(j * span, (j + 1) * span)
        both[at, :tile] = wg_ref[:, j].reshape(span, tile)
        both[at, tile:] = wu_ref[:, j].reshape(span, tile)
    sg_ref[...] = jnp.zeros_like(sg_ref)
    su_ref[...] = jnp.zeros_like(su_ref)

    @pl.when(step == 0)
    def _():
        total[...] = jnp.zeros_like(total)

    def rows_at(i):
        return slice(i * chunk, (i + 1) * chunk)

    def products(i):
        at = rows_at(i)
        return dot(h_ref[at, :], both[...]), contract(gy_ref[at, :], wd_ref[...], ((1,), (1,)))

    def finish(i, pair, grad):
        at = rows_at(i)
        gate = pair[:, :tile] + bg_ref[...]
        upper = pair[:, tile:] + bu_ref[...]
        sigma = jax.nn.sigmoid(gate)
        silu = gate * sigma
        act_ref[at, :] = (silu * upper).astype(bf16)
        dg = (grad * upper * sigma * (1.0 + gate * (1.0 - sigma))).astype(bf16)
        du = (grad * silu).astype(bf16)
        dg_ref[at, :] = dg
        du_ref[at, :] = du
        sg_ref[...] += jnp.sum(dg.astype(f32), axis=0, keepdims=True)
        su_ref[...] += jnp.sum(du.astype(f32), axis=0, keepdims=True)
        return jnp.concatenate([dg, du], axis=1)

    chunks = h_ref.shape[0] // chunk
    now = products(0)
    for i in range(chunks):
        later = products(i + 1) if i + 1 < chunks else None
        grads = finish(i, *now)
        total[rows_at(i), :] += contract(grads, both[...], ((1,), (1,)))
        now = later
    dw_ref[...] = dot(act_ref[...].T, gy_ref[...]).astype(bf16)

    @pl.when(step == pl.num_programs(0) - 1)
    def _():
        dh_ref[...] = total[...].astype(bf16)


def feed(h, gy, w_gateup, w_down, b_gate, b_upper):
    rows = h.shape[0]
    hidden = w_down.shape[0]
    tile = TILE if rows <= 1280 else 128
    steps = hidden // tile
    lead = w_gateup.shape[:3]
    chunk = CHUNK if rows % CHUNK == 0 else rows
    one = pl.Buffered(1)
    rows_all = pl.BlockSpec((rows, D), lambda t: (0, 0), pipeline_mode=one)
    columns = pl.BlockSpec((rows, tile), lambda t: (0, t))
    vector = pl.BlockSpec((1, tile), lambda t: (0, t))
    return pl.pallas_call(
        functools.partial(feed_kernel, chunk),
        out_shape=[jax.ShapeDtypeStruct((rows, hidden), bf16)] * 3
        + [jax.ShapeDtypeStruct((1, hidden), f32)] * 2
        + [jax.ShapeDtypeStruct((rows, D), bf16), jax.ShapeDtypeStruct((hidden, D), bf16)],
        grid=(steps,),
        in_specs=[
            rows_all,
            rows_all,
            pl.BlockSpec(lead + (tile,), lambda t: (0, 0, 0, t)),
            pl.BlockSpec(lead + (tile,), lambda t: (0, 0, 0, t + steps)),
            pl.BlockSpec((tile, D), lambda t: (t, 0)),
            vector,
            vector,
        ],
        out_specs=[columns, columns, columns, vector, vector, rows_all, pl.BlockSpec((tile, D), lambda t: (t, 0))],
        scratch_shapes=[
            pltpu.VMEM((D, 2 * tile), bf16),
            pltpu.VMEM((rows, D), f32),
        ],
        compiler_params=pltpu.CompilerParams(vmem_limit_bytes=LIMIT),
        cost_estimate=pl.CostEstimate(
            flops=2 * 6 * rows * D * hidden,
            bytes_accessed=2 * (3 * rows * D + 3 * rows * hidden + 4 * D * hidden),
            transcendentals=rows * hidden,
        ),
        name="feed",
    )(h, gy, w_gateup, w_gateup, w_down, b_gate[None], b_upper[None])


def place_rows(out_ref, start, value):
    nf, _, r, _ = out_ref.shape
    width = value.shape[1]
    out_ref[:, 0, :, start : start + width] = value.astype(bf16).reshape(nf, r, width)


def gateup_kernel(h_ref, dg_ref, du_ref, out_ref, turned):
    step = pl.program_id(0)
    half = pl.num_programs(0) // 2
    nf, n, r, tile = out_ref.shape
    wide = nf * r

    @pl.when(step == 0)
    def _():
        for s in range(n):
            at = slice(s * wide, (s + 1) * wide)
            turned[at, :] = h_ref[:, at].T

    def fill(grad):
        for s in range(n):
            value = dot(turned[s * wide : (s + 1) * wide, :], grad)
            out_ref[:, s] = value.astype(bf16).reshape(nf, r, tile)

    @pl.when(step < half)
    def _():
        fill(dg_ref[...])

    @pl.when(step >= half)
    def _():
        fill(du_ref[...])


def gateup_grads(h, dg, du, n, nf):
    rows, hidden = dg.shape
    r, wide = D // (n * nf), D // n
    if r % 16 or wide % LANES:
        joined = jnp.concatenate([dg, du], axis=1)
        return columns_by_owner(outer_sum(h, joined), n, nf)
    tile = GTILE
    half = hidden // tile
    out = pl.pallas_call(
        gateup_kernel,
        out_shape=jax.ShapeDtypeStruct((nf, n, r, 2 * hidden), bf16),
        grid=(2 * half,),
        in_specs=[
            pl.BlockSpec((rows, D), lambda t: (0, 0), pipeline_mode=pl.Buffered(1)),
            pl.BlockSpec((rows, tile), lambda t: (0, jnp.minimum(t, half - 1))),
            pl.BlockSpec((rows, tile), lambda t: (0, jnp.maximum(t - half, 0))),
        ],
        out_specs=pl.BlockSpec((nf, n, r, tile), lambda t: (0, 0, 0, t)),
        scratch_shapes=[pltpu.VMEM((D, rows), bf16)],
        compiler_params=pltpu.CompilerParams(vmem_limit_bytes=LIMIT),
        cost_estimate=pl.CostEstimate(
            flops=4 * rows * D * hidden, bytes_accessed=4 * D * hidden + 6 * rows * hidden, transcendentals=0
        ),
        name="gateup_grads",
    )(h, dg, du)
    return out.reshape(D, 2 * hidden)


def mid_kernel(cond_ref, dk_ref, dv_ref, h_ref, dq_ref, mix_ref, gy_ref, vec_ref, out_ref):
    wide = dq_ref.shape[1]
    outer = ((0,), (0,))
    turned = cond_ref[...].T
    place_rows(out_ref, 0, dot(turned, dk_ref[...]))
    place_rows(out_ref, wide, dot(turned, dv_ref[...]))
    place_rows(out_ref, 2 * wide, contract(h_ref[...], dq_ref[...], outer))
    out_ref[:, 0, :, 3 * wide : 3 * wide + LANES] = vec_ref[:, 0]
    place_rows(out_ref, 3 * wide + LANES, contract(mix_ref[...], gy_ref[...], outer))


def mid_grads(cond, dk, dv, h, dq, mix, gy, vectors, n, nf):
    rows, wide = dq.shape
    r = D // (n * nf)
    if r % 16 or wide % LANES:
        return jnp.concatenate(
            [
                columns_by_owner(outer_sum(cond, jnp.concatenate([dk, dv], axis=1)), n, nf),
                columns_by_owner(outer_sum(h, dq), n, nf),
                vectors,
                rows_by_owner(outer_sum(mix, gy).astype(bf16), n, nf),
            ],
            axis=1,
        )
    count = cond.shape[0]
    columns = 4 * wide + LANES

    def full(value):
        return pl.BlockSpec(value.shape, lambda s: (0, 0), pipeline_mode=pl.Buffered(1))

    out = pl.pallas_call(
        mid_kernel,
        out_shape=jax.ShapeDtypeStruct((nf, n, r, columns), bf16),
        grid=(n,),
        in_specs=[
            pl.BlockSpec((count, wide), lambda s: (0, s)),
            full(dk),
            full(dv),
            pl.BlockSpec((rows, wide), lambda s: (0, s)),
            full(dq),
            full(mix),
            pl.BlockSpec((rows, wide), lambda s: (0, s)),
            pl.BlockSpec((nf, 1, r, LANES), lambda s: (0, s, 0, 0)),
        ],
        out_specs=pl.BlockSpec((nf, 1, r, columns), lambda s: (0, s, 0, 0)),
        compiler_params=pltpu.CompilerParams(vmem_limit_bytes=LIMIT),
        cost_estimate=pl.CostEstimate(
            flops=2 * D * wide * (2 * count + 2 * rows),
            bytes_accessed=2 * D * (columns + 2 * rows + count),
            transcendentals=0,
        ),
        name="mid_grads",
    )(cond, dk, dv, h, dq, mix, gy, vectors.reshape(nf, n, r, LANES))
    return out.reshape(D, columns)


def self_kernel(h_ref, dq_ref, dk_ref, dv_ref, w_ref, gain_ref, vec_ref, mix_ref, gy_ref, out_ref):
    wide = dq_ref.shape[1]
    nf, _, r, _ = out_ref.shape
    turned = h_ref[...].T
    along = jnp.zeros((wide, 1), f32)
    for j, ref in enumerate((dq_ref, dk_ref, dv_ref)):
        grad = dot(turned, ref[...])
        place_rows(out_ref, j * wide, grad)
        weight = w_ref[:, j * wide : (j + 1) * wide].astype(f32)
        along = along + jnp.sum(grad * weight, axis=1, keepdims=True)
    along = jnp.broadcast_to(along / gain_ref[:, 0:1].astype(f32), (wide, LANES)).reshape(nf, r, LANES)
    lane = lax.broadcasted_iota(jnp.int32, along.shape, 2)
    vec = jnp.where(lane == 0, along, vec_ref[:, 0].astype(f32))
    out_ref[:, 0, :, 3 * wide : 3 * wide + LANES] = vec.astype(bf16)
    place_rows(out_ref, 3 * wide + LANES, contract(mix_ref[...], gy_ref[...], ((0,), (0,))))


def self_grads(h, dq, dk, dv, w_all, vectors, mix, gy, n, nf):
    rows, wide = dq.shape
    r = D // (n * nf)
    if r % 16 or wide % LANES:
        grad = outer_sum(h, jnp.concatenate([dq, dk, dv], axis=1))
        along = jnp.sum(grad * w_all[:, : 3 * wide].astype(f32), axis=1)
        along = (along / w_all[:, 3 * wide].astype(f32)).astype(bf16)
        along = along.reshape(n, nf, r, 1).transpose(1, 0, 2, 3).reshape(D, 1)
        grad_out = rows_by_owner(outer_sum(mix, gy).astype(bf16), n, nf)
        return jnp.concatenate([columns_by_owner(grad, n, nf), along, vectors[:, 1:], grad_out], axis=1)
    columns = 4 * wide + LANES

    def full(value):
        return pl.BlockSpec(value.shape, lambda s: (0, 0), pipeline_mode=pl.Buffered(1))

    out = pl.pallas_call(
        self_kernel,
        out_shape=jax.ShapeDtypeStruct((nf, n, r, columns), bf16),
        grid=(n,),
        in_specs=[
            pl.BlockSpec((rows, wide), lambda s: (0, s)),
            full(dq),
            full(dk),
            full(dv),
            pl.BlockSpec((wide, 3 * wide), lambda s: (s, 0)),
            pl.BlockSpec((wide, LANES), lambda s: (s, 3 * wide // LANES)),
            pl.BlockSpec((nf, 1, r, LANES), lambda s: (0, s, 0, 0)),
            full(mix),
            pl.BlockSpec((rows, wide), lambda s: (0, s)),
        ],
        out_specs=pl.BlockSpec((nf, 1, r, columns), lambda s: (0, s, 0, 0)),
        compiler_params=pltpu.CompilerParams(vmem_limit_bytes=LIMIT),
        cost_estimate=pl.CostEstimate(
            flops=8 * D * wide * rows, bytes_accessed=2 * D * (columns + rows + 3 * wide), transcendentals=0
        ),
        name="self_grads",
    )(h, dq, dk, dv, w_all, w_all, vectors.reshape(nf, n, r, LANES), mix, gy)
    return out.reshape(D, columns)


def column_parts(shard, parts, n):
    r, columns = shard.shape
    c = columns // (parts * n)
    return shard.reshape(r, parts, n, c).transpose(2, 0, 1, 3).reshape(n, r, parts * c)


def natural_columns(pieces, parts, n):
    r, columns = pieces.shape[1:]
    c = columns // parts
    return pieces.reshape(n, r, parts, c).transpose(1, 2, 0, 3).reshape(r, parts * n * c)


def spread_kernel(in_ref, out_ref):
    c = in_ref.shape[2]
    for s in range(in_ref.shape[0]):
        out_ref[:, s * c : (s + 1) * c] = in_ref[s].astype(f32)


def spread(pieces, width, parts, n, start=0):
    r = pieces.shape[1]
    c = width // n
    if r % 16 or c % LANES:
        return natural_columns(pieces[:, :, start : start + parts * c], parts, n).astype(f32)
    step = math.gcd(c, start) if start else c
    if step < c:
        pieces, start = pieces[:, :, start : start + parts * c], 0
    first = start // c
    return pl.pallas_call(
        spread_kernel,
        out_shape=jax.ShapeDtypeStruct((r, parts * n * c), f32),
        grid=(parts,),
        in_specs=[pl.BlockSpec((n, r, c), lambda p: (0, 0, first + p))],
        out_specs=pl.BlockSpec((r, n * c), lambda p: (0, p)),
        name="spread",
    )(pieces)


def to_seq(pieces):
    return lax.all_to_all(pieces, "seq", 0, 0, tiled=True)


def gather_columns(pieces, n, nf):
    r, c = pieces.shape[1:]
    gathered = lax.all_gather(pieces.reshape(n * r, c), "fsdp", axis=0, tiled=True)
    return gathered.reshape(nf, n, r, c).transpose(1, 0, 2, 3).reshape(n * nf * r, c)


def columns_by_owner(grad, n, nf):
    rows, c = grad.shape
    r = rows // (n * nf)
    return grad.astype(bf16).reshape(n, nf, r, c).transpose(1, 0, 2, 3).reshape(rows, c)


def rows_by_owner(grad, n, nf):
    rows, columns = grad.shape
    r = rows // nf
    return grad.reshape(nf, r, n, columns // n).transpose(0, 2, 1, 3).reshape(nf * n * r, columns // n)


def share(rows_of_fsdp, n):
    rows, c = rows_of_fsdp.shape
    return to_seq(rows_of_fsdp.reshape(n, rows // n, c))


def rows_to_pieces(shard, n):
    r, columns = shard.shape
    return shard.reshape(r, n, columns // n).transpose(1, 0, 2).reshape(n * r, columns // n)


def pair_sum(part, j):
    low = part.astype(bf16)
    return low.astype(f32) + hop(low, j).astype(f32)


def sum_start(value, n):
    if n != 4:
        return (lax.psum(value, "seq"),)
    half = value.shape[1] // 2
    return pair_sum(value[:, :half], 1), pair_sum(value[:, half:], 2)


def sum_end(parts, n):
    if n != 4:
        return parts[0]
    return jnp.concatenate([pair_sum(parts[0], 2), pair_sum(parts[1], 1)], axis=1)


def pad_heads(value, parts):
    rows, columns = value.shape
    c = columns // parts
    if c % LANES == 0:
        return value
    padded = -(-c // LANES) * LANES
    return jnp.pad(value.reshape(rows, parts, c), ((0, 0), (0, 0), (0, padded - c))).reshape(
        rows, parts * padded
    )


def shards(
    tokens,
    conditioning,
    lengths,
    grad_output,
    norm_first,
    proj_self,
    out_self,
    norm_second,
    proj_query,
    proj_keyval,
    out_cross,
    norm_third,
    proj_gateup,
    bias_gateup,
    proj_down,
    bias_down,
):
    rows = tokens.shape[1]
    n = lax.axis_size("seq")
    nf = lax.axis_size("fsdp")
    me = lax.axis_index("seq")
    group = rows * n
    wide = D // n
    pairs = -(-wide // LANES)
    hidden = FF // n
    r = norm_first.shape[0]

    small = jnp.concatenate(
        [v.reshape(r, -1) for v in (norm_first, norm_second, norm_third, bias_down, bias_gateup)],
        axis=1,
    )
    small = jnp.pad(small, ((0, 0), (0, LANES - small.shape[1])))
    self_in = jnp.concatenate(
        [column_parts(proj_self, 3, n), jnp.broadcast_to(small[None], (n, r, LANES))], axis=2
    )
    self_pieces = to_seq(self_in)
    mid_pieces = to_seq(
        after(
            jnp.concatenate([column_parts(proj_keyval, 2, n), column_parts(proj_query, 1, n)], axis=2),
            self_pieces,
        )
    )
    group_tokens, _, ends = gather_rows(after(tokens[0], self_pieces), n)
    group_grad, grad_early, grad_ends = gather_rows(after(grad_output[0], *ends), n)

    self_all = gather_columns(self_pieces, n, nf)
    w_self = self_all[:, : 3 * wide]
    vectors = self_all[:, 3 * wide : 3 * wide + 12]
    gain_one, gain_two, gain_three, b_down = (vectors[:, j].astype(f32) for j in range(4))
    b_gateup = vectors[:, 4:12].reshape(2 * FF).astype(f32)
    b_gate = lax.dynamic_slice_in_dim(b_gateup, me * hidden, hidden, 0)
    b_upper = lax.dynamic_slice_in_dim(b_gateup, FF + me * hidden, hidden, 0)
    mid = jnp.concatenate(
        [
            mid_pieces.reshape(n * r, 3 * wide),
            rows_to_pieces(out_self, n),
            rows_to_pieces(out_cross, n),
        ],
        axis=1,
    )
    mid = lax.all_gather(mid, "fsdp", axis=0, tiled=True).reshape(nf, n, r, 5 * wide)
    kvq = mid[..., : 3 * wide].transpose(1, 0, 2, 3).reshape(D, 3 * wide)
    w_keyval, w_query = kvq[:, : 2 * wide], kvq[:, 2 * wide :]
    w_out = mid[..., 3 * wide : 4 * wide].transpose(0, 2, 1, 3).reshape(nf * r, D)
    w_cross = mid[..., 4 * wide :].transpose(0, 2, 1, 3).reshape(nf * r, D)
    group_lengths = lengths[0]
    order = block_ids(n)
    all_rows = (order[:, None] * rows + jnp.arange(rows, dtype=jnp.int32)[None, :]).reshape(group)
    ids, positions = seq_info(all_rows, group_lengths)
    tables = angle_tables(positions)

    def block(value, j, low, high):
        return lax.slice_in_dim(value, j * rows + low, j * rows + high, axis=0)

    def scattered(rows_of):
        return scatter_rows(rows_of, rows, n)

    inputs = tokens[0].astype(f32)
    normal_one, scaled_one, _ = norm_rows(inputs, gain_one)
    group_tokens, *tables = lax.optimization_barrier((group_tokens, *tables))
    normed_one = norm_rows(group_tokens.astype(f32), gain_one)[2].astype(bf16)
    packed = after(pad_heads(dot(normed_one, w_self), 3), *grad_early)
    gateup_pieces = to_seq(after(column_parts(proj_gateup, 2, n), packed))
    w_down = lax.all_gather(after(proj_down, mid_pieces), "fsdp", axis=0, tiled=True)
    q, k, v, mixed, lse = attend(packed, packed, packed, (0, pairs, 2 * pairs), pairs, ids, ids, tables)
    mixed = after(mixed, *grad_ends)
    gateup_pieces = after(gateup_pieces.reshape(n * r, 2 * hidden), mixed)
    w_gateup = lax.all_gather(gateup_pieces, "fsdp", axis=0, tiled=True)
    w_gateup = w_gateup.reshape(nf, n, r, 2 * hidden)
    if r % 16:
        w_gateup = w_gateup.transpose(1, 0, 2, 3).reshape(1, 1, D, 2 * hidden)
    mixed_in = mixed[:, :wide]
    first = inputs + scattered(lambda *at: dot(block(mixed_in, *at), w_out))[0]

    normal_two, scaled_two, normed = norm_rows(first, gain_two)
    normed_two, _, _ = gather_rows(normed.astype(bf16), n)
    cq = pad_heads(dot(normed_two, w_query).astype(bf16), 1)
    cond_rows = conditioning[0].reshape(SEQS_GRP * COND, D)
    count = SEQS_GRP * COND
    count_pad = -(-count // 16) * 16
    keyval = pad_heads(dot(cond_rows, w_keyval).astype(bf16), 2)
    keyval = jnp.pad(keyval, ((0, count_pad - count), (0, 0)))
    index = jnp.arange(count_pad, dtype=jnp.int32)
    cond_ids = jnp.where(index < count, index // COND, -1)
    cmix, clse = attend(cq, keyval, keyval, (0, 0, pairs), pairs, ids, cond_ids)
    cmix_in = cmix[:, :wide]
    second = first + scattered(lambda *at: dot(block(cmix_in, *at), w_cross))[0]

    normal_three, scaled_three, normed = norm_rows(second, gain_three)
    normed_three, _, _ = gather_rows(normed.astype(bf16), n)
    active, grad_gate, grad_upper, sum_gate, sum_upper, back_three, grad_w_down = feed(
        normed_three, group_grad, w_gateup, w_down, b_gate, b_upper
    )
    grad_rows = grad_output[0].astype(f32)
    grad_b_down = jnp.sum(grad_rows, axis=0)
    through, early = scattered(lambda *at: block(back_three, *at))
    own_down = lax.psum_scatter(grad_w_down, "fsdp", scatter_dimension=0, tiled=True)
    grad_w_gateup = gateup_grads(after(normed_three, *early), grad_gate, grad_upper, n, nf)
    through, grad_w_gateup = lax.optimization_barrier((through, grad_w_gateup))
    through, grad_gain_three = norm_back(through, normal_three, scaled_three, gain_three)
    grad_second = grad_rows + through

    group_second, early, _ = gather_rows(grad_second.astype(bf16), n)
    grad_w_gateup = after(grad_w_gateup, own_down, *early)
    own_gateup = lax.psum_scatter(grad_w_gateup, "fsdp", scatter_dimension=0, tiled=True)
    grad_cmix = pad_heads(back_prod(group_second, w_cross).astype(bf16), 1)
    dcq, dck, dcv = attend_back(
        cq, keyval, keyval, (0, 0, pairs), pairs, grad_cmix, cmix, clse, ids, cond_ids
    )
    dcq, dck, dcv = dcq[:, :wide], dck[:, :wide], dcv[:, :wide]
    cond_full = jnp.pad(cond_rows, ((0, count_pad - count), (0, 0)))
    through, _ = scattered(lambda *at: back_prod(block(dcq, *at), w_query))
    b_whole = lax.dynamic_update_slice(
        jnp.zeros((2, FF), f32), jnp.concatenate([sum_gate, sum_upper], axis=0), (0, me * hidden)
    )
    vectors = jnp.concatenate(
        [v.reshape(n, nf, r, -1) for v in (grad_gain_three, grad_b_down, b_whole)], axis=3
    )
    vectors = vectors.astype(bf16).transpose(1, 0, 2, 3).reshape(nf * n * r, -1)
    vectors = jnp.pad(vectors, ((0, 0), (0, LANES - vectors.shape[1])))
    grad_w_mid = mid_grads(cond_full, dck, dcv, normed_two, dcq, cmix_in, group_second, vectors, n, nf)
    through, grad_w_mid = lax.optimization_barrier((through, grad_w_mid))
    through, grad_gain_two = norm_back(through, normal_two, scaled_two, gain_two)
    grad_first = grad_second + through

    gains = grad_gain_two.astype(bf16).reshape(n, nf, r, 1).transpose(1, 0, 2, 3).reshape(D, 1)
    gains = jnp.pad(gains, ((0, 0), (1, LANES - 2)))
    down = dot(after(active, grad_first), w_down).astype(bf16)
    group_first, _, _ = gather_rows(grad_first.astype(bf16), n, (down,))
    group_first, gains = lax.optimization_barrier((group_first, gains))
    grad_w_mid = after(grad_w_mid, own_gateup, group_first)
    own_mid = lax.psum_scatter(grad_w_mid, "fsdp", scatter_dimension=0, tiled=True)
    own_gateup = share(after(own_gateup, group_first), n)
    grad_keyval = jnp.concatenate([dck, dcv], axis=1)[:count]
    cond_part = after(back_prod(grad_keyval, w_keyval), group_first)
    down = after(down, group_first)
    down_pieces = scatter_start(down, n)
    grad_mixed = pad_heads(back_prod(group_first, w_out).astype(bf16), 1)
    grad_mixed = after(grad_mixed, down)
    dq, dk, dv = attend_back(q, k, v, (0, 0, 0), pairs, grad_mixed, mixed, lse, ids, ids, tables)
    dq, dk, dv = dq[:, :wide], dk[:, :wide], dv[:, :wide]
    dq, own_gateup = lax.optimization_barrier((after(dq, *down_pieces), own_gateup))
    grad_w_self = self_grads(normed_one, dq, dk, dv, self_all, gains, mixed_in, group_first, n, nf)
    dq, dk, dv, grad_w_self = lax.optimization_barrier((dq, dk, dv, grad_w_self))
    own_self = lax.psum_scatter(after(grad_w_self, own_mid), "fsdp", scatter_dimension=0, tiled=True)
    grad_packed = jnp.concatenate([dq, dk, dv], axis=1)
    through, early = scattered(lambda *at: back_prod(block(grad_packed, *at), w_self))
    down_pieces = [after(piece, *early) for piece in down_pieces]
    result = second + scatter_end(down, down_pieces, n) + b_down
    cond_parts = sum_start(after(cond_part, *early), n)
    own_gateup = after(own_gateup, *early)

    def joined(pieces):
        return pieces.reshape(n, r, wide).transpose(1, 0, 2).reshape(r, D)

    split = 3 * wide + LANES
    own_cross = joined(own_mid[:, split:])
    own_out = joined(own_self[:, split:])
    last_part = share(jnp.concatenate([own_mid[:, :split], own_self[:, :split]], axis=1), n)
    grad_cond = sum_end([after(part, last_part) for part in cond_parts], n)
    grad_cond = grad_cond.reshape(1, SEQS_GRP, COND, D)
    vectors = jnp.sum(last_part[:, :, 3 * wide : split].astype(f32), axis=0)
    grad_inputs = grad_first + norm_back(through, normal_one, scaled_one, gain_one)[0]
    gains = jnp.sum(last_part[:, :, split + 3 * wide :].astype(f32), axis=0)

    return (
        result.astype(bf16)[None],
        grad_inputs[None],
        grad_cond,
        gains[:, 0],
        spread(last_part, D, 3, n, split),
        own_out.astype(f32),
        gains[:, 1],
        spread(last_part, D, 1, n, 2 * wide),
        spread(last_part, D, 2, n),
        own_cross.astype(f32),
        vectors[:, 0],
        spread(own_gateup, FF, 2, n),
        vectors[:, 2:10].reshape(8 * r),
        own_down.astype(f32),
        vectors[:, 1],
    )


def solution(mesh):
    rows_of = P("fsdp", "seq", None)
    matrix = P(ALL, None)
    vector = P(ALL)
    return jax.shard_map(
        shards,
        mesh=mesh,
        in_specs=(
            rows_of,
            P("fsdp", None, None, None),
            P("fsdp", None),
            rows_of,
            vector,
            matrix,
            matrix,
            vector,
            matrix,
            matrix,
            matrix,
            vector,
            matrix,
            vector,
            matrix,
            vector,
        ),
        out_specs=(
            rows_of,
            rows_of,
            P("fsdp", None, None, None),
            vector,
            matrix,
            matrix,
            vector,
            matrix,
            matrix,
            matrix,
            vector,
            matrix,
            vector,
            matrix,
            vector,
        ),
        check_vma=False,
    )
```

```python
import functools
import math

import jax
import jax.numpy as jnp
from jax import lax
from jax.experimental import pallas as pl
from jax.experimental.pallas import tpu as pltpu
from jax.sharding import PartitionSpec as P

D = 1536
HEADS = 24
HEAD = 64
FF = 6144
COND = 130
SEQS_GRP = 2
LANES = 128

epsilon = 1e-05
masked_score = -1e30
bf16 = jnp.bfloat16
f32 = jnp.float32
ALL = ("seq", "fsdp")


def seq_info(global_rows, group_lengths):
    ends = jnp.cumsum(group_lengths)
    starts = ends - group_lengths
    ident = jnp.sum((global_rows[:, None] >= ends[None, :]).astype(jnp.int32), axis=1)
    onehot = ident[:, None] == jnp.arange(group_lengths.shape[0], dtype=jnp.int32)[None, :]
    begin = jnp.sum(jnp.where(onehot, starts[None, :], 0), axis=1)
    return (ident, (global_rows - begin).astype(f32))


def angle_tables(positions):
    half = HEAD // 2
    inverse = jnp.power(10000.0, -jnp.arange(half, dtype=f32) / half)
    turned = positions[:, None] * inverse[None, :]
    cosine, sine = jnp.cos(turned), jnp.sin(turned)
    reps = LANES // HEAD
    return (
        jnp.concatenate([cosine, cosine] * reps, axis=1),
        jnp.concatenate([-sine, sine] * reps, axis=1),
    )


def norm_rows(values, gain):
    centre = values - jnp.mean(values, axis=-1, keepdims=True)
    spread = jnp.mean(centre * centre, axis=-1, keepdims=True)
    scaled = lax.rsqrt(spread + epsilon)
    normal = centre * scaled
    return (normal, scaled, normal * gain)


def norm_back(grad_rows, normal, scaled, gain):
    weighted = grad_rows * gain
    mean_one = jnp.mean(weighted, axis=-1, keepdims=True)
    mean_two = jnp.mean(weighted * normal, axis=-1, keepdims=True)
    return (scaled * (weighted - mean_one - normal * mean_two), jnp.sum(grad_rows * normal, axis=0))


def dot(left, right):
    return jnp.dot(left, right, preferred_element_type=f32)


def outer_sum(left, right):
    return lax.dot_general(left, right, (((0,), (0,)), ((), ())), preferred_element_type=f32)


def back_prod(left, weight):
    return lax.dot_general(left, weight, (((1,), (1,)), ((), ())), preferred_element_type=f32)


def after(value, *others):
    if not others:
        return value
    return lax.optimization_barrier((value,) + others)[0]


def hop(value, j):
    return lax.ppermute(value, "seq", [(i, i ^ j) for i in range(4)])


def block_ids(n):
    if n == 4:
        return lax.axis_index("seq") ^ jnp.arange(n, dtype=jnp.int32)
    return jnp.arange(n, dtype=jnp.int32)


def gather_rows(value, n, gates=()):
    if n != 4:
        whole = lax.all_gather(value, "seq", axis=0, tiled=True)
        return whole, (whole,), (whole,)
    half = value.shape[0] // 2
    first, second = hop(value, 1), hop(value, 2)
    first, second = after(first, *gates), after(second, *gates)
    third, fourth = hop(second[:half], 1), hop(first[half:], 2)
    whole = jnp.concatenate([value, first, second, third, fourth], axis=0)
    return whole, (first, second), (third, fourth)


def scatter_rows(blocks, rows, n, gates=()):
    if n != 4:
        whole = jnp.concatenate([blocks(j, 0, rows) for j in range(n)], axis=0).astype(bf16)
        out = lax.psum_scatter(whole, "seq", scatter_dimension=0, tiled=True).astype(f32)
        return out, (out,)
    half = rows // 2
    to_first = hop(blocks(3, 0, half).astype(bf16), 1)
    to_second = hop(blocks(3, half, rows).astype(bf16), 2)
    to_first, to_second = after(to_first, *gates), after(to_second, *gates)
    one, two = blocks(1, 0, rows).astype(f32), blocks(2, 0, rows).astype(f32)
    one = jnp.concatenate([one[:half], one[half:] + to_second.astype(f32)], axis=0)
    two = jnp.concatenate([two[:half] + to_first.astype(f32), two[half:]], axis=0)
    one, two = hop(one.astype(bf16), 1), hop(two.astype(bf16), 2)
    own = blocks(0, 0, rows).astype(f32)
    return own + one.astype(f32) + two.astype(f32), (to_first, to_second)


def scatter_start(partial, n):
    if n != 4:
        return (lax.psum_scatter(partial, "seq", scatter_dimension=0, tiled=True),)
    half = partial.shape[0] // 8
    return (
        hop(partial[6 * half : 7 * half], 1),
        hop(partial[7 * half :], 2),
        hop(partial[2 * half : 3 * half], 1),
        hop(partial[5 * half : 6 * half], 2),
    )


def scatter_end(partial, pieces, n):
    if n != 4:
        return pieces[0].astype(f32)
    half = partial.shape[0] // 8
    to_first, to_second, one, two = (piece.astype(f32) for piece in pieces)
    sum_one = hop((partial[3 * half : 4 * half].astype(f32) + to_second).astype(bf16), 1)
    sum_two = hop((partial[4 * half : 5 * half].astype(f32) + to_first).astype(bf16), 2)
    others = jnp.concatenate([one + sum_two.astype(f32), sum_one.astype(f32) + two], axis=0)
    return partial[: 2 * half].astype(f32) + others


def swap_halves(value):
    lane = lax.broadcasted_iota(jnp.int32, value.shape, 1)
    half = HEAD // 2
    return jnp.where(
        lane % HEAD < half, pltpu.roll(value, LANES - half, 1), pltpu.roll(value, half, 1)
    )


def head_rows(h):
    return slice(h * HEAD, (h + 1) * HEAD)


def lane_mask(value, h):
    lane = lax.broadcasted_iota(jnp.int32, value.shape, 1)
    return jnp.where(lane // HEAD == h, value, jnp.zeros_like(value))


FAR = 1e30


def pieces_of(value):
    high = value.astype(bf16).astype(f32)
    rest = value - high
    middle = rest.astype(bf16).astype(f32)
    return high, middle, rest - middle


def key_lanes(keys, kid, h):
    lane = lax.broadcasted_iota(jnp.int32, keys.shape, 1)
    spare = lane % HEAD
    ones = jnp.where(spare <= SEQS_GRP + 3, 1.0, 0.0)
    padding = jnp.where(spare == SEQS_GRP, jnp.where(kid < 0, 1.0, 0.0), ones)
    extra = jnp.where(spare < SEQS_GRP, jnp.where(kid == spare, 1.0, 0.0), padding)
    return jnp.where(lane // HEAD == h, keys.astype(f32), extra).astype(bf16)


def query_rows(turned, qid, h, offsets=()):
    row = lax.broadcasted_iota(jnp.int32, turned.shape, 0)
    spare = row % HEAD
    extra = jnp.where(spare <= SEQS_GRP, jnp.where(qid == spare, 0.0, -FAR), 0.0)
    for j, offset in enumerate(offsets):
        extra = jnp.where(spare == SEQS_GRP + 1 + j, offset, extra)
    return jnp.where(row // HEAD == h, turned, extra).astype(bf16)


def value_lanes(values, h):
    lane = lax.broadcasted_iota(jnp.int32, values.shape, 1)
    ones = jnp.where(lane % HEAD < 3, 1.0, 0.0)
    return jnp.where(lane // HEAD == h, values.astype(f32), ones).astype(bf16)


def grad_rows_of(turned, h, offsets):
    row = lax.broadcasted_iota(jnp.int32, turned.shape, 0)
    extra = jnp.zeros_like(turned)
    for j, offset in enumerate(offsets):
        extra = jnp.where(row % HEAD == j, offset, extra)
    return jnp.where(row // HEAD == h, turned, extra).astype(bf16)


PAIR = LANES // HEAD


def attend_kernel(rope, tile, *refs):
    if rope:
        q_ref, k_ref, v_ref, cos_ref, sin_ref, qid_ref, kid_ref = refs[:7]
        qo_ref, ko_ref, vo_ref, o_ref, lse_ref, qt, kb, vt, ot = refs[7:]
        q, k = q_ref[...], k_ref[...]
        q = (q * cos_ref[...] + swap_halves(q) * sin_ref[...]).astype(bf16)
        k = (k * cos_ref[...] + swap_halves(k) * sin_ref[...]).astype(bf16)
        v = v_ref[...].astype(bf16)
        qo_ref[...] = q
        ko_ref[...] = k
        vo_ref[...] = v
    else:
        q_ref, k_ref, v_ref, qid_ref, kid_ref, o_ref, lse_ref, qt, kb, vt, ot = refs
        q, k, v = q_ref[...], k_ref[...], v_ref[...]
    turned = q.astype(f32).T * 0.125
    for h in range(PAIR):
        qt[h] = query_rows(turned, qid_ref[...], h)
        kb[h] = key_lanes(k, kid_ref[...], h)
    vt[...] = v.astype(f32).T.astype(bf16)
    units = [(t * tile, h) for t in range(ot.shape[1] // tile) for h in range(PAIR)]

    def scores(unit):
        start, h = unit
        return dot(kb[h], qt[h, :, start : start + tile])

    later = scores(units[0])
    for i, (start, h) in enumerate(units):
        s = later
        if i + 1 < len(units):
            later = scores(units[i + 1])
        at = slice(start, start + tile)
        top = jnp.max(s, axis=0, keepdims=True)
        e = jnp.exp(s - top)
        total = jnp.sum(e, axis=0, keepdims=True)
        ot[head_rows(h), at] = dot(vt[head_rows(h), :], e.astype(bf16)) * (1.0 / total)
        lse_ref[0, h : h + 1, at] = top + jnp.log(total)
    o_ref[...] = ot[...].T.astype(bf16)


def attend_back_kernel(rope, tile, *refs):
    if rope:
        q_ref, k_ref, v_ref, do_ref, o_ref, lse_ref, cos_ref, sin_ref, qid_ref, kid_ref = refs[:10]
        dq_ref, dk_ref, dv_ref, qt, gt, kb, vb, kt, dqt, dk_acc, dv_acc = refs[10:]
    else:
        q_ref, k_ref, v_ref, do_ref, o_ref, lse_ref, qid_ref, kid_ref = refs[:8]
        dq_ref, dk_ref, dv_ref, qt, gt, kb, vb, kt, dqt, dk_acc, dv_acc = refs[8:]
    turned = q_ref[...].astype(f32).T * 0.125
    grads = do_ref[...].astype(f32).T
    product = grads * o_ref[...].astype(f32).T
    kt[...] = k_ref[...].astype(f32).T.astype(bf16)
    for h in range(PAIR):
        delta = jnp.sum(product[head_rows(h), :], axis=0, keepdims=True)
        qt[h] = query_rows(turned, qid_ref[...], h, pieces_of(-lse_ref[0, h : h + 1, :]))
        gt[h] = grad_rows_of(grads, h, pieces_of(-delta))
        kb[h] = key_lanes(k_ref[...], kid_ref[...], h)
        vb[h] = value_lanes(v_ref[...], h)
    tiles = dqt.shape[1] // tile
    units = [(t * tile, h) for t in range(tiles) for h in range(PAIR)]

    def products(unit):
        start, h = unit
        at = slice(start, start + tile)
        return dot(kb[h], qt[h, :, at]), dot(vb[h], gt[h, :, at])

    later = products(units[0])
    low_p, low_ds = [], []
    for i, (start, h) in enumerate(units):
        s, dp = later
        if i + 1 < len(units):
            later = products(units[i + 1])
        at = slice(start, start + tile)
        p = jnp.exp(s)
        ds = (p * dp).astype(bf16)
        dqt[head_rows(h), at] = dot(kt[head_rows(h), :], ds)
        low_p.append(p.astype(bf16))
        low_ds.append(ds)
        if h == PAIR - 1:
            rows_do = jnp.concatenate([lane_mask(do_ref[at, :], j) for j in range(PAIR)], axis=0)
            rows_q = jnp.concatenate([lane_mask(q_ref[at, :], j) for j in range(PAIR)], axis=0)
            dv = dot(jnp.concatenate(low_p, axis=1), rows_do)
            dk = dot(jnp.concatenate(low_ds, axis=1), rows_q)
            dv_acc[...] = dv if start == 0 else dv_acc[...] + dv
            dk_acc[...] = dk if start == 0 else dk_acc[...] + dk
            low_p, low_ds = [], []
    dq = dqt[...].T * 0.125
    dk = dk_acc[...] * 0.125
    if rope:
        dq = dq * cos_ref[...] - swap_halves(dq) * sin_ref[...]
        dk = dk * cos_ref[...] - swap_halves(dk) * sin_ref[...]
    dq_ref[...] = dq.astype(bf16)
    dk_ref[...] = dk.astype(bf16)
    dv_ref[...] = dv_acc[...].astype(bf16)


def query_tile(rows):
    for tile in (256, 128):
        if rows % tile == 0:
            return tile
    return rows


def spec(rows, offset=0):
    return pl.BlockSpec((rows, LANES), lambda i: (0, i + offset))


def whole(shape):
    return pl.BlockSpec(shape, lambda i: (0,) * len(shape), pipeline_mode=pl.Buffered(1))


LIMIT = 56 * 1024 * 1024
TILE, CHUNK, GTILE = 256, 320, 512


def attend(q, k, v, offsets, pairs, qid, kid, tables=None):
    nq, nk = q.shape[0], k.shape[0]
    rope = tables is not None
    tile = query_tile(nq)
    ins = [spec(nq, offsets[0]), spec(nk, offsets[1]), spec(nk, offsets[2])]
    args = [q, k, v]
    outs, shapes = [], []
    if rope:
        ins += [whole((nq, LANES)), whole((nq, LANES))]
        args += list(tables)
        outs += [spec(nq), spec(nk), spec(nk)]
        shapes += [jax.ShapeDtypeStruct((rows, pairs * LANES), bf16) for rows in (nq, nk, nk)]
    ins += [whole((1, nq)), whole((nk, 1))]
    args += [qid[None, :], kid[:, None]]
    outs += [spec(nq), pl.BlockSpec((1, 8, nq), lambda i: (i, 0, 0))]
    shapes += [
        jax.ShapeDtypeStruct((nq, pairs * LANES), bf16),
        jax.ShapeDtypeStruct((pairs, 8, nq), f32),
    ]
    return pl.pallas_call(
        functools.partial(attend_kernel, rope, tile),
        out_shape=shapes,
        grid=(pairs,),
        in_specs=ins,
        out_specs=outs,
        scratch_shapes=[
            pltpu.VMEM((PAIR, LANES, nq), bf16),
            pltpu.VMEM((PAIR, nk, LANES), bf16),
            pltpu.VMEM((LANES, nk), bf16),
            pltpu.VMEM((LANES, nq), f32),
        ],
        compiler_params=pltpu.CompilerParams(vmem_limit_bytes=LIMIT),
        cost_estimate=pl.CostEstimate(
            flops=2 * 2 * 2 * pairs * nq * nk * LANES,
            bytes_accessed=pairs * LANES * (nq + nk) * 12,
            transcendentals=2 * pairs * nq * nk,
        ),
        name="attend_self" if rope else "attend_cross",
    )(*args)


def attend_back(q, k, v, offsets, pairs, grad, mixed, lse, qid, kid, tables=None):
    nq, nk = q.shape[0], k.shape[0]
    rope = tables is not None
    tile = query_tile(nq)
    ins = [spec(nq, offsets[0]), spec(nk, offsets[1]), spec(nk, offsets[2]), spec(nq), spec(nq)]
    args = [q, k, v, grad, mixed]
    ins += [pl.BlockSpec((1, 8, nq), lambda i: (i, 0, 0))]
    args += [lse]
    if rope:
        ins += [whole((nq, LANES)), whole((nq, LANES))]
        args += list(tables)
    ins += [whole((1, nq)), whole((nk, 1))]
    args += [qid[None, :], kid[:, None]]
    return pl.pallas_call(
        functools.partial(attend_back_kernel, rope, tile),
        out_shape=[jax.ShapeDtypeStruct((rows, pairs * LANES), bf16) for rows in (nq, nk, nk)],
        grid=(pairs,),
        in_specs=ins,
        out_specs=[spec(nq), spec(nk), spec(nk)],
        scratch_shapes=[
            pltpu.VMEM((PAIR, LANES, nq), bf16),
            pltpu.VMEM((PAIR, LANES, nq), bf16),
            pltpu.VMEM((PAIR, nk, LANES), bf16),
            pltpu.VMEM((PAIR, nk, LANES), bf16),
            pltpu.VMEM((LANES, nk), bf16),
            pltpu.VMEM((LANES, nq), f32),
            pltpu.VMEM((nk, LANES), f32),
            pltpu.VMEM((nk, LANES), f32),
        ],
        compiler_params=pltpu.CompilerParams(vmem_limit_bytes=LIMIT),
        cost_estimate=pl.CostEstimate(
            flops=2 * 5 * 2 * pairs * nq * nk * LANES,
            bytes_accessed=pairs * LANES * (nq + nk) * 12,
            transcendentals=2 * pairs * nq * nk,
        ),
        name="back_self" if rope else "back_cross",
    )(*args)


def contract(left, right, dims):
    return lax.dot_general(left, right, (dims, ((), ())), preferred_element_type=f32)


def feed_kernel(chunk, *refs):
    h_ref, gy_ref, wg_ref, wu_ref, wd_ref, bg_ref, bu_ref = refs[:7]
    act_ref, dg_ref, du_ref, sg_ref, su_ref, dh_ref, dw_ref, both, total = refs[7:]
    step = pl.program_id(0)
    span = wg_ref.shape[0] * wg_ref.shape[2]
    tile = wg_ref.shape[3]
    for j in range(wg_ref.shape[1]):
        at = slice(j * span, (j + 1) * span)
        both[at, :tile] = wg_ref[:, j].reshape(span, tile)
        both[at, tile:] = wu_ref[:, j].reshape(span, tile)
    sg_ref[...] = jnp.zeros_like(sg_ref)
    su_ref[...] = jnp.zeros_like(su_ref)

    @pl.when(step == 0)
    def _():
        total[...] = jnp.zeros_like(total)

    def rows_at(i):
        return slice(i * chunk, (i + 1) * chunk)

    def products(i):
        at = rows_at(i)
        return dot(h_ref[at, :], both[...]), contract(gy_ref[at, :], wd_ref[...], ((1,), (1,)))

    def finish(i, pair, grad):
        at = rows_at(i)
        gate = pair[:, :tile] + bg_ref[...]
        upper = pair[:, tile:] + bu_ref[...]
        sigma = jax.nn.sigmoid(gate)
        silu = gate * sigma
        act_ref[at, :] = (silu * upper).astype(bf16)
        dg = (grad * upper * sigma * (1.0 + gate * (1.0 - sigma))).astype(bf16)
        du = (grad * silu).astype(bf16)
        dg_ref[at, :] = dg
        du_ref[at, :] = du
        sg_ref[...] += jnp.sum(dg.astype(f32), axis=0, keepdims=True)
        su_ref[...] += jnp.sum(du.astype(f32), axis=0, keepdims=True)
        return jnp.concatenate([dg, du], axis=1)

    chunks = h_ref.shape[0] // chunk
    now = products(0)
    for i in range(chunks):
        later = products(i + 1) if i + 1 < chunks else None
        grads = finish(i, *now)
        total[rows_at(i), :] += contract(grads, both[...], ((1,), (1,)))
        now = later
    dw_ref[...] = dot(act_ref[...].T, gy_ref[...]).astype(bf16)

    @pl.when(step == pl.num_programs(0) - 1)
    def _():
        dh_ref[...] = total[...].astype(bf16)


def feed(h, gy, w_gateup, w_down, b_gate, b_upper):
    rows = h.shape[0]
    hidden = w_down.shape[0]
    tile = TILE if rows <= 1280 else 128
    steps = hidden // tile
    lead = w_gateup.shape[:3]
    chunk = CHUNK if rows % CHUNK == 0 else rows
    one = pl.Buffered(1)
    rows_all = pl.BlockSpec((rows, D), lambda t: (0, 0), pipeline_mode=one)
    columns = pl.BlockSpec((rows, tile), lambda t: (0, t))
    vector = pl.BlockSpec((1, tile), lambda t: (0, t))
    return pl.pallas_call(
        functools.partial(feed_kernel, chunk),
        out_shape=[jax.ShapeDtypeStruct((rows, hidden), bf16)] * 3
        + [jax.ShapeDtypeStruct((1, hidden), f32)] * 2
        + [jax.ShapeDtypeStruct((rows, D), bf16), jax.ShapeDtypeStruct((hidden, D), bf16)],
        grid=(steps,),
        in_specs=[
            rows_all,
            rows_all,
            pl.BlockSpec(lead + (tile,), lambda t: (0, 0, 0, t)),
            pl.BlockSpec(lead + (tile,), lambda t: (0, 0, 0, t + steps)),
            pl.BlockSpec((tile, D), lambda t: (t, 0)),
            vector,
            vector,
        ],
        out_specs=[columns, columns, columns, vector, vector, rows_all, pl.BlockSpec((tile, D), lambda t: (t, 0))],
        scratch_shapes=[
            pltpu.VMEM((D, 2 * tile), bf16),
            pltpu.VMEM((rows, D), f32),
        ],
        compiler_params=pltpu.CompilerParams(vmem_limit_bytes=LIMIT),
        cost_estimate=pl.CostEstimate(
            flops=2 * 6 * rows * D * hidden,
            bytes_accessed=2 * (3 * rows * D + 3 * rows * hidden + 4 * D * hidden),
            transcendentals=rows * hidden,
        ),
        name="feed",
    )(h, gy, w_gateup, w_gateup, w_down, b_gate[None], b_upper[None])


def place_rows(out_ref, start, value):
    nf, _, r, _ = out_ref.shape
    width = value.shape[1]
    out_ref[:, 0, :, start : start + width] = value.astype(bf16).reshape(nf, r, width)


def gateup_kernel(h_ref, dg_ref, du_ref, out_ref, turned):
    step = pl.program_id(0)
    half = pl.num_programs(0) // 2
    nf, n, r, tile = out_ref.shape
    wide = nf * r

    @pl.when(step == 0)
    def _():
        for s in range(n):
            at = slice(s * wide, (s + 1) * wide)
            turned[at, :] = h_ref[:, at].T

    def fill(grad):
        for s in range(n):
            value = dot(turned[s * wide : (s + 1) * wide, :], grad)
            out_ref[:, s] = value.astype(bf16).reshape(nf, r, tile)

    @pl.when(step < half)
    def _():
        fill(dg_ref[...])

    @pl.when(step >= half)
    def _():
        fill(du_ref[...])


def gateup_grads(h, dg, du, n, nf):
    rows, hidden = dg.shape
    r, wide = D // (n * nf), D // n
    if r % 16 or wide % LANES:
        joined = jnp.concatenate([dg, du], axis=1)
        return columns_by_owner(outer_sum(h, joined), n, nf)
    tile = GTILE
    half = hidden // tile
    out = pl.pallas_call(
        gateup_kernel,
        out_shape=jax.ShapeDtypeStruct((nf, n, r, 2 * hidden), bf16),
        grid=(2 * half,),
        in_specs=[
            pl.BlockSpec((rows, D), lambda t: (0, 0), pipeline_mode=pl.Buffered(1)),
            pl.BlockSpec((rows, tile), lambda t: (0, jnp.minimum(t, half - 1))),
            pl.BlockSpec((rows, tile), lambda t: (0, jnp.maximum(t - half, 0))),
        ],
        out_specs=pl.BlockSpec((nf, n, r, tile), lambda t: (0, 0, 0, t)),
        scratch_shapes=[pltpu.VMEM((D, rows), bf16)],
        compiler_params=pltpu.CompilerParams(vmem_limit_bytes=LIMIT),
        cost_estimate=pl.CostEstimate(
            flops=4 * rows * D * hidden, bytes_accessed=4 * D * hidden + 6 * rows * hidden, transcendentals=0
        ),
        name="gateup_grads",
    )(h, dg, du)
    return out.reshape(D, 2 * hidden)


def mid_kernel(cond_ref, dk_ref, dv_ref, h_ref, dq_ref, mix_ref, gy_ref, vec_ref, out_ref):
    wide = dq_ref.shape[1]
    outer = ((0,), (0,))
    turned = cond_ref[...].T
    place_rows(out_ref, 0, dot(turned, dk_ref[...]))
    place_rows(out_ref, wide, dot(turned, dv_ref[...]))
    place_rows(out_ref, 2 * wide, contract(h_ref[...], dq_ref[...], outer))
    out_ref[:, 0, :, 3 * wide : 3 * wide + LANES] = vec_ref[:, 0]
    place_rows(out_ref, 3 * wide + LANES, contract(mix_ref[...], gy_ref[...], outer))


def mid_grads(cond, dk, dv, h, dq, mix, gy, vectors, n, nf):
    rows, wide = dq.shape
    r = D // (n * nf)
    if r % 16 or wide % LANES:
        return jnp.concatenate(
            [
                columns_by_owner(outer_sum(cond, jnp.concatenate([dk, dv], axis=1)), n, nf),
                columns_by_owner(outer_sum(h, dq), n, nf),
                vectors,
                rows_by_owner(outer_sum(mix, gy).astype(bf16), n, nf),
            ],
            axis=1,
        )
    count = cond.shape[0]
    columns = 4 * wide + LANES

    def full(value):
        return pl.BlockSpec(value.shape, lambda s: (0, 0), pipeline_mode=pl.Buffered(1))

    out = pl.pallas_call(
        mid_kernel,
        out_shape=jax.ShapeDtypeStruct((nf, n, r, columns), bf16),
        grid=(n,),
        in_specs=[
            pl.BlockSpec((count, wide), lambda s: (0, s)),
            full(dk),
            full(dv),
            pl.BlockSpec((rows, wide), lambda s: (0, s)),
            full(dq),
            full(mix),
            pl.BlockSpec((rows, wide), lambda s: (0, s)),
            pl.BlockSpec((nf, 1, r, LANES), lambda s: (0, s, 0, 0)),
        ],
        out_specs=pl.BlockSpec((nf, 1, r, columns), lambda s: (0, s, 0, 0)),
        compiler_params=pltpu.CompilerParams(vmem_limit_bytes=LIMIT),
        cost_estimate=pl.CostEstimate(
            flops=2 * D * wide * (2 * count + 2 * rows),
            bytes_accessed=2 * D * (columns + 2 * rows + count),
            transcendentals=0,
        ),
        name="mid_grads",
    )(cond, dk, dv, h, dq, mix, gy, vectors.reshape(nf, n, r, LANES))
    return out.reshape(D, columns)


def self_kernel(h_ref, dq_ref, dk_ref, dv_ref, w_ref, gain_ref, vec_ref, mix_ref, gy_ref, out_ref):
    wide = dq_ref.shape[1]
    nf, _, r, _ = out_ref.shape
    turned = h_ref[...].T
    along = jnp.zeros((wide, 1), f32)
    for j, ref in enumerate((dq_ref, dk_ref, dv_ref)):
        grad = dot(turned, ref[...])
        place_rows(out_ref, j * wide, grad)
        weight = w_ref[:, j * wide : (j + 1) * wide].astype(f32)
        along = along + jnp.sum(grad * weight, axis=1, keepdims=True)
    along = jnp.broadcast_to(along / gain_ref[:, 0:1].astype(f32), (wide, LANES)).reshape(nf, r, LANES)
    lane = lax.broadcasted_iota(jnp.int32, along.shape, 2)
    vec = jnp.where(lane == 0, along, vec_ref[:, 0].astype(f32))
    out_ref[:, 0, :, 3 * wide : 3 * wide + LANES] = vec.astype(bf16)
    place_rows(out_ref, 3 * wide + LANES, contract(mix_ref[...], gy_ref[...], ((0,), (0,))))


def self_grads(h, dq, dk, dv, w_all, vectors, mix, gy, n, nf):
    rows, wide = dq.shape
    r = D // (n * nf)
    if r % 16 or wide % LANES:
        grad = outer_sum(h, jnp.concatenate([dq, dk, dv], axis=1))
        along = jnp.sum(grad * w_all[:, : 3 * wide].astype(f32), axis=1)
        along = (along / w_all[:, 3 * wide].astype(f32)).astype(bf16)
        along = along.reshape(n, nf, r, 1).transpose(1, 0, 2, 3).reshape(D, 1)
        grad_out = rows_by_owner(outer_sum(mix, gy).astype(bf16), n, nf)
        return jnp.concatenate([columns_by_owner(grad, n, nf), along, vectors[:, 1:], grad_out], axis=1)
    columns = 4 * wide + LANES

    def full(value):
        return pl.BlockSpec(value.shape, lambda s: (0, 0), pipeline_mode=pl.Buffered(1))

    out = pl.pallas_call(
        self_kernel,
        out_shape=jax.ShapeDtypeStruct((nf, n, r, columns), bf16),
        grid=(n,),
        in_specs=[
            pl.BlockSpec((rows, wide), lambda s: (0, s)),
            full(dq),
            full(dk),
            full(dv),
            pl.BlockSpec((wide, 3 * wide), lambda s: (s, 0)),
            pl.BlockSpec((wide, LANES), lambda s: (s, 3 * wide // LANES)),
            pl.BlockSpec((nf, 1, r, LANES), lambda s: (0, s, 0, 0)),
            full(mix),
            pl.BlockSpec((rows, wide), lambda s: (0, s)),
        ],
        out_specs=pl.BlockSpec((nf, 1, r, columns), lambda s: (0, s, 0, 0)),
        compiler_params=pltpu.CompilerParams(vmem_limit_bytes=LIMIT),
        cost_estimate=pl.CostEstimate(
            flops=8 * D * wide * rows, bytes_accessed=2 * D * (columns + rows + 3 * wide), transcendentals=0
        ),
        name="self_grads",
    )(h, dq, dk, dv, w_all, w_all, vectors.reshape(nf, n, r, LANES), mix, gy)
    return out.reshape(D, columns)


def column_parts(shard, parts, n):
    r, columns = shard.shape
    c = columns // (parts * n)
    return shard.reshape(r, parts, n, c).transpose(2, 0, 1, 3).reshape(n, r, parts * c)


def natural_columns(pieces, parts, n):
    r, columns = pieces.shape[1:]
    c = columns // parts
    return pieces.reshape(n, r, parts, c).transpose(1, 2, 0, 3).reshape(r, parts * n * c)


def spread_kernel(in_ref, out_ref):
    c = in_ref.shape[2]
    for s in range(in_ref.shape[0]):
        out_ref[:, s * c : (s + 1) * c] = in_ref[s].astype(f32)


def spread(pieces, width, parts, n, start=0):
    r = pieces.shape[1]
    c = width // n
    if r % 16 or c % LANES:
        return natural_columns(pieces[:, :, start : start + parts * c], parts, n).astype(f32)
    step = math.gcd(c, start) if start else c
    if step < c:
        pieces, start = pieces[:, :, start : start + parts * c], 0
    first = start // c
    return pl.pallas_call(
        spread_kernel,
        out_shape=jax.ShapeDtypeStruct((r, parts * n * c), f32),
        grid=(parts,),
        in_specs=[pl.BlockSpec((n, r, c), lambda p: (0, 0, first + p))],
        out_specs=pl.BlockSpec((r, n * c), lambda p: (0, p)),
        name="spread",
    )(pieces)


def to_seq(pieces):
    return lax.all_to_all(pieces, "seq", 0, 0, tiled=True)


def gather_columns(pieces, n, nf):
    r, c = pieces.shape[1:]
    gathered = lax.all_gather(pieces.reshape(n * r, c), "fsdp", axis=0, tiled=True)
    return gathered.reshape(nf, n, r, c).transpose(1, 0, 2, 3).reshape(n * nf * r, c)


def columns_by_owner(grad, n, nf):
    rows, c = grad.shape
    r = rows // (n * nf)
    return grad.astype(bf16).reshape(n, nf, r, c).transpose(1, 0, 2, 3).reshape(rows, c)


def rows_by_owner(grad, n, nf):
    rows, columns = grad.shape
    r = rows // nf
    return grad.reshape(nf, r, n, columns // n).transpose(0, 2, 1, 3).reshape(nf * n * r, columns // n)


def share(rows_of_fsdp, n):
    rows, c = rows_of_fsdp.shape
    return to_seq(rows_of_fsdp.reshape(n, rows // n, c))


def rows_to_pieces(shard, n):
    r, columns = shard.shape
    return shard.reshape(r, n, columns // n).transpose(1, 0, 2).reshape(n * r, columns // n)


def pair_sum(part, j):
    low = part.astype(bf16)
    return low.astype(f32) + hop(low, j).astype(f32)


def sum_start(value, n):
    if n != 4:
        return (lax.psum(value, "seq"),)
    half = value.shape[1] // 2
    return pair_sum(value[:, :half], 1), pair_sum(value[:, half:], 2)


def sum_end(parts, n):
    if n != 4:
        return parts[0]
    return jnp.concatenate([pair_sum(parts[0], 2), pair_sum(parts[1], 1)], axis=1)


def pad_heads(value, parts):
    rows, columns = value.shape
    c = columns // parts
    if c % LANES == 0:
        return value
    padded = -(-c // LANES) * LANES
    return jnp.pad(value.reshape(rows, parts, c), ((0, 0), (0, 0), (0, padded - c))).reshape(
        rows, parts * padded
    )


def shards(
    tokens,
    conditioning,
    lengths,
    grad_output,
    norm_first,
    proj_self,
    out_self,
    norm_second,
    proj_query,
    proj_keyval,
    out_cross,
    norm_third,
    proj_gateup,
    bias_gateup,
    proj_down,
    bias_down,
):
    rows = tokens.shape[1]
    n = lax.axis_size("seq")
    nf = lax.axis_size("fsdp")
    me = lax.axis_index("seq")
    group = rows * n
    wide = D // n
    pairs = -(-wide // LANES)
    hidden = FF // n
    r = norm_first.shape[0]

    small = jnp.concatenate(
        [v.reshape(r, -1) for v in (norm_first, norm_second, norm_third, bias_down, bias_gateup)],
        axis=1,
    )
    small = jnp.pad(small, ((0, 0), (0, LANES - small.shape[1])))
    self_in = jnp.concatenate(
        [column_parts(proj_self, 3, n), jnp.broadcast_to(small[None], (n, r, LANES))], axis=2
    )
    self_pieces = to_seq(self_in)
    mid_pieces = to_seq(
        after(
            jnp.concatenate([column_parts(proj_keyval, 2, n), column_parts(proj_query, 1, n)], axis=2),
            self_pieces,
        )
    )
    group_tokens, _, ends = gather_rows(after(tokens[0], self_pieces), n)
    group_grad, grad_early, grad_ends = gather_rows(after(grad_output[0], *ends), n)

    first_in = jnp.concatenate([self_pieces.reshape(n * r, -1), rows_to_pieces(out_self, n)], axis=1)
    first_all = lax.all_gather(first_in, "fsdp", axis=0, tiled=True).reshape(nf, n, r, 4 * wide + LANES)
    self_all = first_all[..., : 3 * wide + LANES].transpose(1, 0, 2, 3).reshape(D, 3 * wide + LANES)
    w_out = first_all[..., 3 * wide + LANES :].transpose(0, 2, 1, 3).reshape(nf * r, D)
    w_self = self_all[:, : 3 * wide]
    vectors = self_all[:, 3 * wide : 3 * wide + 12]
    gain_one, gain_two, gain_three, b_down = (vectors[:, j].astype(f32) for j in range(4))
    b_gateup = vectors[:, 4:12].reshape(2 * FF).astype(f32)
    b_gate = lax.dynamic_slice_in_dim(b_gateup, me * hidden, hidden, 0)
    b_upper = lax.dynamic_slice_in_dim(b_gateup, FF + me * hidden, hidden, 0)
    mid = jnp.concatenate([mid_pieces.reshape(n * r, 3 * wide), rows_to_pieces(out_cross, n)], axis=1)
    mid = lax.all_gather(mid, "fsdp", axis=0, tiled=True).reshape(nf, n, r, 4 * wide)
    kvq = mid[..., : 3 * wide].transpose(1, 0, 2, 3).reshape(D, 3 * wide)
    w_keyval, w_query = kvq[:, : 2 * wide], kvq[:, 2 * wide :]
    w_cross = mid[..., 3 * wide :].transpose(0, 2, 1, 3).reshape(nf * r, D)
    group_lengths = lengths[0]
    order = block_ids(n)
    all_rows = (order[:, None] * rows + jnp.arange(rows, dtype=jnp.int32)[None, :]).reshape(group)
    ids, positions = seq_info(all_rows, group_lengths)
    tables = angle_tables(positions)

    def block(value, j, low, high):
        return lax.slice_in_dim(value, j * rows + low, j * rows + high, axis=0)

    def scattered(rows_of):
        return scatter_rows(rows_of, rows, n)

    inputs = tokens[0].astype(f32)
    normal_one, scaled_one, _ = norm_rows(inputs, gain_one)
    group_tokens, *tables = lax.optimization_barrier((group_tokens, *tables))
    normed_one = norm_rows(group_tokens.astype(f32), gain_one)[2].astype(bf16)
    packed = after(pad_heads(dot(normed_one, w_self), 3), *grad_early)
    gateup_pieces = to_seq(after(column_parts(proj_gateup, 2, n), packed))
    w_down = lax.all_gather(after(proj_down, mid_pieces), "fsdp", axis=0, tiled=True)
    q, k, v, mixed, lse = attend(packed, packed, packed, (0, pairs, 2 * pairs), pairs, ids, ids, tables)
    mixed = after(mixed, *grad_ends)
    gateup_pieces = after(gateup_pieces.reshape(n * r, 2 * hidden), mixed)
    w_gateup = lax.all_gather(gateup_pieces, "fsdp", axis=0, tiled=True)
    w_gateup = w_gateup.reshape(nf, n, r, 2 * hidden)
    if r % 16:
        w_gateup = w_gateup.transpose(1, 0, 2, 3).reshape(1, 1, D, 2 * hidden)
    mixed_in = mixed[:, :wide]
    first = inputs + scattered(lambda *at: dot(block(mixed_in, *at), w_out))[0]

    normal_two, scaled_two, normed = norm_rows(first, gain_two)
    normed_two, _, _ = gather_rows(normed.astype(bf16), n)
    cq = pad_heads(dot(normed_two, w_query).astype(bf16), 1)
    cond_rows = conditioning[0].reshape(SEQS_GRP * COND, D)
    count = SEQS_GRP * COND
    count_pad = -(-count // 16) * 16
    keyval = pad_heads(dot(cond_rows, w_keyval).astype(bf16), 2)
    keyval = jnp.pad(keyval, ((0, count_pad - count), (0, 0)))
    index = jnp.arange(count_pad, dtype=jnp.int32)
    cond_ids = jnp.where(index < count, index // COND, -1)
    cmix, clse = attend(cq, keyval, keyval, (0, 0, pairs), pairs, ids, cond_ids)
    cmix_in = cmix[:, :wide]
    second = first + scattered(lambda *at: dot(block(cmix_in, *at), w_cross))[0]

    normal_three, scaled_three, normed = norm_rows(second, gain_three)
    normed_three, _, _ = gather_rows(normed.astype(bf16), n)
    active, grad_gate, grad_upper, sum_gate, sum_upper, back_three, grad_w_down = feed(
        normed_three, group_grad, w_gateup, w_down, b_gate, b_upper
    )
    grad_rows = grad_output[0].astype(f32)
    grad_b_down = jnp.sum(grad_rows, axis=0)
    through, early = scattered(lambda *at: block(back_three, *at))
    own_down = lax.psum_scatter(grad_w_down, "fsdp", scatter_dimension=0, tiled=True)
    grad_w_gateup = gateup_grads(after(normed_three, *early), grad_gate, grad_upper, n, nf)
    through, grad_w_gateup = lax.optimization_barrier((through, grad_w_gateup))
    through, grad_gain_three = norm_back(through, normal_three, scaled_three, gain_three)
    grad_second = grad_rows + through

    group_second, early, _ = gather_rows(grad_second.astype(bf16), n)
    grad_w_gateup = after(grad_w_gateup, own_down, *early)
    own_gateup = lax.psum_scatter(grad_w_gateup, "fsdp", scatter_dimension=0, tiled=True)
    grad_cmix = pad_heads(back_prod(group_second, w_cross).astype(bf16), 1)
    dcq, dck, dcv = attend_back(
        cq, keyval, keyval, (0, 0, pairs), pairs, grad_cmix, cmix, clse, ids, cond_ids
    )
    dcq, dck, dcv = dcq[:, :wide], dck[:, :wide], dcv[:, :wide]
    cond_full = jnp.pad(cond_rows, ((0, count_pad - count), (0, 0)))
    through, _ = scattered(lambda *at: back_prod(block(dcq, *at), w_query))
    b_whole = lax.dynamic_update_slice(
        jnp.zeros((2, FF), f32), jnp.concatenate([sum_gate, sum_upper], axis=0), (0, me * hidden)
    )
    vectors = jnp.concatenate(
        [v.reshape(n, nf, r, -1) for v in (grad_gain_three, grad_b_down, b_whole)], axis=3
    )
    vectors = vectors.astype(bf16).transpose(1, 0, 2, 3).reshape(nf * n * r, -1)
    vectors = jnp.pad(vectors, ((0, 0), (0, LANES - vectors.shape[1])))
    grad_w_mid = mid_grads(cond_full, dck, dcv, normed_two, dcq, cmix_in, group_second, vectors, n, nf)
    through, grad_w_mid = lax.optimization_barrier((through, grad_w_mid))
    through, grad_gain_two = norm_back(through, normal_two, scaled_two, gain_two)
    grad_first = grad_second + through

    gains = grad_gain_two.astype(bf16).reshape(n, nf, r, 1).transpose(1, 0, 2, 3).reshape(D, 1)
    gains = jnp.pad(gains, ((0, 0), (1, LANES - 2)))
    down = dot(after(active, grad_first), w_down).astype(bf16)
    group_first, _, _ = gather_rows(grad_first.astype(bf16), n, (down,))
    group_first, gains = lax.optimization_barrier((group_first, gains))
    grad_w_mid = after(grad_w_mid, own_gateup, group_first)
    own_mid = lax.psum_scatter(grad_w_mid, "fsdp", scatter_dimension=0, tiled=True)
    own_gateup = share(after(own_gateup, group_first), n)
    grad_keyval = jnp.concatenate([dck, dcv], axis=1)[:count]
    cond_part = after(back_prod(grad_keyval, w_keyval), group_first)
    down = after(down, group_first)
    down_pieces = scatter_start(down, n)
    grad_mixed = pad_heads(back_prod(group_first, w_out).astype(bf16), 1)
    grad_mixed = after(grad_mixed, down)
    dq, dk, dv = attend_back(q, k, v, (0, 0, 0), pairs, grad_mixed, mixed, lse, ids, ids, tables)
    dq, dk, dv = dq[:, :wide], dk[:, :wide], dv[:, :wide]
    dq, own_gateup = lax.optimization_barrier((after(dq, *down_pieces), own_gateup))
    grad_w_self = self_grads(normed_one, dq, dk, dv, self_all, gains, mixed_in, group_first, n, nf)
    dq, dk, dv, grad_w_self = lax.optimization_barrier((dq, dk, dv, grad_w_self))
    own_self = lax.psum_scatter(after(grad_w_self, own_mid), "fsdp", scatter_dimension=0, tiled=True)
    grad_packed = jnp.concatenate([dq, dk, dv], axis=1)
    through, early = scattered(lambda *at: back_prod(block(grad_packed, *at), w_self))
    down_pieces = [after(piece, *early) for piece in down_pieces]
    result = second + scatter_end(down, down_pieces, n) + b_down
    cond_parts = sum_start(after(cond_part, *early), n)
    own_gateup = after(own_gateup, *early)

    def joined(pieces):
        return pieces.reshape(n, r, wide).transpose(1, 0, 2).reshape(r, D)

    split = 3 * wide + LANES
    own_cross = joined(own_mid[:, split:])
    own_out = joined(own_self[:, split:])
    last_part = share(jnp.concatenate([own_mid[:, :split], own_self[:, :split]], axis=1), n)
    grad_cond = sum_end([after(part, through) for part in cond_parts], n)
    grad_cond = grad_cond.reshape(1, SEQS_GRP, COND, D)
    vectors = jnp.sum(last_part[:, :, 3 * wide : split].astype(f32), axis=0)
    grad_inputs = grad_first + norm_back(through, normal_one, scaled_one, gain_one)[0]
    gains = jnp.sum(last_part[:, :, split + 3 * wide :].astype(f32), axis=0)

    return (
        result.astype(bf16)[None],
        grad_inputs[None],
        grad_cond,
        gains[:, 0],
        spread(last_part, D, 3, n, split),
        own_out.astype(f32),
        gains[:, 1],
        spread(last_part, D, 1, n, 2 * wide),
        spread(last_part, D, 2, n),
        own_cross.astype(f32),
        vectors[:, 0],
        spread(own_gateup, FF, 2, n),
        vectors[:, 2:10].reshape(8 * r),
        own_down.astype(f32),
        vectors[:, 1],
    )


def solution(mesh):
    rows_of = P("fsdp", "seq", None)
    matrix = P(ALL, None)
    vector = P(ALL)
    return jax.shard_map(
        shards,
        mesh=mesh,
        in_specs=(
            rows_of,
            P("fsdp", None, None, None),
            P("fsdp", None),
            rows_of,
            vector,
            matrix,
            matrix,
            vector,
            matrix,
            matrix,
            matrix,
            vector,
            matrix,
            vector,
            matrix,
            vector,
        ),
        out_specs=(
            rows_of,
            rows_of,
            P("fsdp", None, None, None),
            vector,
            matrix,
            matrix,
            vector,
            matrix,
            matrix,
            matrix,
            vector,
            matrix,
            vector,
            matrix,
            vector,
        ),
        check_vma=False,
    )
```

```python
import functools
import math

import jax
import jax.numpy as jnp
from jax import lax
from jax.experimental import pallas as pl
from jax.experimental.pallas import tpu as pltpu
from jax.sharding import PartitionSpec as P

D = 1536
HEADS = 24
HEAD = 64
FF = 6144
COND = 130
SEQS_GRP = 2
LANES = 128

epsilon = 1e-05
masked_score = -1e30
bf16 = jnp.bfloat16
f32 = jnp.float32
ALL = ("seq", "fsdp")


def seq_info(global_rows, group_lengths):
    ends = jnp.cumsum(group_lengths)
    starts = ends - group_lengths
    ident = jnp.sum((global_rows[:, None] >= ends[None, :]).astype(jnp.int32), axis=1)
    onehot = ident[:, None] == jnp.arange(group_lengths.shape[0], dtype=jnp.int32)[None, :]
    begin = jnp.sum(jnp.where(onehot, starts[None, :], 0), axis=1)
    return (ident, (global_rows - begin).astype(f32))


def angle_tables(positions):
    half = HEAD // 2
    inverse = jnp.power(10000.0, -jnp.arange(half, dtype=f32) / half)
    turned = positions[:, None] * inverse[None, :]
    cosine, sine = jnp.cos(turned), jnp.sin(turned)
    reps = LANES // HEAD
    return (
        jnp.concatenate([cosine, cosine] * reps, axis=1),
        jnp.concatenate([-sine, sine] * reps, axis=1),
    )


def norm_rows(values, gain):
    centre = values - jnp.mean(values, axis=-1, keepdims=True)
    spread = jnp.mean(centre * centre, axis=-1, keepdims=True)
    scaled = lax.rsqrt(spread + epsilon)
    normal = centre * scaled
    return (normal, scaled, normal * gain)


def norm_back(grad_rows, normal, scaled, gain):
    weighted = grad_rows * gain
    mean_one = jnp.mean(weighted, axis=-1, keepdims=True)
    mean_two = jnp.mean(weighted * normal, axis=-1, keepdims=True)
    return (scaled * (weighted - mean_one - normal * mean_two), jnp.sum(grad_rows * normal, axis=0))


def dot(left, right):
    return jnp.dot(left, right, preferred_element_type=f32)


def outer_sum(left, right):
    return lax.dot_general(left, right, (((0,), (0,)), ((), ())), preferred_element_type=f32)


def back_prod(left, weight):
    return lax.dot_general(left, weight, (((1,), (1,)), ((), ())), preferred_element_type=f32)


def after(value, *others):
    if not others:
        return value
    return lax.optimization_barrier((value,) + others)[0]


def hop(value, j):
    return lax.ppermute(value, "seq", [(i, i ^ j) for i in range(4)])


def block_ids(n):
    if n == 4:
        return lax.axis_index("seq") ^ jnp.arange(n, dtype=jnp.int32)
    return jnp.arange(n, dtype=jnp.int32)


def gather_rows(value, n, gates=()):
    if n != 4:
        whole = lax.all_gather(value, "seq", axis=0, tiled=True)
        return whole, (whole,), (whole,)
    half = value.shape[0] // 2
    first, second = hop(value, 1), hop(value, 2)
    first, second = after(first, *gates), after(second, *gates)
    third, fourth = hop(second[:half], 1), hop(first[half:], 2)
    whole = jnp.concatenate([value, first, second, third, fourth], axis=0)
    return whole, (first, second), (third, fourth)


def scatter_rows(blocks, rows, n, gates=()):
    if n != 4:
        whole = jnp.concatenate([blocks(j, 0, rows) for j in range(n)], axis=0).astype(bf16)
        out = lax.psum_scatter(whole, "seq", scatter_dimension=0, tiled=True).astype(f32)
        return out, (out,)
    half = rows // 2
    to_first = hop(blocks(3, 0, half).astype(bf16), 1)
    to_second = hop(blocks(3, half, rows).astype(bf16), 2)
    to_first, to_second = after(to_first, *gates), after(to_second, *gates)
    one, two = blocks(1, 0, rows).astype(f32), blocks(2, 0, rows).astype(f32)
    one = jnp.concatenate([one[:half], one[half:] + to_second.astype(f32)], axis=0)
    two = jnp.concatenate([two[:half] + to_first.astype(f32), two[half:]], axis=0)
    one, two = hop(one.astype(bf16), 1), hop(two.astype(bf16), 2)
    own = blocks(0, 0, rows).astype(f32)
    return own + one.astype(f32) + two.astype(f32), (to_first, to_second)


def scatter_start(partial, n):
    if n != 4:
        return (lax.psum_scatter(partial, "seq", scatter_dimension=0, tiled=True),)
    half = partial.shape[0] // 8
    return (
        hop(partial[6 * half : 7 * half], 1),
        hop(partial[7 * half :], 2),
        hop(partial[2 * half : 3 * half], 1),
        hop(partial[5 * half : 6 * half], 2),
    )


def scatter_end(partial, pieces, n):
    if n != 4:
        return pieces[0].astype(f32)
    half = partial.shape[0] // 8
    to_first, to_second, one, two = (piece.astype(f32) for piece in pieces)
    sum_one = hop((partial[3 * half : 4 * half].astype(f32) + to_second).astype(bf16), 1)
    sum_two = hop((partial[4 * half : 5 * half].astype(f32) + to_first).astype(bf16), 2)
    others = jnp.concatenate([one + sum_two.astype(f32), sum_one.astype(f32) + two], axis=0)
    return partial[: 2 * half].astype(f32) + others


def swap_halves(value):
    lane = lax.broadcasted_iota(jnp.int32, value.shape, 1)
    half = HEAD // 2
    return jnp.where(
        lane % HEAD < half, pltpu.roll(value, LANES - half, 1), pltpu.roll(value, half, 1)
    )


def head_rows(h):
    return slice(h * HEAD, (h + 1) * HEAD)


def lane_mask(value, h):
    lane = lax.broadcasted_iota(jnp.int32, value.shape, 1)
    return jnp.where(lane // HEAD == h, value, jnp.zeros_like(value))


FAR = 1e30


def pieces_of(value):
    high = value.astype(bf16).astype(f32)
    rest = value - high
    middle = rest.astype(bf16).astype(f32)
    return high, middle, rest - middle


def key_lanes(keys, kid, h):
    lane = lax.broadcasted_iota(jnp.int32, keys.shape, 1)
    spare = lane % HEAD
    ones = jnp.where(spare <= SEQS_GRP + 3, 1.0, 0.0)
    padding = jnp.where(spare == SEQS_GRP, jnp.where(kid < 0, 1.0, 0.0), ones)
    extra = jnp.where(spare < SEQS_GRP, jnp.where(kid == spare, 1.0, 0.0), padding)
    return jnp.where(lane // HEAD == h, keys.astype(f32), extra).astype(bf16)


def query_rows(turned, qid, h, offsets=()):
    row = lax.broadcasted_iota(jnp.int32, turned.shape, 0)
    spare = row % HEAD
    extra = jnp.where(spare <= SEQS_GRP, jnp.where(qid == spare, 0.0, -FAR), 0.0)
    for j, offset in enumerate(offsets):
        extra = jnp.where(spare == SEQS_GRP + 1 + j, offset, extra)
    return jnp.where(row // HEAD == h, turned, extra).astype(bf16)


def value_lanes(values, h):
    lane = lax.broadcasted_iota(jnp.int32, values.shape, 1)
    ones = jnp.where(lane % HEAD < 3, 1.0, 0.0)
    return jnp.where(lane // HEAD == h, values.astype(f32), ones).astype(bf16)


def grad_rows_of(turned, h, offsets):
    row = lax.broadcasted_iota(jnp.int32, turned.shape, 0)
    extra = jnp.zeros_like(turned)
    for j, offset in enumerate(offsets):
        extra = jnp.where(row % HEAD == j, offset, extra)
    return jnp.where(row // HEAD == h, turned, extra).astype(bf16)


PAIR = LANES // HEAD


def attend_kernel(rope, tile, *refs):
    if rope:
        q_ref, k_ref, v_ref, cos_ref, sin_ref, qid_ref, kid_ref = refs[:7]
        qo_ref, ko_ref, vo_ref, o_ref, lse_ref, qt, kb, vt, ot = refs[7:]
        q, k = q_ref[...], k_ref[...]
        q = (q * cos_ref[...] + swap_halves(q) * sin_ref[...]).astype(bf16)
        k = (k * cos_ref[...] + swap_halves(k) * sin_ref[...]).astype(bf16)
        v = v_ref[...].astype(bf16)
        qo_ref[...] = q
        ko_ref[...] = k
        vo_ref[...] = v
    else:
        q_ref, k_ref, v_ref, qid_ref, kid_ref, o_ref, lse_ref, qt, kb, vt, ot = refs
        q, k, v = q_ref[...], k_ref[...], v_ref[...]
    turned = q.astype(f32).T * 0.125
    for h in range(PAIR):
        qt[h] = query_rows(turned, qid_ref[...], h)
        kb[h] = key_lanes(k, kid_ref[...], h)
    vt[...] = v.astype(f32).T.astype(bf16)
    units = [(t * tile, h) for t in range(ot.shape[1] // tile) for h in range(PAIR)]

    def scores(unit):
        start, h = unit
        return dot(kb[h], qt[h, :, start : start + tile])

    later = scores(units[0])
    for i, (start, h) in enumerate(units):
        s = later
        if i + 1 < len(units):
            later = scores(units[i + 1])
        at = slice(start, start + tile)
        top = jnp.max(s, axis=0, keepdims=True)
        e = jnp.exp(s - top)
        total = jnp.sum(e, axis=0, keepdims=True)
        ot[head_rows(h), at] = dot(vt[head_rows(h), :], e.astype(bf16)) * (1.0 / total)
        lse_ref[0, h : h + 1, at] = top + jnp.log(total)
    o_ref[...] = ot[...].T.astype(bf16)


def attend_back_kernel(rope, tile, *refs):
    if rope:
        q_ref, k_ref, v_ref, do_ref, o_ref, lse_ref, cos_ref, sin_ref, qid_ref, kid_ref = refs[:10]
        dq_ref, dk_ref, dv_ref, qt, gt, kb, vb, kt, dqt, dk_acc, dv_acc = refs[10:]
    else:
        q_ref, k_ref, v_ref, do_ref, o_ref, lse_ref, qid_ref, kid_ref = refs[:8]
        dq_ref, dk_ref, dv_ref, qt, gt, kb, vb, kt, dqt, dk_acc, dv_acc = refs[8:]
    turned = q_ref[...].astype(f32).T * 0.125
    grads = do_ref[...].astype(f32).T
    product = grads * o_ref[...].astype(f32).T
    kt[...] = k_ref[...].astype(f32).T.astype(bf16)
    for h in range(PAIR):
        delta = jnp.sum(product[head_rows(h), :], axis=0, keepdims=True)
        qt[h] = query_rows(turned, qid_ref[...], h, pieces_of(-lse_ref[0, h : h + 1, :]))
        gt[h] = grad_rows_of(grads, h, pieces_of(-delta))
        kb[h] = key_lanes(k_ref[...], kid_ref[...], h)
        vb[h] = value_lanes(v_ref[...], h)
    tiles = dqt.shape[1] // tile
    units = [(t * tile, h) for t in range(tiles) for h in range(PAIR)]

    def products(unit):
        start, h = unit
        at = slice(start, start + tile)
        return dot(kb[h], qt[h, :, at]), dot(vb[h], gt[h, :, at])

    later = products(units[0])
    low_p, low_ds = [], []
    for i, (start, h) in enumerate(units):
        s, dp = later
        if i + 1 < len(units):
            later = products(units[i + 1])
        at = slice(start, start + tile)
        p = jnp.exp(s)
        ds = (p * dp).astype(bf16)
        dqt[head_rows(h), at] = dot(kt[head_rows(h), :], ds)
        low_p.append(p.astype(bf16))
        low_ds.append(ds)
        if h == PAIR - 1:
            rows_do = jnp.concatenate([lane_mask(do_ref[at, :], j) for j in range(PAIR)], axis=0)
            rows_q = jnp.concatenate([lane_mask(q_ref[at, :], j) for j in range(PAIR)], axis=0)
            dv = dot(jnp.concatenate(low_p, axis=1), rows_do)
            dk = dot(jnp.concatenate(low_ds, axis=1), rows_q)
            dv_acc[...] = dv if start == 0 else dv_acc[...] + dv
            dk_acc[...] = dk if start == 0 else dk_acc[...] + dk
            low_p, low_ds = [], []
    dq = dqt[...].T * 0.125
    dk = dk_acc[...] * 0.125
    if rope:
        dq = dq * cos_ref[...] - swap_halves(dq) * sin_ref[...]
        dk = dk * cos_ref[...] - swap_halves(dk) * sin_ref[...]
    dq_ref[...] = dq.astype(bf16)
    dk_ref[...] = dk.astype(bf16)
    dv_ref[...] = dv_acc[...].astype(bf16)


def query_tile(rows):
    for tile in (256, 128):
        if rows % tile == 0:
            return tile
    return rows


def spec(rows, offset=0):
    return pl.BlockSpec((rows, LANES), lambda i: (0, i + offset))


def whole(shape):
    return pl.BlockSpec(shape, lambda i: (0,) * len(shape), pipeline_mode=pl.Buffered(1))


LIMIT = 56 * 1024 * 1024
TILE, CHUNK, GTILE = 256, 320, 512


def attend(q, k, v, offsets, pairs, qid, kid, tables=None):
    nq, nk = q.shape[0], k.shape[0]
    rope = tables is not None
    tile = query_tile(nq)
    ins = [spec(nq, offsets[0]), spec(nk, offsets[1]), spec(nk, offsets[2])]
    args = [q, k, v]
    outs, shapes = [], []
    if rope:
        ins += [whole((nq, LANES)), whole((nq, LANES))]
        args += list(tables)
        outs += [spec(nq), spec(nk), spec(nk)]
        shapes += [jax.ShapeDtypeStruct((rows, pairs * LANES), bf16) for rows in (nq, nk, nk)]
    ins += [whole((1, nq)), whole((nk, 1))]
    args += [qid[None, :], kid[:, None]]
    outs += [spec(nq), pl.BlockSpec((1, 8, nq), lambda i: (i, 0, 0))]
    shapes += [
        jax.ShapeDtypeStruct((nq, pairs * LANES), bf16),
        jax.ShapeDtypeStruct((pairs, 8, nq), f32),
    ]
    return pl.pallas_call(
        functools.partial(attend_kernel, rope, tile),
        out_shape=shapes,
        grid=(pairs,),
        in_specs=ins,
        out_specs=outs,
        scratch_shapes=[
            pltpu.VMEM((PAIR, LANES, nq), bf16),
            pltpu.VMEM((PAIR, nk, LANES), bf16),
            pltpu.VMEM((LANES, nk), bf16),
            pltpu.VMEM((LANES, nq), f32),
        ],
        compiler_params=pltpu.CompilerParams(vmem_limit_bytes=LIMIT),
        cost_estimate=pl.CostEstimate(
            flops=2 * 2 * 2 * pairs * nq * nk * LANES,
            bytes_accessed=pairs * LANES * (nq + nk) * 12,
            transcendentals=2 * pairs * nq * nk,
        ),
        name="attend_self" if rope else "attend_cross",
    )(*args)


def attend_back(q, k, v, offsets, pairs, grad, mixed, lse, qid, kid, tables=None):
    nq, nk = q.shape[0], k.shape[0]
    rope = tables is not None
    tile = query_tile(nq)
    ins = [spec(nq, offsets[0]), spec(nk, offsets[1]), spec(nk, offsets[2]), spec(nq), spec(nq)]
    args = [q, k, v, grad, mixed]
    ins += [pl.BlockSpec((1, 8, nq), lambda i: (i, 0, 0))]
    args += [lse]
    if rope:
        ins += [whole((nq, LANES)), whole((nq, LANES))]
        args += list(tables)
    ins += [whole((1, nq)), whole((nk, 1))]
    args += [qid[None, :], kid[:, None]]
    return pl.pallas_call(
        functools.partial(attend_back_kernel, rope, tile),
        out_shape=[jax.ShapeDtypeStruct((rows, pairs * LANES), bf16) for rows in (nq, nk, nk)],
        grid=(pairs,),
        in_specs=ins,
        out_specs=[spec(nq), spec(nk), spec(nk)],
        scratch_shapes=[
            pltpu.VMEM((PAIR, LANES, nq), bf16),
            pltpu.VMEM((PAIR, LANES, nq), bf16),
            pltpu.VMEM((PAIR, nk, LANES), bf16),
            pltpu.VMEM((PAIR, nk, LANES), bf16),
            pltpu.VMEM((LANES, nk), bf16),
            pltpu.VMEM((LANES, nq), f32),
            pltpu.VMEM((nk, LANES), f32),
            pltpu.VMEM((nk, LANES), f32),
        ],
        compiler_params=pltpu.CompilerParams(vmem_limit_bytes=LIMIT),
        cost_estimate=pl.CostEstimate(
            flops=2 * 5 * 2 * pairs * nq * nk * LANES,
            bytes_accessed=pairs * LANES * (nq + nk) * 12,
            transcendentals=2 * pairs * nq * nk,
        ),
        name="back_self" if rope else "back_cross",
    )(*args)


def contract(left, right, dims):
    return lax.dot_general(left, right, (dims, ((), ())), preferred_element_type=f32)


def feed_kernel(chunk, *refs):
    h_ref, gy_ref, wg_ref, wu_ref, wd_ref, bg_ref, bu_ref = refs[:7]
    act_ref, dg_ref, du_ref, sg_ref, su_ref, dh_ref, dw_ref, both, total = refs[7:]
    step = pl.program_id(0)
    span = wg_ref.shape[0] * wg_ref.shape[2]
    tile = wg_ref.shape[3]
    for j in range(wg_ref.shape[1]):
        at = slice(j * span, (j + 1) * span)
        both[at, :tile] = wg_ref[:, j].reshape(span, tile)
        both[at, tile:] = wu_ref[:, j].reshape(span, tile)
    sg_ref[...] = jnp.zeros_like(sg_ref)
    su_ref[...] = jnp.zeros_like(su_ref)

    @pl.when(step == 0)
    def _():
        total[...] = jnp.zeros_like(total)

    def rows_at(i):
        return slice(i * chunk, (i + 1) * chunk)

    def products(i):
        at = rows_at(i)
        return dot(h_ref[at, :], both[...]), contract(gy_ref[at, :], wd_ref[...], ((1,), (1,)))

    def finish(i, pair, grad):
        at = rows_at(i)
        gate = pair[:, :tile] + bg_ref[...]
        upper = pair[:, tile:] + bu_ref[...]
        sigma = jax.nn.sigmoid(gate)
        silu = gate * sigma
        act_ref[at, :] = (silu * upper).astype(bf16)
        dg = (grad * upper * sigma * (1.0 + gate * (1.0 - sigma))).astype(bf16)
        du = (grad * silu).astype(bf16)
        dg_ref[at, :] = dg
        du_ref[at, :] = du
        sg_ref[...] += jnp.sum(dg.astype(f32), axis=0, keepdims=True)
        su_ref[...] += jnp.sum(du.astype(f32), axis=0, keepdims=True)
        return jnp.concatenate([dg, du], axis=1)

    chunks = h_ref.shape[0] // chunk
    now = products(0)
    for i in range(chunks):
        later = products(i + 1) if i + 1 < chunks else None
        grads = finish(i, *now)
        total[rows_at(i), :] += contract(grads, both[...], ((1,), (1,)))
        now = later
    dw_ref[...] = dot(act_ref[...].T, gy_ref[...]).astype(bf16)

    @pl.when(step == pl.num_programs(0) - 1)
    def _():
        dh_ref[...] = total[...].astype(bf16)


def feed(h, gy, w_gateup, w_down, b_gate, b_upper):
    rows = h.shape[0]
    hidden = w_down.shape[0]
    tile = TILE if rows <= 1280 else 128
    steps = hidden // tile
    lead = w_gateup.shape[:3]
    chunk = CHUNK if rows % CHUNK == 0 else rows
    one = pl.Buffered(1)
    rows_all = pl.BlockSpec((rows, D), lambda t: (0, 0), pipeline_mode=one)
    columns = pl.BlockSpec((rows, tile), lambda t: (0, t))
    vector = pl.BlockSpec((1, tile), lambda t: (0, t))
    return pl.pallas_call(
        functools.partial(feed_kernel, chunk),
        out_shape=[jax.ShapeDtypeStruct((rows, hidden), bf16)] * 3
        + [jax.ShapeDtypeStruct((1, hidden), f32)] * 2
        + [jax.ShapeDtypeStruct((rows, D), bf16), jax.ShapeDtypeStruct((hidden, D), bf16)],
        grid=(steps,),
        in_specs=[
            rows_all,
            rows_all,
            pl.BlockSpec(lead + (tile,), lambda t: (0, 0, 0, t)),
            pl.BlockSpec(lead + (tile,), lambda t: (0, 0, 0, t + steps)),
            pl.BlockSpec((tile, D), lambda t: (t, 0)),
            vector,
            vector,
        ],
        out_specs=[columns, columns, columns, vector, vector, rows_all, pl.BlockSpec((tile, D), lambda t: (t, 0))],
        scratch_shapes=[
            pltpu.VMEM((D, 2 * tile), bf16),
            pltpu.VMEM((rows, D), f32),
        ],
        compiler_params=pltpu.CompilerParams(vmem_limit_bytes=LIMIT),
        cost_estimate=pl.CostEstimate(
            flops=2 * 6 * rows * D * hidden,
            bytes_accessed=2 * (3 * rows * D + 3 * rows * hidden + 4 * D * hidden),
            transcendentals=rows * hidden,
        ),
        name="feed",
    )(h, gy, w_gateup, w_gateup, w_down, b_gate[None], b_upper[None])


def place_rows(out_ref, start, value):
    nf, _, r, _ = out_ref.shape
    width = value.shape[1]
    out_ref[:, 0, :, start : start + width] = value.astype(bf16).reshape(nf, r, width)


def gateup_kernel(h_ref, dg_ref, du_ref, out_ref, turned):
    step = pl.program_id(0)
    half = pl.num_programs(0) // 2
    nf, n, r, tile = out_ref.shape
    wide = nf * r

    @pl.when(step == 0)
    def _():
        for s in range(n):
            at = slice(s * wide, (s + 1) * wide)
            turned[at, :] = h_ref[:, at].T

    def fill(grad):
        for s in range(n):
            value = dot(turned[s * wide : (s + 1) * wide, :], grad)
            out_ref[:, s] = value.astype(bf16).reshape(nf, r, tile)

    @pl.when(step < half)
    def _():
        fill(dg_ref[...])

    @pl.when(step >= half)
    def _():
        fill(du_ref[...])


def gateup_grads(h, dg, du, n, nf):
    rows, hidden = dg.shape
    r, wide = D // (n * nf), D // n
    if r % 16 or wide % LANES:
        joined = jnp.concatenate([dg, du], axis=1)
        return columns_by_owner(outer_sum(h, joined), n, nf)
    tile = GTILE
    half = hidden // tile
    out = pl.pallas_call(
        gateup_kernel,
        out_shape=jax.ShapeDtypeStruct((nf, n, r, 2 * hidden), bf16),
        grid=(2 * half,),
        in_specs=[
            pl.BlockSpec((rows, D), lambda t: (0, 0), pipeline_mode=pl.Buffered(1)),
            pl.BlockSpec((rows, tile), lambda t: (0, jnp.minimum(t, half - 1))),
            pl.BlockSpec((rows, tile), lambda t: (0, jnp.maximum(t - half, 0))),
        ],
        out_specs=pl.BlockSpec((nf, n, r, tile), lambda t: (0, 0, 0, t)),
        scratch_shapes=[pltpu.VMEM((D, rows), bf16)],
        compiler_params=pltpu.CompilerParams(vmem_limit_bytes=LIMIT),
        cost_estimate=pl.CostEstimate(
            flops=4 * rows * D * hidden, bytes_accessed=4 * D * hidden + 6 * rows * hidden, transcendentals=0
        ),
        name="gateup_grads",
    )(h, dg, du)
    return out.reshape(D, 2 * hidden)


def mid_kernel(cond_ref, dk_ref, dv_ref, h_ref, dq_ref, mix_ref, gy_ref, vec_ref, out_ref):
    wide = dq_ref.shape[1]
    outer = ((0,), (0,))
    turned = cond_ref[...].T
    place_rows(out_ref, 0, dot(turned, dk_ref[...]))
    place_rows(out_ref, wide, dot(turned, dv_ref[...]))
    place_rows(out_ref, 2 * wide, contract(h_ref[...], dq_ref[...], outer))
    out_ref[:, 0, :, 3 * wide : 3 * wide + LANES] = vec_ref[:, 0]
    place_rows(out_ref, 3 * wide + LANES, contract(mix_ref[...], gy_ref[...], outer))


def mid_grads(cond, dk, dv, h, dq, mix, gy, vectors, n, nf):
    rows, wide = dq.shape
    r = D // (n * nf)
    if r % 16 or wide % LANES:
        return jnp.concatenate(
            [
                columns_by_owner(outer_sum(cond, jnp.concatenate([dk, dv], axis=1)), n, nf),
                columns_by_owner(outer_sum(h, dq), n, nf),
                vectors,
                rows_by_owner(outer_sum(mix, gy).astype(bf16), n, nf),
            ],
            axis=1,
        )
    count = cond.shape[0]
    columns = 4 * wide + LANES

    def full(value):
        return pl.BlockSpec(value.shape, lambda s: (0, 0), pipeline_mode=pl.Buffered(1))

    out = pl.pallas_call(
        mid_kernel,
        out_shape=jax.ShapeDtypeStruct((nf, n, r, columns), bf16),
        grid=(n,),
        in_specs=[
            pl.BlockSpec((count, wide), lambda s: (0, s)),
            full(dk),
            full(dv),
            pl.BlockSpec((rows, wide), lambda s: (0, s)),
            full(dq),
            full(mix),
            pl.BlockSpec((rows, wide), lambda s: (0, s)),
            pl.BlockSpec((nf, 1, r, LANES), lambda s: (0, s, 0, 0)),
        ],
        out_specs=pl.BlockSpec((nf, 1, r, columns), lambda s: (0, s, 0, 0)),
        compiler_params=pltpu.CompilerParams(vmem_limit_bytes=LIMIT),
        cost_estimate=pl.CostEstimate(
            flops=2 * D * wide * (2 * count + 2 * rows),
            bytes_accessed=2 * D * (columns + 2 * rows + count),
            transcendentals=0,
        ),
        name="mid_grads",
    )(cond, dk, dv, h, dq, mix, gy, vectors.reshape(nf, n, r, LANES))
    return out.reshape(D, columns)


def self_kernel(h_ref, dq_ref, dk_ref, dv_ref, w_ref, gain_ref, vec_ref, mix_ref, gy_ref, out_ref):
    wide = dq_ref.shape[1]
    nf, _, r, _ = out_ref.shape
    turned = h_ref[...].T
    along = jnp.zeros((wide, 1), f32)
    for j, ref in enumerate((dq_ref, dk_ref, dv_ref)):
        grad = dot(turned, ref[...])
        place_rows(out_ref, j * wide, grad)
        weight = w_ref[:, j * wide : (j + 1) * wide].astype(f32)
        along = along + jnp.sum(grad * weight, axis=1, keepdims=True)
    along = jnp.broadcast_to(along / gain_ref[:, 0:1].astype(f32), (wide, LANES)).reshape(nf, r, LANES)
    lane = lax.broadcasted_iota(jnp.int32, along.shape, 2)
    vec = jnp.where(lane == 0, along, vec_ref[:, 0].astype(f32))
    out_ref[:, 0, :, 3 * wide : 3 * wide + LANES] = vec.astype(bf16)
    place_rows(out_ref, 3 * wide + LANES, contract(mix_ref[...], gy_ref[...], ((0,), (0,))))


def self_grads(h, dq, dk, dv, w_all, vectors, mix, gy, n, nf):
    rows, wide = dq.shape
    r = D // (n * nf)
    if r % 16 or wide % LANES:
        grad = outer_sum(h, jnp.concatenate([dq, dk, dv], axis=1))
        along = jnp.sum(grad * w_all[:, : 3 * wide].astype(f32), axis=1)
        along = (along / w_all[:, 3 * wide].astype(f32)).astype(bf16)
        along = along.reshape(n, nf, r, 1).transpose(1, 0, 2, 3).reshape(D, 1)
        grad_out = rows_by_owner(outer_sum(mix, gy).astype(bf16), n, nf)
        return jnp.concatenate([columns_by_owner(grad, n, nf), along, vectors[:, 1:], grad_out], axis=1)
    columns = 4 * wide + LANES

    def full(value):
        return pl.BlockSpec(value.shape, lambda s: (0, 0), pipeline_mode=pl.Buffered(1))

    out = pl.pallas_call(
        self_kernel,
        out_shape=jax.ShapeDtypeStruct((nf, n, r, columns), bf16),
        grid=(n,),
        in_specs=[
            pl.BlockSpec((rows, wide), lambda s: (0, s)),
            full(dq),
            full(dk),
            full(dv),
            pl.BlockSpec((wide, 3 * wide), lambda s: (s, 0)),
            pl.BlockSpec((wide, LANES), lambda s: (s, 3 * wide // LANES)),
            pl.BlockSpec((nf, 1, r, LANES), lambda s: (0, s, 0, 0)),
            full(mix),
            pl.BlockSpec((rows, wide), lambda s: (0, s)),
        ],
        out_specs=pl.BlockSpec((nf, 1, r, columns), lambda s: (0, s, 0, 0)),
        compiler_params=pltpu.CompilerParams(vmem_limit_bytes=LIMIT),
        cost_estimate=pl.CostEstimate(
            flops=8 * D * wide * rows, bytes_accessed=2 * D * (columns + rows + 3 * wide), transcendentals=0
        ),
        name="self_grads",
    )(h, dq, dk, dv, w_all, w_all, vectors.reshape(nf, n, r, LANES), mix, gy)
    return out.reshape(D, columns)


def column_parts(shard, parts, n):
    r, columns = shard.shape
    c = columns // (parts * n)
    return shard.reshape(r, parts, n, c).transpose(2, 0, 1, 3).reshape(n, r, parts * c)


def natural_columns(pieces, parts, n):
    r, columns = pieces.shape[1:]
    c = columns // parts
    return pieces.reshape(n, r, parts, c).transpose(1, 2, 0, 3).reshape(r, parts * n * c)


def spread_kernel(in_ref, out_ref):
    c = in_ref.shape[2]
    for s in range(in_ref.shape[0]):
        out_ref[:, s * c : (s + 1) * c] = in_ref[s].astype(f32)


def spread(pieces, width, parts, n, start=0):
    r = pieces.shape[1]
    c = width // n
    if r % 16 or c % LANES:
        return natural_columns(pieces[:, :, start : start + parts * c], parts, n).astype(f32)
    step = math.gcd(c, start) if start else c
    if step < c:
        pieces, start = pieces[:, :, start : start + parts * c], 0
    first = start // c
    return pl.pallas_call(
        spread_kernel,
        out_shape=jax.ShapeDtypeStruct((r, parts * n * c), f32),
        grid=(parts,),
        in_specs=[pl.BlockSpec((n, r, c), lambda p: (0, 0, first + p))],
        out_specs=pl.BlockSpec((r, n * c), lambda p: (0, p)),
        name="spread",
    )(pieces)


def to_seq(pieces):
    return lax.all_to_all(pieces, "seq", 0, 0, tiled=True)


def gather_columns(pieces, n, nf):
    r, c = pieces.shape[1:]
    gathered = lax.all_gather(pieces.reshape(n * r, c), "fsdp", axis=0, tiled=True)
    return gathered.reshape(nf, n, r, c).transpose(1, 0, 2, 3).reshape(n * nf * r, c)


def columns_by_owner(grad, n, nf):
    rows, c = grad.shape
    r = rows // (n * nf)
    return grad.astype(bf16).reshape(n, nf, r, c).transpose(1, 0, 2, 3).reshape(rows, c)


def rows_by_owner(grad, n, nf):
    rows, columns = grad.shape
    r = rows // nf
    return grad.reshape(nf, r, n, columns // n).transpose(0, 2, 1, 3).reshape(nf * n * r, columns // n)


def share(rows_of_fsdp, n):
    rows, c = rows_of_fsdp.shape
    return to_seq(rows_of_fsdp.reshape(n, rows // n, c))


def rows_to_pieces(shard, n):
    r, columns = shard.shape
    return shard.reshape(r, n, columns // n).transpose(1, 0, 2).reshape(n * r, columns // n)


def pair_sum(part, j):
    low = part.astype(bf16)
    return low.astype(f32) + hop(low, j).astype(f32)


def sum_start(value, n):
    if n != 4:
        return (lax.psum(value, "seq"),)
    half = value.shape[1] // 2
    return pair_sum(value[:, :half], 1), pair_sum(value[:, half:], 2)


def sum_end(parts, n):
    if n != 4:
        return parts[0]
    return jnp.concatenate([pair_sum(parts[0], 2), pair_sum(parts[1], 1)], axis=1)


def pad_heads(value, parts):
    rows, columns = value.shape
    c = columns // parts
    if c % LANES == 0:
        return value
    padded = -(-c // LANES) * LANES
    return jnp.pad(value.reshape(rows, parts, c), ((0, 0), (0, 0), (0, padded - c))).reshape(
        rows, parts * padded
    )


def shards(
    tokens,
    conditioning,
    lengths,
    grad_output,
    norm_first,
    proj_self,
    out_self,
    norm_second,
    proj_query,
    proj_keyval,
    out_cross,
    norm_third,
    proj_gateup,
    bias_gateup,
    proj_down,
    bias_down,
):
    rows = tokens.shape[1]
    n = lax.axis_size("seq")
    nf = lax.axis_size("fsdp")
    me = lax.axis_index("seq")
    group = rows * n
    wide = D // n
    pairs = -(-wide // LANES)
    hidden = FF // n
    r = norm_first.shape[0]

    small = jnp.concatenate(
        [v.reshape(r, -1) for v in (norm_first, norm_second, norm_third, bias_down, bias_gateup)],
        axis=1,
    )
    small = jnp.pad(small, ((0, 0), (0, LANES - small.shape[1])))
    self_in = jnp.concatenate(
        [column_parts(proj_self, 3, n), jnp.broadcast_to(small[None], (n, r, LANES))], axis=2
    )
    self_pieces = to_seq(self_in)
    mid_pieces = to_seq(
        after(
            jnp.concatenate([column_parts(proj_keyval, 2, n), column_parts(proj_query, 1, n)], axis=2),
            self_pieces,
        )
    )
    group_tokens, _, ends = gather_rows(after(tokens[0], self_pieces), n)
    group_grad, grad_early, grad_ends = gather_rows(after(grad_output[0], *ends), n)

    first_in = jnp.concatenate([self_pieces.reshape(n * r, -1), rows_to_pieces(out_self, n)], axis=1)
    first_all = lax.all_gather(first_in, "fsdp", axis=0, tiled=True).reshape(nf, n, r, 4 * wide + LANES)
    self_all = first_all[..., : 3 * wide + LANES].transpose(1, 0, 2, 3).reshape(D, 3 * wide + LANES)
    w_out = first_all[..., 3 * wide + LANES :].transpose(0, 2, 1, 3).reshape(nf * r, D)
    w_self = self_all[:, : 3 * wide]
    vectors = self_all[:, 3 * wide : 3 * wide + 12]
    gain_one, gain_two, gain_three, b_down = (vectors[:, j].astype(f32) for j in range(4))
    b_gateup = vectors[:, 4:12].reshape(2 * FF).astype(f32)
    b_gate = lax.dynamic_slice_in_dim(b_gateup, me * hidden, hidden, 0)
    b_upper = lax.dynamic_slice_in_dim(b_gateup, FF + me * hidden, hidden, 0)
    mid = jnp.concatenate([mid_pieces.reshape(n * r, 3 * wide), rows_to_pieces(out_cross, n)], axis=1)
    mid = lax.all_gather(mid, "fsdp", axis=0, tiled=True).reshape(nf, n, r, 4 * wide)
    kvq = mid[..., : 3 * wide].transpose(1, 0, 2, 3).reshape(D, 3 * wide)
    w_keyval, w_query = kvq[:, : 2 * wide], kvq[:, 2 * wide :]
    w_cross = mid[..., 3 * wide :].transpose(0, 2, 1, 3).reshape(nf * r, D)
    group_lengths = lengths[0]
    order = block_ids(n)
    all_rows = (order[:, None] * rows + jnp.arange(rows, dtype=jnp.int32)[None, :]).reshape(group)
    ids, positions = seq_info(all_rows, group_lengths)
    tables = angle_tables(positions)

    def block(value, j, low, high):
        return lax.slice_in_dim(value, j * rows + low, j * rows + high, axis=0)

    def scattered(rows_of):
        return scatter_rows(rows_of, rows, n)

    inputs = tokens[0].astype(f32)
    normal_one, scaled_one, _ = norm_rows(inputs, gain_one)
    group_tokens, *tables = lax.optimization_barrier((group_tokens, *tables))
    normed_one = norm_rows(group_tokens.astype(f32), gain_one)[2].astype(bf16)
    packed = after(pad_heads(dot(normed_one, w_self), 3), *grad_early)
    gateup_pieces = to_seq(after(column_parts(proj_gateup, 2, n), packed))
    w_down = lax.all_gather(after(proj_down, mid_pieces), "fsdp", axis=0, tiled=True)
    q, k, v, mixed, lse = attend(packed, packed, packed, (0, pairs, 2 * pairs), pairs, ids, ids, tables)
    mixed = after(mixed, *grad_ends)
    gateup_pieces = after(gateup_pieces.reshape(n * r, 2 * hidden), mixed)
    w_gateup = lax.all_gather(gateup_pieces, "fsdp", axis=0, tiled=True)
    w_gateup = w_gateup.reshape(nf, n, r, 2 * hidden)
    if r % 16:
        w_gateup = w_gateup.transpose(1, 0, 2, 3).reshape(1, 1, D, 2 * hidden)
    mixed_in = mixed[:, :wide]
    first = inputs + scattered(lambda *at: dot(block(mixed_in, *at), w_out))[0]

    normal_two, scaled_two, normed = norm_rows(first, gain_two)
    normed_two, _, _ = gather_rows(normed.astype(bf16), n)
    cq = pad_heads(dot(normed_two, w_query).astype(bf16), 1)
    cond_rows = conditioning[0].reshape(SEQS_GRP * COND, D)
    count = SEQS_GRP * COND
    count_pad = -(-count // 16) * 16
    keyval = pad_heads(dot(cond_rows, w_keyval).astype(bf16), 2)
    keyval = jnp.pad(keyval, ((0, count_pad - count), (0, 0)))
    index = jnp.arange(count_pad, dtype=jnp.int32)
    cond_ids = jnp.where(index < count, index // COND, -1)
    cmix, clse = attend(cq, keyval, keyval, (0, 0, pairs), pairs, ids, cond_ids)
    cmix_in = cmix[:, :wide]
    second = first + scattered(lambda *at: dot(block(cmix_in, *at), w_cross))[0]

    normal_three, scaled_three, normed = norm_rows(second, gain_three)
    normed_three, _, _ = gather_rows(normed.astype(bf16), n)
    active, grad_gate, grad_upper, sum_gate, sum_upper, back_three, grad_w_down = feed(
        normed_three, group_grad, w_gateup, w_down, b_gate, b_upper
    )
    grad_rows = grad_output[0].astype(f32)
    grad_b_down = jnp.sum(grad_rows, axis=0)
    through, early = scattered(lambda *at: block(back_three, *at))
    own_down = lax.psum_scatter(grad_w_down, "fsdp", scatter_dimension=0, tiled=True)
    grad_w_gateup = gateup_grads(after(normed_three, *early), grad_gate, grad_upper, n, nf)
    through, grad_w_gateup = lax.optimization_barrier((through, grad_w_gateup))
    through, grad_gain_three = norm_back(through, normal_three, scaled_three, gain_three)
    grad_second = grad_rows + through

    group_second, early, _ = gather_rows(grad_second.astype(bf16), n)
    grad_w_gateup = after(grad_w_gateup, own_down, *early)
    own_gateup = lax.psum_scatter(grad_w_gateup, "fsdp", scatter_dimension=0, tiled=True)
    grad_cmix = pad_heads(back_prod(group_second, w_cross).astype(bf16), 1)
    dcq, dck, dcv = attend_back(
        cq, keyval, keyval, (0, 0, pairs), pairs, grad_cmix, cmix, clse, ids, cond_ids
    )
    dcq, dck, dcv = dcq[:, :wide], dck[:, :wide], dcv[:, :wide]
    cond_full = jnp.pad(cond_rows, ((0, count_pad - count), (0, 0)))
    through, _ = scattered(lambda *at: back_prod(block(dcq, *at), w_query))
    b_whole = lax.dynamic_update_slice(
        jnp.zeros((2, FF), f32), jnp.concatenate([sum_gate, sum_upper], axis=0), (0, me * hidden)
    )
    vectors = jnp.concatenate(
        [v.reshape(n, nf, r, -1) for v in (grad_gain_three, grad_b_down, b_whole)], axis=3
    )
    vectors = vectors.astype(bf16).transpose(1, 0, 2, 3).reshape(nf * n * r, -1)
    vectors = jnp.pad(vectors, ((0, 0), (0, LANES - vectors.shape[1])))
    grad_w_mid = mid_grads(cond_full, dck, dcv, normed_two, dcq, cmix_in, group_second, vectors, n, nf)
    through, grad_w_mid = lax.optimization_barrier((through, grad_w_mid))
    through, grad_gain_two = norm_back(through, normal_two, scaled_two, gain_two)
    grad_first = grad_second + through

    gains = grad_gain_two.astype(bf16).reshape(n, nf, r, 1).transpose(1, 0, 2, 3).reshape(D, 1)
    gains = jnp.pad(gains, ((0, 0), (1, LANES - 2)))
    down = dot(after(active, grad_first), w_down).astype(bf16)
    group_first, _, _ = gather_rows(grad_first.astype(bf16), n, (down,))
    group_first, gains = lax.optimization_barrier((group_first, gains))
    grad_w_mid = after(grad_w_mid, own_gateup, group_first)
    own_mid = lax.psum_scatter(grad_w_mid, "fsdp", scatter_dimension=0, tiled=True)
    own_gateup = share(after(own_gateup, group_first), n)
    grad_keyval = jnp.concatenate([dck, dcv], axis=1)[:count]
    cond_part = after(back_prod(grad_keyval, w_keyval), group_first)
    down = after(down, group_first)
    down_pieces = scatter_start(down, n)
    grad_mixed = pad_heads(back_prod(group_first, w_out).astype(bf16), 1)
    grad_mixed = after(grad_mixed, down)
    dq, dk, dv = attend_back(q, k, v, (0, 0, 0), pairs, grad_mixed, mixed, lse, ids, ids, tables)
    dq, dk, dv = dq[:, :wide], dk[:, :wide], dv[:, :wide]
    dq, own_gateup = lax.optimization_barrier((after(dq, *down_pieces), own_gateup))
    grad_w_self = self_grads(normed_one, dq, dk, dv, self_all, gains, mixed_in, group_first, n, nf)
    dq, dk, dv, grad_w_self = lax.optimization_barrier((dq, dk, dv, grad_w_self))
    own_self = lax.psum_scatter(after(grad_w_self, own_mid), "fsdp", scatter_dimension=0, tiled=True)
    grad_packed = jnp.concatenate([dq, dk, dv], axis=1)
    through, early = scattered(lambda *at: back_prod(block(grad_packed, *at), w_self))
    down_pieces = [after(piece, through) for piece in down_pieces]
    result = second + scatter_end(down, down_pieces, n) + b_down
    cond_parts = sum_start(after(cond_part, *early), n)
    own_gateup = after(own_gateup, *early)

    def joined(pieces):
        return pieces.reshape(n, r, wide).transpose(1, 0, 2).reshape(r, D)

    split = 3 * wide + LANES
    own_cross = joined(own_mid[:, split:])
    own_out = joined(own_self[:, split:])
    last_part = share(jnp.concatenate([own_mid[:, :split], own_self[:, :split]], axis=1), n)
    grad_cond = sum_end([after(part, last_part) for part in cond_parts], n)
    grad_cond = grad_cond.reshape(1, SEQS_GRP, COND, D)
    vectors = jnp.sum(last_part[:, :, 3 * wide : split].astype(f32), axis=0)
    grad_inputs = grad_first + norm_back(through, normal_one, scaled_one, gain_one)[0]
    gains = jnp.sum(last_part[:, :, split + 3 * wide :].astype(f32), axis=0)

    return (
        result.astype(bf16)[None],
        grad_inputs[None],
        grad_cond,
        gains[:, 0],
        spread(last_part, D, 3, n, split),
        own_out.astype(f32),
        gains[:, 1],
        spread(last_part, D, 1, n, 2 * wide),
        spread(last_part, D, 2, n),
        own_cross.astype(f32),
        vectors[:, 0],
        spread(own_gateup, FF, 2, n),
        vectors[:, 2:10].reshape(8 * r),
        own_down.astype(f32),
        vectors[:, 1],
    )


def solution(mesh):
    rows_of = P("fsdp", "seq", None)
    matrix = P(ALL, None)
    vector = P(ALL)
    return jax.shard_map(
        shards,
        mesh=mesh,
        in_specs=(
            rows_of,
            P("fsdp", None, None, None),
            P("fsdp", None),
            rows_of,
            vector,
            matrix,
            matrix,
            vector,
            matrix,
            matrix,
            matrix,
            vector,
            matrix,
            vector,
            matrix,
            vector,
        ),
        out_specs=(
            rows_of,
            rows_of,
            P("fsdp", None, None, None),
            vector,
            matrix,
            matrix,
            vector,
            matrix,
            matrix,
            matrix,
            vector,
            matrix,
            vector,
            matrix,
            vector,
        ),
        check_vma=False,
    )
```
